32 devices in a mesh: crop: 2 (over y), rows: 4 (over x, core), hid: 4 (over z).
Axes of the slice: x: 2, y: 2, z: 4, core: 2. Of those that a mesh axis runs over, the one named last changes fastest.
Arguments:
- tokens: bfloat16 [2, 8, 64, 4096], P('crop', 'rows', None, 'hid'), may hold values from -6 to 6
- cotangent: bfloat16 [2, 8, 64, 4096], P('crop', 'rows', None, 'hid'), may hold values from -6 to 6
- weight_in: bfloat16 [256, 64, 5, 256], P('rows', 'hid'), may hold values from -0.15625 to 0.15625
- weight_out: bfloat16 [256, 64, 5, 256], P('rows', 'hid'), may hold values from -0.078125 to 0.078125
- mix_kernel: float32 [9, 16384], P(None, 'hid'), may hold values from -4 to 4
- block_rows: int32 [64, 5], P('hid'), may hold values from 0 to 15, as said below
Outputs:
- grad_tokens: bfloat16 [2, 8, 64, 4096], P('crop', 'rows', None, 'hid')
- grad_w_in: float32 [256, 64, 5, 256], P(('crop', 'rows'), 'hid')
- grad_w_out: float32 [256, 64, 5, 256], P(('crop', 'rows'), 'hid')
- grad_kernel: float32 [9, 16384], P(None, 'hid')
The draws below stay inside these ranges and needn't reach their ends.
Inputs may be any that keep to these rules, and one draw needn't show every extreme that they name: In each block column c, block_rows[c, 0] is a label L and block_rows[c, k] for k >= 1 is L with bit k - 1 flipped, so the 5 entries of a column differ; every value is the label of equally many block columns.
All inputs are finite; a program needn't handle non-finite values.
Results may differ from the reference program's by a relative error of at most 0.019.
Values may be sent and summed in bfloat16 or wider, within the bound.
A program may use at most 128 MiB of HBM per device.

```python
import jax
import jax.numpy as jnp
from jax import lax

D = 4096
F = 16384
BS = 256
NNZ = 5
PW = 64
CROPS = 2
GH = 8
FB = 64
N_ROWS = 4


def draw_block_rows(key, part):
    block_count = D // BS
    perm_key, flip_key = jax.random.split(jax.random.fold_in(key, 7))
    labels = jax.random.permutation(perm_key, jnp.arange(F // BS, dtype=jnp.int32)) % block_count
    flip_bits = jax.random.randint(flip_key, (), 0, block_count).astype(jnp.int32)
    labels = jnp.bitwise_xor(labels, flip_bits)
    shifts = jnp.left_shift(jnp.ones((NNZ - 1,), jnp.int32), jnp.arange(NNZ - 1, dtype=jnp.int32))
    masks = jnp.concatenate([jnp.zeros((1,), jnp.int32), shifts])
    return jnp.bitwise_xor(labels[:, None], masks[None, :]).astype(jnp.int32)


def steps_of(own_key, dims, shards, low, largest):
    gain, own = 1.0, jax.random.fold_in(own_key, 6)
    for axis_at, shards_of in shards:
        steps = jnp.exp(jax.random.uniform(jax.random.fold_in(own, axis_at), (shards_of,), jnp.float32, low / len(shards), largest / len(shards)))
        gain = gain * jnp.repeat(steps, dims[axis_at] // shards_of).reshape([-1 if axis == axis_at else 1 for axis in range(len(dims))])
    return gain


def noise(own_key, shape, width, bound, cuts=(), held_as=jnp.bfloat16):
    entries = width * jax.random.normal(own_key, shape, jnp.float32)
    if cuts:
        entries = entries * steps_of(own_key, shape, cuts, -0.22, 0.18)
    return jnp.clip(entries, -bound, bound).astype(held_as)


def setup_inputs(seed: int = 0) -> dict:
    splits = jax.random.split(jax.random.key(seed), 7)
    tokens = noise(splits[0], (CROPS, GH, PW, D), 1.0, 6.0, ((0, 2), (1, 4), (3, 4)))
    cotangent = noise(splits[1], (CROPS, GH, PW, D), 1.0, 6.0, ((0, 2), (1, 4), (3, 4)))
    weight_in = noise(splits[2], (BS, FB, NNZ, BS), (NNZ * BS) ** -0.5, 0.15625, ((0, 4), (1, 4)))
    weight_out = noise(splits[3], (BS, FB, NNZ, BS), (FB * NNZ * BS * BS // D) ** -0.5, 0.078125, ((0, 4), (1, 4)))
    mix_kernel = noise(splits[4], (9, F), 0.35, 4.0, ((1, 4),), jnp.float32)
    block_rows = draw_block_rows(jax.random.fold_in(splits[6], 71), 0)
    return dict(tokens=tokens, cotangent=cotangent, weight_in=weight_in, weight_out=weight_out, mix_kernel=mix_kernel, block_rows=block_rows)


root_two_pi = 0.7978845608
cubic_coef = 0.044715
loss_scale = 0.03125


def gelu_pair(preact):
    inner = root_two_pi * (preact + cubic_coef * preact * preact * preact)
    tanh_val = jnp.tanh(inner)
    gelu_out = 0.5 * preact * (1.0 + tanh_val)
    slopes = 0.5 * (1.0 + tanh_val) + 0.5 * preact * (1.0 - tanh_val * tanh_val) * root_two_pi * (1.0 + 3.0 * cubic_coef * preact * preact)
    return gelu_out, slopes


def reference(tokens, cotangent, weight_in, weight_out, mix_kernel, block_rows):
    crop_count, height, grid_width, depth_all = tokens.shape
    block_count = depth_all // BS
    tok_count = crop_count * height * grid_width
    groups = crop_count * N_ROWS
    in_blocks = tokens.reshape(tok_count, block_count, BS)
    cot_blocks = cotangent.reshape(tok_count, block_count, BS)
    in_cols = jnp.moveaxis(weight_in, 1, 0)
    out_cols = jnp.moveaxis(weight_out, 1, 0)
    kern_cols = jnp.transpose(mix_kernel.reshape(9, FB, BS), (1, 0, 2))

    def column(dx_carry, slices):
        in_panel, out_panel, kern_local, row_ids = slices
        in_select = jnp.take(in_blocks, row_ids, axis=1).astype(jnp.float32)
        grad_select = jnp.take(cot_blocks, row_ids, axis=1).astype(jnp.float32)
        pre_act = jnp.einsum('nkb,bke->ne', in_select, in_panel.astype(jnp.float32))
        gelu_out, slopes = gelu_pair(pre_act)
        active = gelu_out.astype(jnp.bfloat16).astype(jnp.float32).reshape(crop_count, height, grid_width, BS)
        padded = jnp.pad(active, ((0, 0), (1, 1), (1, 1), (0, 0)))
        mix_sum = jnp.zeros((crop_count, height, grid_width, BS), jnp.float32)
        for row_off in range(3):
            for col_off in range(3):
                mix_sum = mix_sum + kern_local[3 * row_off + col_off] * padded[:, row_off:row_off + height, col_off:col_off + grid_width]
        mix_out = mix_sum.astype(jnp.bfloat16).astype(jnp.float32).reshape(tok_count, BS)
        mix_grad = jnp.einsum('nkd,fkd->nf', grad_select, out_panel.astype(jnp.float32)).astype(jnp.bfloat16).astype(jnp.float32)
        grad_grid = mix_grad.reshape(crop_count, height, grid_width, BS)
        grad_pad = jnp.pad(grad_grid, ((0, 0), (1, 1), (1, 1), (0, 0)))
        act_grad = jnp.zeros((crop_count, height, grid_width, BS), jnp.float32)
        kern_terms = []
        for row_off in range(3):
            for col_off in range(3):
                act_grad = act_grad + kern_local[3 * row_off + col_off] * grad_pad[:, 2 - row_off:2 - row_off + height, 2 - col_off:2 - col_off + grid_width]
                kern_terms.append(jnp.sum(padded[:, row_off:row_off + height, col_off:col_off + grid_width] * grad_grid, axis=(0, 1, 2)))
        kern_sum = jnp.stack(kern_terms, axis=0) * loss_scale
        pre_grad = (act_grad.reshape(tok_count, BS) * slopes).astype(jnp.bfloat16).astype(jnp.float32)
        mix_groups = mix_out.reshape(groups, tok_count // groups, BS)
        cot_groups = grad_select.reshape(groups, tok_count // groups, NNZ, BS)
        out_parts = (jnp.einsum('gtf,gtkd->gfkd', mix_groups, cot_groups) * loss_scale).astype(jnp.bfloat16).astype(jnp.float32)
        in_groups = in_select.reshape(groups, tok_count // groups, NNZ, BS)
        pre_groups = pre_grad.reshape(groups, tok_count // groups, BS)
        in_parts = (jnp.einsum('gtkb,gte->gbke', in_groups, pre_groups) * loss_scale).astype(jnp.bfloat16).astype(jnp.float32)
        back_select = jnp.einsum('ne,bke->nkb', pre_grad, in_panel.astype(jnp.float32))
        dx_carry = dx_carry.at[:, row_ids].add(back_select)
        return dx_carry, (jnp.sum(in_parts, axis=0), jnp.sum(out_parts, axis=0), kern_sum)

    dx_start = jnp.zeros((tok_count, block_count, BS), jnp.float32)
    dx_total, (in_grads, out_grads, kern_grads) = lax.scan(column, dx_start, (in_cols, out_cols, kern_cols, block_rows))
    grad_tokens = dx_total.reshape(crop_count, height, grid_width, depth_all).astype(jnp.bfloat16)
    grad_w_in = jnp.moveaxis(in_grads, 0, 1)
    grad_w_out = jnp.moveaxis(out_grads, 0, 1)
    grad_kernel = jnp.transpose(kern_grads, (1, 0, 2)).reshape(9, FB * BS)
    return grad_tokens, grad_w_in, grad_w_out, grad_kernel
```

```python
import functools

import jax
import jax.numpy as jnp
from jax import lax
from jax.experimental import pallas as pl
from jax.experimental.pallas import tpu as pltpu
from jax.sharding import PartitionSpec as P

root_two_pi = 0.7978845608
cubic_coef = 0.044715
loss_scale = 0.03125

MESH_ID = pl.DeviceIdType.MESH
ANY = pl.BlockSpec(memory_space=pl.ANY)
VMEM = pl.BlockSpec(memory_space=pltpu.VMEM)
SMEM = pl.BlockSpec(memory_space=pltpu.SMEM)


def span(start, size):
    return pl.ds(pl.multiple_of(start * size, size), size)


def neighbours():
    y, r, z = lax.axis_index("crop"), lax.axis_index("rows"), lax.axis_index("hid")
    x, core = r // 2, r % 2
    same_chip = x * 2 + (1 - core)
    across = (1 - x) * 2 + core
    diagonal = (1 - x) * 2 + (1 - core)
    return y, r, z, same_chip, across, diagonal


def enter(partners):
    barrier = pltpu.get_barrier_semaphore()
    for partner in partners:
        pl.semaphore_signal(barrier, inc=1, device_id=partner, device_id_type=MESH_ID)
    pl.semaphore_wait(barrier, len(partners))


def remote(src, dst, send_sem, recv_sem, target):
    return pltpu.make_async_remote_copy(
        src_ref=src,
        dst_ref=dst,
        send_sem=send_sem,
        recv_sem=recv_sem,
        device_id=target,
        device_id_type=MESH_ID,
    )


def gather_kernel(
    depth, tok, cot, w_in, w_out, tok_all, cot_all, in_all, out_all,
    raw, flat, stage, tok_send, tok_recv, w_send, w_recv, own_sem, raw_sem,
):
    y, r, z, same_chip, across, diagonal = neighbours()
    tokens, features = tok.shape
    rows = w_in.shape[0]
    lanes = in_all.shape[1]
    half = rows // 2
    block = w_in.shape[2]
    all_cols = stage.shape[1] // rows
    nnz = w_in.shape[1] // all_cols
    loads = [
        pltpu.make_async_copy(src, raw.at[a], raw_sem.at[a]) for a, src in enumerate((w_in, w_out))
    ]
    for load in loads:
        load.start()
    enter(
        [{"rows": same_chip}, {"rows": across}, {"rows": diagonal}, {"crop": 1 - y}]
        + [{"hid": (z + step) % depth} for step in range(1, depth)]
    )
    streams = ((tok, tok_all), (cot, cot_all))
    panels = ((flat.at[0], in_all), (flat.at[1], out_all))
    targets = ({"hid": z + 1}, {"hid": z - 1}, {"rows": across}, {"rows": same_chip})
    has_up, has_down = z + 1 < depth, z >= 1
    sends, local = [], []

    def launch(make, have=None):
        sends.append((make, have))
        if have is None:
            make().start()
        else:
            pl.when(have)(lambda: make().start())

    def piece(full, row, col):
        return full.at[span(row, tokens), span(col, features)]

    def pass_on(a, which, col, kind, have=None, own=False):
        def make():
            row = (r, across)[which]
            part = piece(streams[a][1], row, col)
            return remote(
                streams[a][0] if own else part,
                part,
                tok_send.at[a, which, col, kind],
                tok_recv.at[a, row, col],
                targets[kind],
            )

        launch(make, have)

    def await_piece(a, row, col, have=None):
        def wait():
            part = piece(streams[a][1], row, col)
            remote(
                part, part, tok_send.at[a, 0, 0, 3], tok_recv.at[a, row, col], {"rows": same_chip}
            ).wait_recv()

        if have is None:
            wait()
        else:
            pl.when(have)(wait)

    def half_rows(full, row, h):
        return full.at[pl.ds(pl.multiple_of(row * rows + h * half, half), half), :]

    def flatten(a):
        def turn(k, carry):
            for h in range(block // 128):
                part = raw[a, :, span(k, all_cols), h * 128 : (h + 1) * 128]
                stage[h] = part.astype(jnp.float32).reshape(rows * all_cols, 128)
            for c in range(all_cols):
                for h in range(block // 128):
                    flat[a, :, pl.ds(pl.multiple_of((c * nnz + k) * block + h * 128, 128), 128)] = stage[
                        h, pl.ds(c, rows, stride=all_cols), :
                    ].astype(jnp.bfloat16)
            return carry

        lax.fori_loop(0, nnz, turn, 0)

    def give_weights(a):
        src, full = panels[a]
        loads[a].wait()
        flatten(a)
        for slot, dest in ((1, across), (2, diagonal)):
            launch(
                lambda slot=slot, dest=dest: remote(
                    src.at[span(y, half), span(dest, lanes)],
                    half_rows(full, r, y),
                    w_send.at[a, slot],
                    w_recv.at[a, r, y],
                    {"rows": dest},
                )
            )
        launch(
            lambda: remote(
                src.at[:, span(same_chip, lanes)],
                full.at[span(r, rows), :],
                w_send.at[a, 0],
                w_recv.at[a, r, 0],
                {"rows": same_chip},
            )
        )
        keep = pltpu.make_async_copy(
            src.at[:, span(r, lanes)], full.at[span(r, rows), :], own_sem.at[a, 1]
        )
        keep.start()
        local.append(keep)

    def mirror_weights(a):
        full = panels[a][1]
        for slot, row in ((3, across), (4, diagonal)):
            part = half_rows(full, row, y)
            remote(part, part, w_send.at[a, slot], w_recv.at[a, row, y], {"rows": row}).wait_recv()
            launch(
                lambda slot=slot, row=row, part=part: remote(
                    part, part, w_send.at[a, slot], w_recv.at[a, row, y], {"crop": 1 - y}
                )
            )

    def line_step(step):
        for below in (True, False):
            col = z - step if below else z + step
            have = col >= 0 if below else col < depth
            onward = jnp.logical_and(have, has_up if below else has_down)
            for a, which in ((0, 0), (1, 0), (1, 1)):
                await_piece(a, (r, across)[which], col, have)
                pass_on(a, which, col, 0 if below else 1, onward)
                if a == 0:
                    pass_on(a, which, col, 2, have)
                pass_on(a, which, col, 3, have)

    for a, kind in ((1, 2), (0, 0), (0, 1), (1, 0), (1, 1), (0, 2), (0, 3), (1, 3)):
        pass_on(a, 0, z, kind, (has_up, has_down, None, None)[kind], own=True)
    for a in range(2):
        keep = pltpu.make_async_copy(streams[a][0], piece(streams[a][1], r, z), own_sem.at[a, 0])
        keep.start()
        local.append(keep)
    give_weights(0)
    await_piece(1, across, z)
    for kind in (0, 1, 3):
        pass_on(1, 1, z, kind, (has_up, has_down, None, None)[kind])
    give_weights(1)
    for step in range(1, depth):
        line_step(step)
        if step <= 2:
            mirror_weights(step - 1)
    for a in range(depth - 1, 2):
        mirror_weights(a)
    for step in range(depth):
        col = (z + step) % depth
        await_piece(0, across, col)
        pass_on(0, 1, col, 3)
    for a in range(2):
        full = panels[a][1]
        part = full.at[span(same_chip, rows), :]
        remote(
            part, part, w_send.at[a, 0], w_recv.at[a, same_chip, 0], {"rows": same_chip}
        ).wait_recv()
        for row in (across, diagonal):
            part = half_rows(full, row, 1 - y)
            remote(
                part, part, w_send.at[a, 0], w_recv.at[a, row, 1 - y], {"crop": 1 - y}
            ).wait_recv()
        for row in (same_chip, diagonal):
            for step in range(depth):
                await_piece(a, row, (z + step) % depth)
    for copy in local:
        copy.wait()
    for make, have in sends:
        if have is None:
            make().wait_send()
        else:
            pl.when(have)(lambda make=make: make().wait_send())


def nt(a, b):
    return lax.dot_general(a, b, (((1,), (1,)), ((), ())), preferred_element_type=jnp.float32)


def tn(a, b):
    return lax.dot_general(a, b, (((0,), (0,)), ((), ())), preferred_element_type=jnp.float32)


def column_math(width, block, cols, nnz, ids, tok, cot, w_in, w_out, taps, kern, mixed, pgrad, pre_s, act_s, slope_s, mg_s, gw):
    count = tok.shape[1]
    me = lax.axis_index("rows")
    place = lax.broadcasted_iota(jnp.int32, (count, block), 0) % width

    def spread(value):
        before = jnp.where(place == 0, 0.0, pltpu.roll(value, 1, 0))
        after = jnp.where(place == width - 1, 0.0, pltpu.roll(value, count - 1, 0))
        return (before, value, after)

    def stack_rows(up, mid, down):
        edge = jnp.zeros((width, block), jnp.float32)
        return (
            mid
            + jnp.concatenate([edge, up[:-width]], axis=0)
            + jnp.concatenate([down[width:], edge], axis=0)
        )

    def feats(c, k):
        return ids[k, me * cols + c]

    def panel(c, k):
        return span(c * nnz + k, block)

    def tap(c, a, b):
        row = 3 * (a + 1) + (b + 1)
        return taps[row : row + 1, span(me * cols + c, block)]

    def forward(c, ready=None):
        hidden = span(c, block)
        pre = jnp.dot(tok[feats(c, 0)], w_in[c * nnz], preferred_element_type=jnp.float32)
        for k in range(1, nnz):
            pre += jnp.dot(tok[feats(c, k)], w_in[c * nnz + k], preferred_element_type=jnp.float32)
        pre_s[...] = pre
        p = pre_s[...]
        t = jnp.tanh(root_two_pi * (p + cubic_coef * p * p * p))
        act_s[...] = (0.5 * p * (1.0 + t)).astype(jnp.bfloat16).astype(jnp.float32)
        slope_s[...] = 0.5 * (1.0 + t) + 0.5 * p * (1.0 - t * t) * root_two_pi * (
            1.0 + 3.0 * cubic_coef * p * p
        )
        acts = spread(act_s[...])
        mixed[:, hidden] = stack_rows(
            *[sum(tap(c, a, b) * acts[b + 1] for b in (-1, 0, 1)) for a in (-1, 0, 1)]
        ).astype(jnp.bfloat16)
        if ready is not None:
            ready()

    def backward(c):
        hidden = span(c, block)
        mg = nt(cot[feats(c, 0)], w_out[:, panel(c, 0)])
        for k in range(1, nnz):
            mg += nt(cot[feats(c, k)], w_out[:, panel(c, k)])
        mg_s[...] = mg.astype(jnp.bfloat16).astype(jnp.float32)
        acts = spread(act_s[...])
        grads = mg_s[...]
        for b in (-1, 0, 1):
            seen = acts[b + 1]
            sums = (
                jnp.sum(seen[:-width] * grads[width:], axis=0, keepdims=True),
                jnp.sum(seen * grads, axis=0, keepdims=True),
                jnp.sum(seen[width:] * grads[:-width], axis=0, keepdims=True),
            )
            for a in (-1, 0, 1):
                row = 3 * (a + 1) + (b + 1)
                kern[row : row + 1, hidden] = sums[a + 1] * loss_scale
        backs = spread(mg_s[...])
        gathered = stack_rows(
            *[sum(tap(c, a, b) * backs[1 - b] for b in (-1, 0, 1)) for a in (1, 0, -1)]
        )
        pgrad[:, hidden] = (gathered * slope_s[...]).astype(jnp.bfloat16)

    def grad_out(c):
        left = mixed[:, span(c, block)]
        for k in range(nnz):
            gw[1, :, panel(c, k)] = (tn(left, cot[feats(c, k)]) * loss_scale).astype(jnp.bfloat16)

    def grad_in(c):
        right = pgrad[:, span(c, block)]
        for k in range(nnz):
            gw[0, :, panel(c, k)] = (tn(tok[feats(c, k)], right) * loss_scale).astype(jnp.bfloat16)

    limit = tok.shape[0] ** 2

    def token_grad(g):
        total = jnp.zeros((count, block), jnp.float32)
        for c in range(cols):
            at = cols * nnz
            for k in range(nnz):
                apart = ids[k, me * cols + c] - g
                same = 1 - lax.div(apart * apart + (limit - 1), jnp.int32(limit))
                at += same * (c * nnz + k - at)
            total += nt(pgrad[:, span(c, block)], w_in[at])
        return total.astype(jnp.bfloat16)

    return forward, backward, grad_out, grad_in, token_grad


def grads_kernel(
    depth, width, block, cols, nnz, ids, tok_h, cot_h, in_h, out_h, taps,
    dx_mine, mine, kern_all,
    tok, cot, w_in, w_out, kern, mixed, pgrad, pre_s, act_s, slope_s, mg_s, gw, gw_part,
    dx, dx_near, dx_half, dx_far, dx_sum, dx_last, kern_own, kern_part,
    dx_send, dx_recv, far_send, far_recv, gw_send, gw_recv, part_send, part_recv,
    kern_send, kern_recv, load_sem,
):
    y, r, z, same_chip, across, diagonal = neighbours()
    group = [same_chip, across, diagonal]
    tokens, features = dx_mine.shape
    rows = mine.shape[1]
    half = block // 2
    lanes = nnz * block
    per_part = features // block
    def stack(i, src, dst, at):
        return pltpu.make_async_copy(src.at[:, span(at, block)], dst.at[at], load_sem.at[i, at])

    def each(i, act):
        src, dst, many = ((tok_h, tok, tok.shape[0]), (in_h, w_in, cols * nnz), (cot_h, cot, cot.shape[0]))[i]

        def turn(at, carry):
            act(stack(i, src, dst, at))
            return carry

        lax.fori_loop(0, many, turn, 0)

    out_load = pltpu.make_async_copy(out_h, w_out, load_sem.at[3, 0])
    for i in range(3):
        each(i, lambda copy: copy.start())
    out_load.start()
    w_in[cols * nnz] = jnp.zeros((block, block), jnp.bfloat16)
    kern[...] = jnp.zeros_like(kern)
    enter(
        [{"rows": row} for row in group]
        + [{"crop": 1 - y}]
        + [{"hid": (z + step) % depth} for step in range(1, depth)]
    )
    started = []

    def go(*args):
        copy = remote(*args)
        copy.start()
        started.append(copy)

    def arrived(ref, send_sem, recv_sem, target):
        remote(ref, ref, send_sem, recv_sem, target).wait_recv()

    forward, backward, grad_out, grad_in, token_grad = column_math(
        width, block, cols, nnz, ids, tok, cot, w_in, w_out, taps, kern, mixed, pgrad,
        pre_s, act_s, slope_s, mg_s, gw,
    )

    def give(a, c):
        go(
            gw.at[a, span(1 - y, half), span(c, lanes)],
            gw_part.at[a, c],
            gw_send.at[a, c],
            gw_recv.at[a, c],
            {"crop": 1 - y},
        )

    def settle(a, c):
        arrived(gw_part.at[a, c], gw_send.at[a, c], gw_recv.at[a, c], {"crop": 1 - y})
        gw_part[a, c] = (
            gw[a, span(y, half), span(c, lanes)].astype(jnp.float32) + gw_part[a, c].astype(jnp.float32)
        ).astype(jnp.bfloat16)
        at = span(r * cols + c, lanes)
        for slot, row in enumerate((across, diagonal, same_chip)):
            go(
                gw_part.at[a, c, span(row, rows), :],
                mine.at[a, :, at],
                part_send.at[a, c, slot],
                part_recv.at[a, c, slot],
                {"rows": row},
            )
        mine[a, :, at] = gw_part[a, c, span(r, rows), :]

    def part_of(i):
        return (z + 1 + i) % depth

    def lanes_of(i):
        return span(part_of(i), features)

    each(0, lambda copy: copy.wait())
    each(1, lambda copy: copy.wait())
    forward(0, lambda: each(2, lambda copy: copy.wait()))
    grad_out(0)
    give(1, 0)
    out_load.wait()
    backward(0)
    grad_in(0)
    give(0, 0)

    def one_column(c, carry):
        forward(c)
        backward(c)
        return carry

    lax.fori_loop(1, cols, one_column, 0)

    near = ((0, diagonal), (1, same_chip))

    def near_copy(slot, row, i):
        at = lanes_of(i)
        return remote(
            dx.at[span(row, tokens), at],
            dx_near.at[slot, :, at],
            dx_send.at[slot, i],
            dx_recv.at[slot, i],
            {"rows": same_chip},
        )

    for i in range(depth):

        def one_block(j, carry):
            g = part_of(i) * per_part + j
            dx[:, span(g, block)] = token_grad(g)
            return carry

        lax.fori_loop(0, per_part, one_block, 0)
        for slot, row in near:
            near_copy(slot, row, i).start()
    grad_out(1)
    give(1, 1)
    settle(1, 0)
    for i in range(depth):
        near_copy(0, diagonal, i).wait_recv()
        at = lanes_of(i)
        dx_half[:, at] = (
            dx[span(across, tokens), at].astype(jnp.float32) + dx_near[0, :, at].astype(jnp.float32)
        ).astype(jnp.bfloat16)
        go(dx_half.at[:, at], dx_far.at[:, at], far_send.at[0, i], far_recv.at[0, i], {"rows": across})
    grad_in(1)
    give(0, 1)
    settle(0, 0)

    def later(c, carry):
        grad_out(c)
        grad_in(c)
        return carry

    lax.fori_loop(2, cols, later, 0)
    for c in range(2, cols):
        give(1, c)
        give(0, c)
    kern_own[...] = kern[...].astype(jnp.bfloat16)
    go(kern_own, kern_part.at[1, 0], kern_send.at[0], kern_recv.at[1, 0], {"crop": 1 - y})

    def pass_sum(i):
        at = lanes_of(i)
        near_copy(1, same_chip, i).wait_recv()
        arrived(dx_far.at[:, at], far_send.at[0, i], far_recv.at[0, i], {"rows": across})
        dx_sum[i] = (
            dx[span(r, tokens), at].astype(jnp.float32)
            + dx_near[1, :, at].astype(jnp.float32)
            + dx_far[:, at].astype(jnp.float32)
        ).astype(jnp.bfloat16)
        if i < depth - 1:
            go(
                dx_sum.at[i],
                dx_last.at[i],
                far_send.at[1, i],
                far_recv.at[1, i],
                {"hid": part_of(i)},
            )

    waits = [(a, c) for c in range(1, cols) for a in (1, 0)]
    sums = list(range(depth))
    pass_sum(sums.pop(0))
    arrived(kern_part.at[1, 0], kern_send.at[0], kern_recv.at[1, 0], {"crop": 1 - y})
    kern_part[0, r] = (
        kern_own[...].astype(jnp.float32) + kern_part[1, 0].astype(jnp.float32)
    ).astype(jnp.bfloat16)
    for slot, row in enumerate(group):
        go(
            kern_part.at[0, r],
            kern_part.at[0, r],
            kern_send.at[slot + 1],
            kern_recv.at[0, r],
            {"rows": row},
        )
    while len(waits) > 1:
        settle(*waits.pop(0))
        if sums:
            pass_sum(sums.pop(0))
    while sums:
        pass_sum(sums.pop(0))
    total = dx_sum[depth - 1].astype(jnp.float32)
    for step in range(depth - 1):
        arrived(dx_last.at[step], far_send.at[1, step], far_recv.at[1, step], {"hid": part_of(step)})
        total += dx_last[step].astype(jnp.float32)
    dx_mine[...] = total.astype(jnp.bfloat16)
    for row in group:
        arrived(kern_part.at[0, row], kern_send.at[0], kern_recv.at[0, row], {"rows": same_chip})
    wide = kern.shape[1]
    for row in range(4):
        kern_all[:, row * wide : (row + 1) * wide] = kern_part[0, row].astype(jnp.float32)
    for a, c in waits:
        settle(a, c)
    for a in (1, 0):
        for c in range(cols):
            for slot, row in enumerate((across, diagonal, same_chip)):
                arrived(
                    mine.at[a, :, span(row * cols + c, lanes)],
                    part_send.at[a, c, slot],
                    part_recv.at[a, c, slot],
                    {"rows": row},
                )
    for i in range(depth):
        for slot, row in near:
            near_copy(slot, row, i).wait_send()
    for copy in started:
        copy.wait_send()


def finish_kernel(
    all_cols, nnz, mine, dx_mine, kern_all, in_grad, out_grad, dx_grad, kern_grad
):
    block = in_grad.shape[2]
    dx_grad[...] = dx_mine[...]
    kern_grad[...] = kern_all[: kern_grad.shape[0]]
    for src, dst in ((mine.at[0], in_grad), (mine.at[1], out_grad)):
        for c in range(all_cols):
            for k in range(nnz):
                at = (c * nnz + k) * block
                dst[:, k * all_cols + c, :] = src[:, at : at + block].astype(jnp.float32)


def split_hidden(tokens, cotangent, weight_in, weight_out, mix_kernel, block_rows):
    n_rows, depth = lax.axis_size("rows"), lax.axis_size("hid")
    _, height, width, features = tokens.shape
    rows, all_cols, nnz, block = weight_in.shape
    count = height * width
    whole = count * n_rows
    model = features * depth
    cols = all_cols // n_rows
    lanes = cols * nnz * block
    hidden = cols * block
    bf16, f32 = jnp.bfloat16, jnp.float32
    dma, sds = pltpu.SemaphoreType.DMA, jax.ShapeDtypeStruct
    params = functools.partial(pltpu.CompilerParams, vmem_limit_bytes=60 * 1024 * 1024)
    tok_all, cot_all, in_all, out_all = pl.pallas_call(
        functools.partial(gather_kernel, depth),
        name="gather_parts",
        out_shape=[sds((whole, model), bf16)] * 2 + [sds((rows * n_rows, lanes), bf16)] * 2,
        in_specs=[ANY] * 4,
        out_specs=[ANY] * 4,
        scratch_shapes=[
            pltpu.VMEM((2, rows, nnz * all_cols, block), bf16),
            pltpu.VMEM((2, rows, all_cols * nnz * block), bf16),
            pltpu.VMEM((block // 128, rows * all_cols, 128), f32),
            dma((2, 2, depth, 4)),
            dma((2, n_rows, depth)),
            dma((2, 5)),
            dma((2, n_rows, 2)),
            dma((2, 2)),
            dma((2,)),
        ],
        compiler_params=params(collective_id=1, has_side_effects=True),
    )(
        tokens.reshape(count, features),
        cotangent.reshape(count, features),
        weight_in.transpose(0, 2, 1, 3).reshape(rows, nnz * all_cols, block),
        weight_out.transpose(0, 2, 1, 3).reshape(rows, nnz * all_cols, block),
    )
    out_rows = block // (n_rows * lax.axis_size("crop"))
    panel = nnz * block
    dx_mine, mine, kern_all = pl.pallas_call(
        functools.partial(grads_kernel, depth, width, block, cols, nnz),
        name="grads_and_sums",
        out_shape=[
            sds((count, features), bf16),
            sds((2, out_rows, all_cols * panel), bf16),
            sds((16, hidden * n_rows), f32),
        ],
        in_specs=[SMEM] + [ANY] * 4 + [VMEM],
        out_specs=[VMEM] * 3,
        scratch_shapes=[
            pltpu.VMEM((model // block, whole, block), bf16),
            pltpu.VMEM((model // block, whole, block), bf16),
            pltpu.VMEM((cols * nnz + 1, block, block), bf16),
            pltpu.VMEM((block, lanes), bf16),
            pltpu.VMEM((16, hidden), f32),
            pltpu.VMEM((whole, hidden), bf16),
            pltpu.VMEM((whole, hidden), bf16),
        ]
        + [pltpu.VMEM((whole, block), f32)] * 4
        + [
            pltpu.VMEM((2, block, lanes), bf16),
            pltpu.VMEM((2, cols, block // 2, panel), bf16),
            pltpu.VMEM((whole, model), bf16),
            pltpu.VMEM((2, count, model), bf16),
            pltpu.VMEM((count, model), bf16),
            pltpu.VMEM((count, model), bf16),
            pltpu.VMEM((depth, count, features), bf16),
            pltpu.VMEM((depth - 1, count, features), bf16),
            pltpu.VMEM((16, hidden), bf16),
            pltpu.VMEM((2, n_rows, 16, hidden), bf16),
            dma((2, depth)),
            dma((2, depth)),
            dma((2, depth)),
            dma((2, depth)),
            dma((2, cols)),
            dma((2, cols)),
            dma((2, cols, 3)),
            dma((2, cols, 3)),
            dma((4,)),
            dma((2, n_rows)),
            dma((4, max(model // block, cols * nnz))),
        ],
        compiler_params=params(collective_id=2, has_side_effects=True),
    )(block_rows.T, tok_all, cot_all, in_all, out_all, mix_kernel)
    step = 8
    part = pl.BlockSpec((count * step // out_rows, features), lambda i: (i, 0))
    flat_spec = pl.BlockSpec((2, step, all_cols * nnz * block), lambda i: (0, i, 0))
    grad_spec = pl.BlockSpec((step, nnz * all_cols, block), lambda i: (i, 0, 0))
    in_grad, out_grad, dx_grad, kern_grad = pl.pallas_call(
        functools.partial(finish_kernel, all_cols, nnz),
        name="finish_weights",
        grid=(out_rows // step,),
        out_shape=[sds((out_rows, nnz * all_cols, block), f32)] * 2
        + [sds((count, features), bf16), sds(mix_kernel.shape, f32)],
        in_specs=[flat_spec, part, VMEM],
        out_specs=[grad_spec] * 2 + [part, VMEM],
        compiler_params=params(),
    )(mine, dx_mine, kern_all)
    in_grad, out_grad = [
        grad.reshape(out_rows, nnz, all_cols, block).transpose(0, 2, 1, 3) for grad in (in_grad, out_grad)
    ]
    return (dx_grad.reshape(tokens.shape), in_grad, out_grad, kern_grad)


def padded(shard, sides, width):
    for axis, dim in sides:
        devices, length = (lax.axis_size(axis), shard.shape[dim])
        up = [(i, (i + 1) % devices) for i in range(devices - 1)]
        down = [(j, i) for i, j in up]
        last = lax.slice_in_dim(shard, length - width, length, axis=dim)
        initial = lax.slice_in_dim(shard, 0, width, axis=dim)
        before = lax.ppermute(last, axis, up)
        after = lax.ppermute(initial, axis, down)
        shard = jnp.concatenate([before, shard, after], axis=dim)
    return shard


def gelu_pair(preact):
    inner = root_two_pi * (preact + cubic_coef * preact * preact * preact)
    tanh_val = jnp.tanh(inner)
    gelu_out = 0.5 * preact * (1.0 + tanh_val)
    slopes = 0.5 * (1.0 + tanh_val) + 0.5 * preact * (1.0 - tanh_val * tanh_val) * root_two_pi * (
        1.0 + 3.0 * cubic_coef * preact * preact
    )
    return (gelu_out, slopes)


def on_device(tokens, cotangent, weight_in, weight_out, mix_kernel, block_rows):
    in_panel, out_panel = (
        lax.all_gather(weight_in, "rows", axis=0, tiled=True),
        lax.all_gather(weight_out, "rows", axis=0, tiled=True),
    )
    tok_full, cot_full = (
        lax.all_gather(tokens, "hid", axis=3, tiled=True),
        lax.all_gather(cotangent, "hid", axis=3, tiled=True),
    )
    crop_count, height, grid_width, depth_all = tok_full.shape
    tok_count = crop_count * height * grid_width
    block_size = in_panel.shape[0]
    col_count = in_panel.shape[1]
    nnz_count = in_panel.shape[2]
    block_count = depth_all // block_size
    hidden_local = col_count * block_size
    flat_rows = block_rows.reshape(-1)
    in_select = jnp.take(
        tok_full.reshape(tok_count, block_count, block_size), flat_rows, axis=1
    ).reshape(tok_count, col_count, nnz_count, block_size)
    grad_select = jnp.take(
        cot_full.reshape(tok_count, block_count, block_size), flat_rows, axis=1
    ).reshape(tok_count, col_count, nnz_count, block_size)
    pre_act = jnp.einsum("tckb,bcke->tce", in_select, in_panel, preferred_element_type=jnp.float32)
    gelu_out, slopes = gelu_pair(pre_act)
    active = gelu_out.astype(jnp.bfloat16).reshape(crop_count, height, grid_width, hidden_local)
    act_rim = padded(active, (("rows", 1),), 1)
    mix_grad = (
        jnp.einsum("tckd,fckd->tcf", grad_select, out_panel, preferred_element_type=jnp.float32)
        .astype(jnp.bfloat16)
        .reshape(crop_count, height, grid_width, hidden_local)
    )
    grad_rim = padded(mix_grad, (("rows", 1),), 1)
    act_pad = jnp.pad(act_rim.astype(jnp.float32), ((0, 0), (0, 0), (1, 1), (0, 0)))
    grad_pad = jnp.pad(grad_rim.astype(jnp.float32), ((0, 0), (0, 0), (1, 1), (0, 0)))
    grad_grid = mix_grad.astype(jnp.float32)
    mix_sum = jnp.zeros((crop_count, height, grid_width, hidden_local), jnp.float32)
    act_grad = jnp.zeros((crop_count, height, grid_width, hidden_local), jnp.float32)
    kern_terms = []
    for row_off in range(3):
        for col_off in range(3):
            tap = mix_kernel[3 * row_off + col_off]
            shifted = act_pad[:, row_off : row_off + height, col_off : col_off + grid_width]
            mix_sum = mix_sum + tap * shifted
            act_grad = (
                act_grad
                + tap
                * grad_pad[
                    :, 2 - row_off : 2 - row_off + height, 2 - col_off : 2 - col_off + grid_width
                ]
            )
            kern_terms.append(jnp.sum(shifted * grad_grid, axis=(0, 1, 2)))
    kern_local = jnp.stack(kern_terms, axis=0) * loss_scale
    mix_out = mix_sum.astype(jnp.bfloat16).reshape(tok_count, col_count, block_size)
    pre_grad = (act_grad.reshape(tok_count, col_count, block_size) * slopes).astype(jnp.bfloat16)
    kern_total = lax.psum(kern_local.astype(jnp.bfloat16), ("crop", "rows")).astype(jnp.float32)
    back_select = jnp.einsum(
        "tce,bcke->tckb", pre_grad, in_panel, preferred_element_type=jnp.float32
    )
    one_hot = (
        block_rows[:, :, None] == jnp.arange(block_count, dtype=jnp.int32)[None, None, :]
    ).astype(jnp.float32)
    token_terms = jnp.einsum(
        "tckb,ckr->trb", back_select, one_hot, precision=lax.Precision.HIGHEST
    ).reshape(crop_count, height, grid_width, depth_all)
    grad_tokens = lax.psum_scatter(
        token_terms.astype(jnp.bfloat16), "hid", scatter_dimension=3, tiled=True
    )
    first_term = jnp.einsum(
        "tckb,tce->bcke", in_select, pre_grad, preferred_element_type=jnp.float32
    )
    second_term = jnp.einsum(
        "tcf,tckd->fckd", mix_out, grad_select, preferred_element_type=jnp.float32
    )
    share_sums = lax.psum_scatter(
        (jnp.stack([first_term, second_term], axis=1) * loss_scale).astype(jnp.bfloat16),
        ("crop", "rows"),
        scatter_dimension=0,
        tiled=True,
    ).astype(jnp.float32)
    return (grad_tokens, share_sums[:, 0], share_sums[:, 1], kern_total)


def solution(mesh):
    placed = (
        P("crop", "rows", None, "hid"),
        P("crop", "rows", None, "hid"),
        P("rows", "hid", None, None),
        P("rows", "hid", None, None),
        P(None, "hid"),
        P("hid", None),
    )
    n_crop, n_rows = mesh.shape["crop"], mesh.shape["rows"]
    n_hid = mesh.shape["hid"]

    def step(tokens, cotangent, weight_in, weight_out, mix_kernel, block_rows):
        fits = (
            n_crop == 2
            and n_rows == 4
            and tokens.shape[0] == 1
            and weight_in.shape[1] % n_rows == 0
            and tokens.shape[1] * tokens.shape[2] * n_rows * tokens.shape[3] * n_hid <= 2**22
        )
        chosen = split_hidden if fits else on_device
        return chosen(tokens, cotangent, weight_in, weight_out, mix_kernel, block_rows)

    return jax.shard_map(
        step,
        mesh=mesh,
        in_specs=placed,
        out_specs=(
            P("crop", "rows", None, "hid"),
            P(("crop", "rows"), "hid", None, None),
            P(("crop", "rows"), "hid", None, None),
            P(None, "hid"),
        ),
        check_vma=False,
    )
```

```python
import functools

import jax
import jax.numpy as jnp
from jax import lax
from jax.experimental import pallas as pl
from jax.experimental.pallas import tpu as pltpu
from jax.sharding import PartitionSpec as P

root_two_pi = 0.7978845608
cubic_coef = 0.044715
loss_scale = 0.03125

MESH_ID = pl.DeviceIdType.MESH
ANY = pl.BlockSpec(memory_space=pl.ANY)
VMEM = pl.BlockSpec(memory_space=pltpu.VMEM)
SMEM = pl.BlockSpec(memory_space=pltpu.SMEM)


def span(start, size):
    return pl.ds(pl.multiple_of(start * size, size), size)


def neighbours():
    y, r, z = lax.axis_index("crop"), lax.axis_index("rows"), lax.axis_index("hid")
    x, core = r // 2, r % 2
    same_chip = x * 2 + (1 - core)
    across = (1 - x) * 2 + core
    diagonal = (1 - x) * 2 + (1 - core)
    return y, r, z, same_chip, across, diagonal


def enter(partners):
    barrier = pltpu.get_barrier_semaphore()
    for partner in partners:
        pl.semaphore_signal(barrier, inc=1, device_id=partner, device_id_type=MESH_ID)
    pl.semaphore_wait(barrier, len(partners))


def remote(src, dst, send_sem, recv_sem, target):
    return pltpu.make_async_remote_copy(
        src_ref=src,
        dst_ref=dst,
        send_sem=send_sem,
        recv_sem=recv_sem,
        device_id=target,
        device_id_type=MESH_ID,
    )


def gather_kernel(
    depth, tok, cot, w_in, w_out, tok_all, cot_all, in_all, out_all,
    raw, flat, stage, tok_send, tok_recv, w_send, w_recv, own_sem, raw_sem,
):
    y, r, z, same_chip, across, diagonal = neighbours()
    tokens, features = tok.shape
    rows = w_in.shape[0]
    lanes = in_all.shape[1]
    half = rows // 2
    block = w_in.shape[2]
    all_cols = stage.shape[1] // rows
    nnz = w_in.shape[1] // all_cols
    loads = [
        pltpu.make_async_copy(src, raw.at[a], raw_sem.at[a]) for a, src in enumerate((w_in, w_out))
    ]
    for load in loads:
        load.start()
    enter(
        [{"rows": same_chip}, {"rows": across}, {"rows": diagonal}, {"crop": 1 - y}]
        + [{"hid": (z + step) % depth} for step in range(1, depth)]
    )
    streams = ((tok, tok_all), (cot, cot_all))
    panels = ((flat.at[0], in_all), (flat.at[1], out_all))
    targets = ({"hid": z + 1}, {"hid": z - 1}, {"rows": across}, {"rows": same_chip})
    has_up, has_down = z + 1 < depth, z >= 1
    sends, local = [], []

    def launch(make, have=None):
        sends.append((make, have))
        if have is None:
            make().start()
        else:
            pl.when(have)(lambda: make().start())

    def piece(full, row, col):
        return full.at[span(row, tokens), span(col, features)]

    def pass_on(a, which, col, kind, have=None, own=False):
        def make():
            row = (r, across)[which]
            part = piece(streams[a][1], row, col)
            return remote(
                streams[a][0] if own else part,
                part,
                tok_send.at[a, which, col, kind],
                tok_recv.at[a, row, col],
                targets[kind],
            )

        launch(make, have)

    def await_piece(a, row, col, have=None):
        def wait():
            part = piece(streams[a][1], row, col)
            remote(
                part, part, tok_send.at[a, 0, 0, 3], tok_recv.at[a, row, col], {"rows": same_chip}
            ).wait_recv()

        if have is None:
            wait()
        else:
            pl.when(have)(wait)

    def half_rows(full, row, h):
        return full.at[pl.ds(pl.multiple_of(row * rows + h * half, half), half), :]

    def flatten(a):
        def turn(k, carry):
            for h in range(block // 128):
                part = raw[a, :, span(k, all_cols), h * 128 : (h + 1) * 128]
                stage[h] = part.astype(jnp.float32).reshape(rows * all_cols, 128)
            for c in range(all_cols):
                for h in range(block // 128):
                    flat[a, :, pl.ds(pl.multiple_of((c * nnz + k) * block + h * 128, 128), 128)] = stage[
                        h, pl.ds(c, rows, stride=all_cols), :
                    ].astype(jnp.bfloat16)
            return carry

        lax.fori_loop(0, nnz, turn, 0)

    def give_weights(a):
        src, full = panels[a]
        loads[a].wait()
        flatten(a)
        for slot, dest in ((1, across), (2, diagonal)):
            launch(
                lambda slot=slot, dest=dest: remote(
                    src.at[span(y, half), span(dest, lanes)],
                    half_rows(full, r, y),
                    w_send.at[a, slot],
                    w_recv.at[a, r, y],
                    {"rows": dest},
                )
            )
        launch(
            lambda: remote(
                src.at[:, span(same_chip, lanes)],
                full.at[span(r, rows), :],
                w_send.at[a, 0],
                w_recv.at[a, r, 0],
                {"rows": same_chip},
            )
        )
        keep = pltpu.make_async_copy(
            src.at[:, span(r, lanes)], full.at[span(r, rows), :], own_sem.at[a, 1]
        )
        keep.start()
        local.append(keep)

    def mirror_weights(a):
        full = panels[a][1]
        for slot, row in ((3, across), (4, diagonal)):
            part = half_rows(full, row, y)
            remote(part, part, w_send.at[a, slot], w_recv.at[a, row, y], {"rows": row}).wait_recv()
            launch(
                lambda slot=slot, row=row, part=part: remote(
                    part, part, w_send.at[a, slot], w_recv.at[a, row, y], {"crop": 1 - y}
                )
            )

    def line_step(step):
        for below in (True, False):
            col = z - step if below else z + step
            have = col >= 0 if below else col < depth
            onward = jnp.logical_and(have, has_up if below else has_down)
            for a, which in ((0, 0), (1, 0), (1, 1)):
                await_piece(a, (r, across)[which], col, have)
                pass_on(a, which, col, 0 if below else 1, onward)
                if a == 0:
                    pass_on(a, which, col, 2, have)
                pass_on(a, which, col, 3, have)

    for a, kind in ((1, 2), (0, 0), (0, 1), (1, 0), (1, 1), (0, 2), (0, 3), (1, 3)):
        pass_on(a, 0, z, kind, (has_up, has_down, None, None)[kind], own=True)
    for a in range(2):
        keep = pltpu.make_async_copy(streams[a][0], piece(streams[a][1], r, z), own_sem.at[a, 0])
        keep.start()
        local.append(keep)
    give_weights(0)
    await_piece(1, across, z)
    for kind in (0, 1, 3):
        pass_on(1, 1, z, kind, (has_up, has_down, None, None)[kind])
    give_weights(1)
    for step in range(1, depth):
        line_step(step)
        if step <= 2:
            mirror_weights(step - 1)
    for a in range(depth - 1, 2):
        mirror_weights(a)
    for step in range(depth):
        col = (z + step) % depth
        await_piece(0, across, col)
        pass_on(0, 1, col, 3)
    for a in range(2):
        full = panels[a][1]
        part = full.at[span(same_chip, rows), :]
        remote(
            part, part, w_send.at[a, 0], w_recv.at[a, same_chip, 0], {"rows": same_chip}
        ).wait_recv()
        for row in (across, diagonal):
            part = half_rows(full, row, 1 - y)
            remote(
                part, part, w_send.at[a, 0], w_recv.at[a, row, 1 - y], {"crop": 1 - y}
            ).wait_recv()
        for row in (same_chip, diagonal):
            for step in range(depth):
                await_piece(a, row, (z + step) % depth)
    for copy in local:
        copy.wait()
    for make, have in sends:
        if have is None:
            make().wait_send()
        else:
            pl.when(have)(lambda make=make: make().wait_send())


def nt(a, b):
    return lax.dot_general(a, b, (((1,), (1,)), ((), ())), preferred_element_type=jnp.float32)


def tn(a, b):
    return lax.dot_general(a, b, (((0,), (0,)), ((), ())), preferred_element_type=jnp.float32)


def column_math(width, block, cols, nnz, ids, tok, cot, w_in, w_out, taps, kern, mixed, pgrad, pre_s, act_s, slope_s, mg_s, gw):
    count = tok.shape[1]
    me = lax.axis_index("rows")
    place = lax.broadcasted_iota(jnp.int32, (count, block), 0) % width

    def spread(value):
        before = jnp.where(place == 0, 0.0, pltpu.roll(value, 1, 0))
        after = jnp.where(place == width - 1, 0.0, pltpu.roll(value, count - 1, 0))
        return (before, value, after)

    def stack_rows(up, mid, down):
        edge = jnp.zeros((width, block), jnp.float32)
        return (
            mid
            + jnp.concatenate([edge, up[:-width]], axis=0)
            + jnp.concatenate([down[width:], edge], axis=0)
        )

    def feats(c, k):
        return ids[k, me * cols + c]

    def panel(c, k):
        return span(c * nnz + k, block)

    def tap(c, a, b):
        row = 3 * (a + 1) + (b + 1)
        return taps[row : row + 1, span(me * cols + c, block)]

    def forward(c, ready=None):
        hidden = span(c, block)
        pre = jnp.dot(tok[feats(c, 0)], w_in[c * nnz], preferred_element_type=jnp.float32)
        for k in range(1, nnz):
            pre += jnp.dot(tok[feats(c, k)], w_in[c * nnz + k], preferred_element_type=jnp.float32)
        pre_s[...] = pre
        p = pre_s[...]
        t = jnp.tanh(root_two_pi * (p + cubic_coef * p * p * p))
        act_s[...] = (0.5 * p * (1.0 + t)).astype(jnp.bfloat16).astype(jnp.float32)
        slope_s[...] = 0.5 * (1.0 + t) + 0.5 * p * (1.0 - t * t) * root_two_pi * (
            1.0 + 3.0 * cubic_coef * p * p
        )
        acts = spread(act_s[...])
        mixed[:, hidden] = stack_rows(
            *[sum(tap(c, a, b) * acts[b + 1] for b in (-1, 0, 1)) for a in (-1, 0, 1)]
        ).astype(jnp.bfloat16)
        if ready is not None:
            ready()

    def backward(c):
        hidden = span(c, block)
        mg = nt(cot[feats(c, 0)], w_out[:, panel(c, 0)])
        for k in range(1, nnz):
            mg += nt(cot[feats(c, k)], w_out[:, panel(c, k)])
        mg_s[...] = mg.astype(jnp.bfloat16).astype(jnp.float32)
        acts = spread(act_s[...])
        grads = mg_s[...]
        for b in (-1, 0, 1):
            seen = acts[b + 1]
            sums = (
                jnp.sum(seen[:-width] * grads[width:], axis=0, keepdims=True),
                jnp.sum(seen * grads, axis=0, keepdims=True),
                jnp.sum(seen[width:] * grads[:-width], axis=0, keepdims=True),
            )
            for a in (-1, 0, 1):
                row = 3 * (a + 1) + (b + 1)
                kern[row : row + 1, hidden] = sums[a + 1] * loss_scale
        backs = spread(mg_s[...])
        gathered = stack_rows(
            *[sum(tap(c, a, b) * backs[1 - b] for b in (-1, 0, 1)) for a in (1, 0, -1)]
        )
        pgrad[:, hidden] = (gathered * slope_s[...]).astype(jnp.bfloat16)

    def grad_out(c):
        left = mixed[:, span(c, block)]
        for k in range(nnz):
            gw[1, :, panel(c, k)] = (tn(left, cot[feats(c, k)]) * loss_scale).astype(jnp.bfloat16)

    def grad_in(c):
        right = pgrad[:, span(c, block)]
        for k in range(nnz):
            gw[0, :, panel(c, k)] = (tn(tok[feats(c, k)], right) * loss_scale).astype(jnp.bfloat16)

    limit = tok.shape[0] ** 2

    def token_grad(g):
        total = jnp.zeros((count, block), jnp.float32)
        for c in range(cols):
            at = cols * nnz
            for k in range(nnz):
                apart = ids[k, me * cols + c] - g
                same = 1 - lax.div(apart * apart + (limit - 1), jnp.int32(limit))
                at += same * (c * nnz + k - at)
            total += nt(pgrad[:, span(c, block)], w_in[at])
        return total.astype(jnp.bfloat16)

    return forward, backward, grad_out, grad_in, token_grad


def grads_kernel(
    depth, width, block, cols, nnz, ids, tok_h, cot_h, in_h, out_h, taps,
    dx_mine, mine, kern_all,
    tok, cot, w_in, w_out, kern, mixed, pgrad, pre_s, act_s, slope_s, mg_s, gw, gw_part,
    dx, dx_near, dx_half, dx_far, dx_sum, dx_last, kern_own, kern_part,
    dx_send, dx_recv, far_send, far_recv, gw_send, gw_recv, part_send, part_recv,
    kern_send, kern_recv, load_sem,
):
    y, r, z, same_chip, across, diagonal = neighbours()
    group = [same_chip, across, diagonal]
    tokens, features = dx_mine.shape
    rows = mine.shape[1]
    half = block // 2
    lanes = nnz * block
    per_part = features // block
    def stack(i, src, dst, at):
        return pltpu.make_async_copy(src.at[:, span(at, block)], dst.at[at], load_sem.at[i, at])

    def each(i, act):
        src, dst, many = ((tok_h, tok, tok.shape[0]), (in_h, w_in, cols * nnz), (cot_h, cot, cot.shape[0]))[i]

        def turn(at, carry):
            act(stack(i, src, dst, at))
            return carry

        lax.fori_loop(0, many, turn, 0)

    out_load = pltpu.make_async_copy(out_h, w_out, load_sem.at[3, 0])
    for i in range(3):
        each(i, lambda copy: copy.start())
    out_load.start()
    w_in[cols * nnz] = jnp.zeros((block, block), jnp.bfloat16)
    kern[...] = jnp.zeros_like(kern)
    enter(
        [{"rows": row} for row in group]
        + [{"crop": 1 - y}]
        + [{"hid": (z + step) % depth} for step in range(1, depth)]
    )
    started = []

    def go(*args):
        copy = remote(*args)
        copy.start()
        started.append(copy)

    def arrived(ref, send_sem, recv_sem, target):
        remote(ref, ref, send_sem, recv_sem, target).wait_recv()

    forward, backward, grad_out, grad_in, token_grad = column_math(
        width, block, cols, nnz, ids, tok, cot, w_in, w_out, taps, kern, mixed, pgrad,
        pre_s, act_s, slope_s, mg_s, gw,
    )

    def give(a, c):
        go(
            gw.at[a, span(1 - y, half), span(c, lanes)],
            gw_part.at[a, c],
            gw_send.at[a, c],
            gw_recv.at[a, c],
            {"crop": 1 - y},
        )

    def settle(a, c):
        arrived(gw_part.at[a, c], gw_send.at[a, c], gw_recv.at[a, c], {"crop": 1 - y})
        gw_part[a, c] = (
            gw[a, span(y, half), span(c, lanes)].astype(jnp.float32) + gw_part[a, c].astype(jnp.float32)
        ).astype(jnp.bfloat16)
        at = span(r * cols + c, lanes)
        for slot, row in enumerate((across, diagonal, same_chip)):
            go(
                gw_part.at[a, c, span(row, rows), :],
                mine.at[a, :, at],
                part_send.at[a, c, slot],
                part_recv.at[a, c, slot],
                {"rows": row},
            )
        mine[a, :, at] = gw_part[a, c, span(r, rows), :]

    def part_of(i):
        return (z + 1 + i) % depth

    def lanes_of(i):
        return span(part_of(i), features)

    each(0, lambda copy: copy.wait())
    each(1, lambda copy: copy.wait())
    forward(0, lambda: each(2, lambda copy: copy.wait()))
    grad_out(0)
    give(1, 0)
    out_load.wait()
    backward(0)
    grad_in(0)
    give(0, 0)

    def one_column(c, carry):
        forward(c)
        grad_out(c)
        backward(c)
        grad_in(c)
        return carry

    near = ((0, diagonal), (1, same_chip))

    def near_copy(slot, row, i):
        at = lanes_of(i)
        return remote(
            dx.at[span(row, tokens), at],
            dx_near.at[slot, :, at],
            dx_send.at[slot, i],
            dx_recv.at[slot, i],
            {"rows": same_chip},
        )

    def pass_half(i):
        near_copy(0, diagonal, i).wait_recv()
        at = lanes_of(i)
        dx_half[:, at] = (
            dx[span(across, tokens), at].astype(jnp.float32) + dx_near[0, :, at].astype(jnp.float32)
        ).astype(jnp.bfloat16)
        go(dx_half.at[:, at], dx_far.at[:, at], far_send.at[0, i], far_recv.at[0, i], {"rows": across})

    for c in range(1, cols):
        lax.fori_loop(c, c + 1, one_column, 0)
        if c == cols - 1:
            settle(1, 0)
            kern_own[...] = kern[...].astype(jnp.bfloat16)
            go(kern_own, kern_part.at[1, 0], kern_send.at[0], kern_recv.at[1, 0], {"crop": 1 - y})
        give(1, c)
        give(0, c)
    settle(0, 0)
    for i in range(depth):

        def one_block(j, carry):
            g = part_of(i) * per_part + j
            dx[:, span(g, block)] = token_grad(g)
            return carry

        lax.fori_loop(0, per_part, one_block, 0)
        for slot, row in near:
            near_copy(slot, row, i).start()
        if i > 0:
            pass_half(i - 1)
    pass_half(depth - 1)

    def pass_sum(i):
        at = lanes_of(i)
        near_copy(1, same_chip, i).wait_recv()
        arrived(dx_far.at[:, at], far_send.at[0, i], far_recv.at[0, i], {"rows": across})
        dx_sum[i] = (
            dx[span(r, tokens), at].astype(jnp.float32)
            + dx_near[1, :, at].astype(jnp.float32)
            + dx_far[:, at].astype(jnp.float32)
        ).astype(jnp.bfloat16)
        if i < depth - 1:
            go(
                dx_sum.at[i],
                dx_last.at[i],
                far_send.at[1, i],
                far_recv.at[1, i],
                {"hid": part_of(i)},
            )

    waits = [(a, c) for c in range(1, cols) for a in (1, 0)]
    sums = list(range(depth))
    while len(waits) > 2:
        settle(*waits.pop(0))
        if sums:
            pass_sum(sums.pop(0))
    while sums:
        pass_sum(sums.pop(0))
    arrived(kern_part.at[1, 0], kern_send.at[0], kern_recv.at[1, 0], {"crop": 1 - y})
    kern_part[0, r] = (
        kern_own[...].astype(jnp.float32) + kern_part[1, 0].astype(jnp.float32)
    ).astype(jnp.bfloat16)
    for slot, row in enumerate(group):
        go(
            kern_part.at[0, r],
            kern_part.at[0, r],
            kern_send.at[slot + 1],
            kern_recv.at[0, r],
            {"rows": row},
        )
    settle(*waits.pop(0))
    total = dx_sum[depth - 1].astype(jnp.float32)
    for step in range(depth - 1):
        arrived(dx_last.at[step], far_send.at[1, step], far_recv.at[1, step], {"hid": part_of(step)})
        total += dx_last[step].astype(jnp.float32)
    dx_mine[...] = total.astype(jnp.bfloat16)
    for row in group:
        arrived(kern_part.at[0, row], kern_send.at[0], kern_recv.at[0, row], {"rows": same_chip})
    wide = kern.shape[1]
    for row in range(4):
        kern_all[:, row * wide : (row + 1) * wide] = kern_part[0, row].astype(jnp.float32)
    for a, c in waits:
        settle(a, c)
    for a in (1, 0):
        for c in range(cols):
            for slot, row in enumerate((across, diagonal, same_chip)):
                arrived(
                    mine.at[a, :, span(row * cols + c, lanes)],
                    part_send.at[a, c, slot],
                    part_recv.at[a, c, slot],
                    {"rows": row},
                )
    for i in range(depth):
        for slot, row in near:
            near_copy(slot, row, i).wait_send()
    for copy in started:
        copy.wait_send()


def finish_kernel(
    all_cols, nnz, mine, dx_mine, kern_all, in_grad, out_grad, dx_grad, kern_grad
):
    block = in_grad.shape[2]
    dx_grad[...] = dx_mine[...]
    kern_grad[...] = kern_all[: kern_grad.shape[0]]
    for src, dst in ((mine.at[0], in_grad), (mine.at[1], out_grad)):
        for c in range(all_cols):
            for k in range(nnz):
                at = (c * nnz + k) * block
                dst[:, k * all_cols + c, :] = src[:, at : at + block].astype(jnp.float32)


def split_hidden(tokens, cotangent, weight_in, weight_out, mix_kernel, block_rows):
    n_rows, depth = lax.axis_size("rows"), lax.axis_size("hid")
    _, height, width, features = tokens.shape
    rows, all_cols, nnz, block = weight_in.shape
    count = height * width
    whole = count * n_rows
    model = features * depth
    cols = all_cols // n_rows
    lanes = cols * nnz * block
    hidden = cols * block
    bf16, f32 = jnp.bfloat16, jnp.float32
    dma, sds = pltpu.SemaphoreType.DMA, jax.ShapeDtypeStruct
    params = functools.partial(pltpu.CompilerParams, vmem_limit_bytes=60 * 1024 * 1024)
    tok_all, cot_all, in_all, out_all = pl.pallas_call(
        functools.partial(gather_kernel, depth),
        name="gather_parts",
        out_shape=[sds((whole, model), bf16)] * 2 + [sds((rows * n_rows, lanes), bf16)] * 2,
        in_specs=[ANY] * 4,
        out_specs=[ANY] * 4,
        scratch_shapes=[
            pltpu.VMEM((2, rows, nnz * all_cols, block), bf16),
            pltpu.VMEM((2, rows, all_cols * nnz * block), bf16),
            pltpu.VMEM((block // 128, rows * all_cols, 128), f32),
            dma((2, 2, depth, 4)),
            dma((2, n_rows, depth)),
            dma((2, 5)),
            dma((2, n_rows, 2)),
            dma((2, 2)),
            dma((2,)),
        ],
        compiler_params=params(collective_id=1, has_side_effects=True),
    )(
        tokens.reshape(count, features),
        cotangent.reshape(count, features),
        weight_in.transpose(0, 2, 1, 3).reshape(rows, nnz * all_cols, block),
        weight_out.transpose(0, 2, 1, 3).reshape(rows, nnz * all_cols, block),
    )
    out_rows = block // (n_rows * lax.axis_size("crop"))
    panel = nnz * block
    dx_mine, mine, kern_all = pl.pallas_call(
        functools.partial(grads_kernel, depth, width, block, cols, nnz),
        name="grads_and_sums",
        out_shape=[
            sds((count, features), bf16),
            sds((2, out_rows, all_cols * panel), bf16),
            sds((16, hidden * n_rows), f32),
        ],
        in_specs=[SMEM] + [ANY] * 4 + [VMEM],
        out_specs=[VMEM] * 3,
        scratch_shapes=[
            pltpu.VMEM((model // block, whole, block), bf16),
            pltpu.VMEM((model // block, whole, block), bf16),
            pltpu.VMEM((cols * nnz + 1, block, block), bf16),
            pltpu.VMEM((block, lanes), bf16),
            pltpu.VMEM((16, hidden), f32),
            pltpu.VMEM((whole, hidden), bf16),
            pltpu.VMEM((whole, hidden), bf16),
        ]
        + [pltpu.VMEM((whole, block), f32)] * 4
        + [
            pltpu.VMEM((2, block, lanes), bf16),
            pltpu.VMEM((2, cols, block // 2, panel), bf16),
            pltpu.VMEM((whole, model), bf16),
            pltpu.VMEM((2, count, model), bf16),
            pltpu.VMEM((count, model), bf16),
            pltpu.VMEM((count, model), bf16),
            pltpu.VMEM((depth, count, features), bf16),
            pltpu.VMEM((depth - 1, count, features), bf16),
            pltpu.VMEM((16, hidden), bf16),
            pltpu.VMEM((2, n_rows, 16, hidden), bf16),
            dma((2, depth)),
            dma((2, depth)),
            dma((2, depth)),
            dma((2, depth)),
            dma((2, cols)),
            dma((2, cols)),
            dma((2, cols, 3)),
            dma((2, cols, 3)),
            dma((4,)),
            dma((2, n_rows)),
            dma((4, max(model // block, cols * nnz))),
        ],
        compiler_params=params(collective_id=2, has_side_effects=True),
    )(block_rows.T, tok_all, cot_all, in_all, out_all, mix_kernel)
    step = 8
    part = pl.BlockSpec((count * step // out_rows, features), lambda i: (i, 0))
    flat_spec = pl.BlockSpec((2, step, all_cols * nnz * block), lambda i: (0, i, 0))
    grad_spec = pl.BlockSpec((step, nnz * all_cols, block), lambda i: (i, 0, 0))
    in_grad, out_grad, dx_grad, kern_grad = pl.pallas_call(
        functools.partial(finish_kernel, all_cols, nnz),
        name="finish_weights",
        grid=(out_rows // step,),
        out_shape=[sds((out_rows, nnz * all_cols, block), f32)] * 2
        + [sds((count, features), bf16), sds(mix_kernel.shape, f32)],
        in_specs=[flat_spec, part, VMEM],
        out_specs=[grad_spec] * 2 + [part, VMEM],
        compiler_params=params(),
    )(mine, dx_mine, kern_all)
    in_grad, out_grad = [
        grad.reshape(out_rows, nnz, all_cols, block).transpose(0, 2, 1, 3) for grad in (in_grad, out_grad)
    ]
    return (dx_grad.reshape(tokens.shape), in_grad, out_grad, kern_grad)


def padded(shard, sides, width):
    for axis, dim in sides:
        devices, length = (lax.axis_size(axis), shard.shape[dim])
        up = [(i, (i + 1) % devices) for i in range(devices - 1)]
        down = [(j, i) for i, j in up]
        last = lax.slice_in_dim(shard, length - width, length, axis=dim)
        initial = lax.slice_in_dim(shard, 0, width, axis=dim)
        before = lax.ppermute(last, axis, up)
        after = lax.ppermute(initial, axis, down)
        shard = jnp.concatenate([before, shard, after], axis=dim)
    return shard


def gelu_pair(preact):
    inner = root_two_pi * (preact + cubic_coef * preact * preact * preact)
    tanh_val = jnp.tanh(inner)
    gelu_out = 0.5 * preact * (1.0 + tanh_val)
    slopes = 0.5 * (1.0 + tanh_val) + 0.5 * preact * (1.0 - tanh_val * tanh_val) * root_two_pi * (
        1.0 + 3.0 * cubic_coef * preact * preact
    )
    return (gelu_out, slopes)


def on_device(tokens, cotangent, weight_in, weight_out, mix_kernel, block_rows):
    in_panel, out_panel = (
        lax.all_gather(weight_in, "rows", axis=0, tiled=True),
        lax.all_gather(weight_out, "rows", axis=0, tiled=True),
    )
    tok_full, cot_full = (
        lax.all_gather(tokens, "hid", axis=3, tiled=True),
        lax.all_gather(cotangent, "hid", axis=3, tiled=True),
    )
    crop_count, height, grid_width, depth_all = tok_full.shape
    tok_count = crop_count * height * grid_width
    block_size = in_panel.shape[0]
    col_count = in_panel.shape[1]
    nnz_count = in_panel.shape[2]
    block_count = depth_all // block_size
    hidden_local = col_count * block_size
    flat_rows = block_rows.reshape(-1)
    in_select = jnp.take(
        tok_full.reshape(tok_count, block_count, block_size), flat_rows, axis=1
    ).reshape(tok_count, col_count, nnz_count, block_size)
    grad_select = jnp.take(
        cot_full.reshape(tok_count, block_count, block_size), flat_rows, axis=1
    ).reshape(tok_count, col_count, nnz_count, block_size)
    pre_act = jnp.einsum("tckb,bcke->tce", in_select, in_panel, preferred_element_type=jnp.float32)
    gelu_out, slopes = gelu_pair(pre_act)
    active = gelu_out.astype(jnp.bfloat16).reshape(crop_count, height, grid_width, hidden_local)
    act_rim = padded(active, (("rows", 1),), 1)
    mix_grad = (
        jnp.einsum("tckd,fckd->tcf", grad_select, out_panel, preferred_element_type=jnp.float32)
        .astype(jnp.bfloat16)
        .reshape(crop_count, height, grid_width, hidden_local)
    )
    grad_rim = padded(mix_grad, (("rows", 1),), 1)
    act_pad = jnp.pad(act_rim.astype(jnp.float32), ((0, 0), (0, 0), (1, 1), (0, 0)))
    grad_pad = jnp.pad(grad_rim.astype(jnp.float32), ((0, 0), (0, 0), (1, 1), (0, 0)))
    grad_grid = mix_grad.astype(jnp.float32)
    mix_sum = jnp.zeros((crop_count, height, grid_width, hidden_local), jnp.float32)
    act_grad = jnp.zeros((crop_count, height, grid_width, hidden_local), jnp.float32)
    kern_terms = []
    for row_off in range(3):
        for col_off in range(3):
            tap = mix_kernel[3 * row_off + col_off]
            shifted = act_pad[:, row_off : row_off + height, col_off : col_off + grid_width]
            mix_sum = mix_sum + tap * shifted
            act_grad = (
                act_grad
                + tap
                * grad_pad[
                    :, 2 - row_off : 2 - row_off + height, 2 - col_off : 2 - col_off + grid_width
                ]
            )
            kern_terms.append(jnp.sum(shifted * grad_grid, axis=(0, 1, 2)))
    kern_local = jnp.stack(kern_terms, axis=0) * loss_scale
    mix_out = mix_sum.astype(jnp.bfloat16).reshape(tok_count, col_count, block_size)
    pre_grad = (act_grad.reshape(tok_count, col_count, block_size) * slopes).astype(jnp.bfloat16)
    kern_total = lax.psum(kern_local.astype(jnp.bfloat16), ("crop", "rows")).astype(jnp.float32)
    back_select = jnp.einsum(
        "tce,bcke->tckb", pre_grad, in_panel, preferred_element_type=jnp.float32
    )
    one_hot = (
        block_rows[:, :, None] == jnp.arange(block_count, dtype=jnp.int32)[None, None, :]
    ).astype(jnp.float32)
    token_terms = jnp.einsum(
        "tckb,ckr->trb", back_select, one_hot, precision=lax.Precision.HIGHEST
    ).reshape(crop_count, height, grid_width, depth_all)
    grad_tokens = lax.psum_scatter(
        token_terms.astype(jnp.bfloat16), "hid", scatter_dimension=3, tiled=True
    )
    first_term = jnp.einsum(
        "tckb,tce->bcke", in_select, pre_grad, preferred_element_type=jnp.float32
    )
    second_term = jnp.einsum(
        "tcf,tckd->fckd", mix_out, grad_select, preferred_element_type=jnp.float32
    )
    share_sums = lax.psum_scatter(
        (jnp.stack([first_term, second_term], axis=1) * loss_scale).astype(jnp.bfloat16),
        ("crop", "rows"),
        scatter_dimension=0,
        tiled=True,
    ).astype(jnp.float32)
    return (grad_tokens, share_sums[:, 0], share_sums[:, 1], kern_total)


def solution(mesh):
    placed = (
        P("crop", "rows", None, "hid"),
        P("crop", "rows", None, "hid"),
        P("rows", "hid", None, None),
        P("rows", "hid", None, None),
        P(None, "hid"),
        P("hid", None),
    )
    n_crop, n_rows = mesh.shape["crop"], mesh.shape["rows"]
    n_hid = mesh.shape["hid"]

    def step(tokens, cotangent, weight_in, weight_out, mix_kernel, block_rows):
        fits = (
            n_crop == 2
            and n_rows == 4
            and tokens.shape[0] == 1
            and weight_in.shape[1] % n_rows == 0
            and tokens.shape[1] * tokens.shape[2] * n_rows * tokens.shape[3] * n_hid <= 2**22
        )
        chosen = split_hidden if fits else on_device
        return chosen(tokens, cotangent, weight_in, weight_out, mix_kernel, block_rows)

    return jax.shard_map(
        step,
        mesh=mesh,
        in_specs=placed,
        out_specs=(
            P("crop", "rows", None, "hid"),
            P(("crop", "rows"), "hid", None, None),
            P(("crop", "rows"), "hid", None, None),
            P(None, "hid"),
        ),
        check_vma=False,
    )
```

```python
import functools

import jax
import jax.numpy as jnp
from jax import lax
from jax.experimental import pallas as pl
from jax.experimental.pallas import tpu as pltpu
from jax.sharding import PartitionSpec as P

root_two_pi = 0.7978845608
cubic_coef = 0.044715
loss_scale = 0.03125

MESH_ID = pl.DeviceIdType.MESH
ANY = pl.BlockSpec(memory_space=pl.ANY)
VMEM = pl.BlockSpec(memory_space=pltpu.VMEM)
SMEM = pl.BlockSpec(memory_space=pltpu.SMEM)


def span(start, size):
    return pl.ds(pl.multiple_of(start * size, size), size)


def neighbours():
    y, r, z = lax.axis_index("crop"), lax.axis_index("rows"), lax.axis_index("hid")
    x, core = r // 2, r % 2
    same_chip = x * 2 + (1 - core)
    across = (1 - x) * 2 + core
    diagonal = (1 - x) * 2 + (1 - core)
    return y, r, z, same_chip, across, diagonal


def enter(partners):
    barrier = pltpu.get_barrier_semaphore()
    for partner in partners:
        pl.semaphore_signal(barrier, inc=1, device_id=partner, device_id_type=MESH_ID)
    pl.semaphore_wait(barrier, len(partners))


def remote(src, dst, send_sem, recv_sem, target):
    return pltpu.make_async_remote_copy(
        src_ref=src,
        dst_ref=dst,
        send_sem=send_sem,
        recv_sem=recv_sem,
        device_id=target,
        device_id_type=MESH_ID,
    )


def gather_stage(
    depth, partners, tok_h, cot_h, in_h, out_h, tok, cot, w_in, w_out,
    raw, flat, stage, tok_send, tok_recv, w_send, w_recv, own_sem, raw_sem,
):
    y, r, z, same_chip, across, diagonal = neighbours()
    tokens, features = tok_h.shape
    rows = in_h.shape[0]
    half = rows // 2
    block = tok.shape[2]
    per_part = features // block
    panels_own = w_out.shape[0]
    all_cols = stage.shape[1] // rows
    nnz = in_h.shape[1] // all_cols
    own = [
        pltpu.make_async_copy(
            src.at[:, j * block : (j + 1) * block],
            full.at[z * per_part + j, span(r, tokens), :],
            own_sem.at[a, j],
        )
        for a, (src, full) in enumerate(((tok_h, tok), (cot_h, cot)))
        for j in range(per_part)
    ]
    loads = [
        pltpu.make_async_copy(src, raw.at[a], raw_sem.at[a]) for a, src in enumerate((in_h, out_h))
    ]
    for load in own + loads:
        load.start()
    enter(partners)
    for load in own:
        load.wait()
    streams = (tok, cot)
    panels = ((flat.at[0], w_in), (flat.at[1], w_out))
    targets = ({"hid": z + 1}, {"hid": z - 1}, {"rows": across}, {"rows": same_chip})
    has_up, has_down = z + 1 < depth, z >= 1
    sends, local = [], []

    def launch(make, have=None):
        sends.append((make, have))
        if have is None:
            make().start()
        else:
            pl.when(have)(lambda: make().start())

    def piece(full, row, col):
        return full.at[span(col, per_part), span(row, tokens), :]

    def pass_on(a, which, col, kind, have=None):
        def make():
            row = (r, across)[which]
            part = piece(streams[a], row, col)
            return remote(
                part,
                part,
                tok_send.at[a, which, col, kind],
                tok_recv.at[a, row, col],
                targets[kind],
            )

        launch(make, have)

    def await_piece(a, row, col, have=None):
        def wait():
            part = piece(streams[a], row, col)
            remote(
                part, part, tok_send.at[a, 0, 0, 3], tok_recv.at[a, row, col], {"rows": same_chip}
            ).wait_recv()

        if have is None:
            wait()
        else:
            pl.when(have)(wait)

    def half_rows(full, row, h):
        at = pl.ds(pl.multiple_of(row * rows + h * half, half), half)
        return full.at[pl.ds(0, panels_own), at, :]

    def whole_rows(full, row):
        return full.at[pl.ds(0, panels_own), span(row, rows), :]

    def flatten(a):
        def turn(k, carry):
            for h in range(block // 128):
                part = raw[a, :, span(k, all_cols), h * 128 : (h + 1) * 128]
                stage[h] = part.astype(jnp.float32).reshape(rows * all_cols, 128)
            for c in range(all_cols):
                for h in range(block // 128):
                    flat[a, c * nnz + k, :, h * 128 : (h + 1) * 128] = stage[
                        h, pl.ds(c, rows, stride=all_cols), :
                    ].astype(jnp.bfloat16)
            return carry

        lax.fori_loop(0, nnz, turn, 0)

    def give_weights(a):
        src, full = panels[a]
        loads[a].wait()
        flatten(a)
        for slot, dest in ((1, across), (2, diagonal)):
            launch(
                lambda slot=slot, dest=dest: remote(
                    src.at[span(dest, panels_own), span(y, half), :],
                    half_rows(full, r, y),
                    w_send.at[a, slot],
                    w_recv.at[a, r, y],
                    {"rows": dest},
                )
            )
        launch(
            lambda: remote(
                src.at[span(same_chip, panels_own)],
                whole_rows(full, r),
                w_send.at[a, 0],
                w_recv.at[a, r, 0],
                {"rows": same_chip},
            )
        )
        keep = pltpu.make_async_copy(
            src.at[span(r, panels_own)], whole_rows(full, r), own_sem.at[a, per_part]
        )
        keep.start()
        local.append(keep)

    def mirror_weights(a):
        full = panels[a][1]
        for slot, row in ((3, across), (4, diagonal)):
            part = half_rows(full, row, y)
            remote(part, part, w_send.at[a, slot], w_recv.at[a, row, y], {"rows": row}).wait_recv()
            launch(
                lambda slot=slot, row=row, part=part: remote(
                    part, part, w_send.at[a, slot], w_recv.at[a, row, y], {"crop": 1 - y}
                )
            )

    def line_step(step):
        for below in (True, False):
            col = z - step if below else z + step
            have = col >= 0 if below else col < depth
            onward = jnp.logical_and(have, has_up if below else has_down)
            for a, which in ((0, 0), (1, 0), (1, 1)):
                await_piece(a, (r, across)[which], col, have)
                pass_on(a, which, col, 0 if below else 1, onward)
                if a == 0:
                    pass_on(a, which, col, 2, have)
                pass_on(a, which, col, 3, have)

    for a, kind in ((1, 2), (0, 0), (0, 1), (1, 0), (1, 1), (0, 2), (0, 3), (1, 3)):
        pass_on(a, 0, z, kind, (has_up, has_down, None, None)[kind])
    give_weights(0)
    await_piece(1, across, z)
    for kind in (0, 1, 3):
        pass_on(1, 1, z, kind, (has_up, has_down, None, None)[kind])
    give_weights(1)
    for step in range(1, depth):
        line_step(step)
        if step <= 2:
            mirror_weights(step - 1)
    for a in range(depth - 1, 2):
        mirror_weights(a)
    for step in range(depth):
        col = (z + step) % depth
        await_piece(0, across, col)
        pass_on(0, 1, col, 3)
    for a in range(2):
        full = panels[a][1]
        part = whole_rows(full, same_chip)
        remote(
            part, part, w_send.at[a, 0], w_recv.at[a, same_chip, 0], {"rows": same_chip}
        ).wait_recv()
        for row in (across, diagonal):
            part = half_rows(full, row, 1 - y)
            remote(
                part, part, w_send.at[a, 0], w_recv.at[a, row, 1 - y], {"crop": 1 - y}
            ).wait_recv()
        for row in (same_chip, diagonal):
            for step in range(depth):
                await_piece(a, row, (z + step) % depth)
    for copy in local:
        copy.wait()

    def drain():
        for make, have in sends:
            if have is None:
                make().wait_send()
            else:
                pl.when(have)(lambda make=make: make().wait_send())

    return drain


def nt(a, b):
    return lax.dot_general(a, b, (((1,), (1,)), ((), ())), preferred_element_type=jnp.float32)


def tn(a, b):
    return lax.dot_general(a, b, (((0,), (0,)), ((), ())), preferred_element_type=jnp.float32)


def column_math(width, block, cols, nnz, ids, tok, cot, w_in, w_out, taps, kern, mixed, pgrad, pre_s, act_s, slope_s, mg_s, gw):
    count = tok.shape[1]
    me = lax.axis_index("rows")
    place = lax.broadcasted_iota(jnp.int32, (count, block), 0) % width

    def spread(value):
        before = jnp.where(place == 0, 0.0, pltpu.roll(value, 1, 0))
        after = jnp.where(place == width - 1, 0.0, pltpu.roll(value, count - 1, 0))
        return (before, value, after)

    def stack_rows(up, mid, down):
        edge = jnp.zeros((width, block), jnp.float32)
        return (
            mid
            + jnp.concatenate([edge, up[:-width]], axis=0)
            + jnp.concatenate([down[width:], edge], axis=0)
        )

    def feats(c, k):
        return ids[k, me * cols + c]

    def panel(c, k):
        return span(c * nnz + k, block)

    def tap(c, a, b):
        row = 3 * (a + 1) + (b + 1)
        return taps[row : row + 1, span(me * cols + c, block)]

    def forward(c):
        hidden = span(c, block)
        pre = jnp.dot(tok[feats(c, 0)], w_in[c * nnz], preferred_element_type=jnp.float32)
        for k in range(1, nnz):
            pre += jnp.dot(tok[feats(c, k)], w_in[c * nnz + k], preferred_element_type=jnp.float32)
        pre_s[...] = pre
        p = pre_s[...]
        t = jnp.tanh(root_two_pi * (p + cubic_coef * p * p * p))
        act_s[...] = (0.5 * p * (1.0 + t)).astype(jnp.bfloat16).astype(jnp.float32)
        slope_s[...] = 0.5 * (1.0 + t) + 0.5 * p * (1.0 - t * t) * root_two_pi * (
            1.0 + 3.0 * cubic_coef * p * p
        )
        acts = spread(act_s[...])
        mixed[:, hidden] = stack_rows(
            *[sum(tap(c, a, b) * acts[b + 1] for b in (-1, 0, 1)) for a in (-1, 0, 1)]
        ).astype(jnp.bfloat16)

    def backward(c):
        hidden = span(c, block)
        mg = nt(cot[feats(c, 0)], w_out[c * nnz])
        for k in range(1, nnz):
            mg += nt(cot[feats(c, k)], w_out[c * nnz + k])
        mg_s[...] = mg.astype(jnp.bfloat16).astype(jnp.float32)
        acts = spread(act_s[...])
        grads = mg_s[...]
        for b in (-1, 0, 1):
            seen = acts[b + 1]
            sums = (
                jnp.sum(seen[:-width] * grads[width:], axis=0, keepdims=True),
                jnp.sum(seen * grads, axis=0, keepdims=True),
                jnp.sum(seen[width:] * grads[:-width], axis=0, keepdims=True),
            )
            for a in (-1, 0, 1):
                row = 3 * (a + 1) + (b + 1)
                kern[row : row + 1, hidden] = sums[a + 1] * loss_scale
        backs = spread(mg_s[...])
        gathered = stack_rows(
            *[sum(tap(c, a, b) * backs[1 - b] for b in (-1, 0, 1)) for a in (1, 0, -1)]
        )
        pgrad[:, hidden] = (gathered * slope_s[...]).astype(jnp.bfloat16)

    def grad_out(c):
        left = mixed[:, span(c, block)]
        for k in range(nnz):
            gw[1, :, panel(c, k)] = (tn(left, cot[feats(c, k)]) * loss_scale).astype(jnp.bfloat16)

    def grad_in(c):
        right = pgrad[:, span(c, block)]
        for k in range(nnz):
            gw[0, :, panel(c, k)] = (tn(tok[feats(c, k)], right) * loss_scale).astype(jnp.bfloat16)

    limit = tok.shape[0] ** 2

    def token_grad(g):
        total = jnp.zeros((count, block), jnp.float32)
        for c in range(cols):
            at = cols * nnz
            for k in range(nnz):
                apart = ids[k, me * cols + c] - g
                same = 1 - lax.div(apart * apart + (limit - 1), jnp.int32(limit))
                at += same * (c * nnz + k - at)
            total += nt(pgrad[:, span(c, block)], w_in[at])
        return total.astype(jnp.bfloat16)

    return forward, backward, grad_out, grad_in, token_grad


def grads_kernel(
    depth, width, block, cols, nnz, ids, tok_h, cot_h, in_h, out_h, taps,
    dx_mine, mine, kern_all,
    tok, cot, w_in, w_out, raw, flat, stage, tok_send, tok_recv, w_send, w_recv, own_sem, raw_sem, kern, mixed, pgrad, pre_s, act_s, slope_s, mg_s, gw, gw_part,
    dx, dx_near, dx_half, dx_far, dx_sum, dx_last, kern_own, kern_part,
    dx_send, dx_recv, far_send, far_recv, gw_send, gw_recv, part_send, part_recv,
    kern_send, kern_recv,
):
    y, r, z, same_chip, across, diagonal = neighbours()
    group = [same_chip, across, diagonal]
    tokens, features = dx_mine.shape
    rows = mine.shape[1]
    half = block // 2
    lanes = nnz * block
    per_part = features // block
    w_in[cols * nnz] = jnp.zeros((block, block), jnp.bfloat16)
    kern[...] = jnp.zeros_like(kern)
    drain = gather_stage(
        depth,
        [{"rows": row} for row in group]
        + [{"crop": 1 - y}]
        + [{"hid": (z + step) % depth} for step in range(1, depth)],
        tok_h, cot_h, in_h, out_h, tok, cot, w_in, w_out,
        raw, flat, stage, tok_send, tok_recv, w_send, w_recv, own_sem, raw_sem,
    )
    started = []

    def go(*args):
        copy = remote(*args)
        copy.start()
        started.append(copy)

    def arrived(ref, send_sem, recv_sem, target):
        remote(ref, ref, send_sem, recv_sem, target).wait_recv()

    forward, backward, grad_out, grad_in, token_grad = column_math(
        width, block, cols, nnz, ids, tok, cot, w_in, w_out, taps, kern, mixed, pgrad,
        pre_s, act_s, slope_s, mg_s, gw,
    )

    def give_copy(a, c):
        return remote(
            gw.at[a, span(1 - y, half), span(c, lanes)],
            gw_part.at[a, c],
            gw_send.at[a, c],
            gw_recv.at[a, c],
            {"crop": 1 - y},
        )

    def give(a, c):
        give_copy(a, c).start()

    def settle(a, c):
        arrived(gw_part.at[a, c], gw_send.at[a, c], gw_recv.at[a, c], {"crop": 1 - y})
        gw_part[a, c] = (
            gw[a, span(y, half), span(c, lanes)].astype(jnp.float32) + gw_part[a, c].astype(jnp.float32)
        ).astype(jnp.bfloat16)
        at = span(r * cols + c, lanes)
        for slot, row in enumerate((across, diagonal, same_chip)):
            go(
                gw_part.at[a, c, span(row, rows), :],
                mine.at[a, :, at],
                part_send.at[a, c, slot],
                part_recv.at[a, c, slot],
                {"rows": row},
            )
        mine[a, :, at] = gw_part[a, c, span(r, rows), :]

    def part_of(i):
        return (z + 1 + i) % depth

    def lanes_of(i):
        return span(part_of(i), features)

    forward(0)
    grad_out(0)
    give(1, 0)
    backward(0)
    grad_in(0)
    give(0, 0)

    def one_column(c, carry):
        forward(c)
        grad_out(c)
        backward(c)
        grad_in(c)
        return carry

    near = ((0, diagonal), (1, same_chip))

    def near_copy(slot, row, i):
        at = lanes_of(i)
        return remote(
            dx.at[span(row, tokens), at],
            dx_near.at[slot, :, at],
            dx_send.at[slot, i],
            dx_recv.at[slot, i],
            {"rows": same_chip},
        )

    def pass_half(i):
        near_copy(0, diagonal, i).wait_recv()
        at = lanes_of(i)
        dx_half[:, at] = (
            dx[span(across, tokens), at].astype(jnp.float32) + dx_near[0, :, at].astype(jnp.float32)
        ).astype(jnp.bfloat16)
        go(dx_half.at[:, at], dx_far.at[:, at], far_send.at[0, i], far_recv.at[0, i], {"rows": across})

    def inner_column(c, carry):
        one_column(c, carry)
        for a in (1, 0):
            give_copy(a, c).start()
        return carry

    lax.fori_loop(1, cols - 1, inner_column, 0)
    for c in range(cols - 1, cols):
        lax.fori_loop(c, c + 1, one_column, 0)
        if c == cols - 1:
            settle(1, 0)
            kern_own[...] = kern[...].astype(jnp.bfloat16)
            go(kern_own, kern_part.at[1, 0], kern_send.at[0], kern_recv.at[1, 0], {"crop": 1 - y})
        give(1, c)
        give(0, c)
    settle(0, 0)
    for i in range(depth):

        def one_block(j, carry):
            g = part_of(i) * per_part + j
            dx[:, span(g, block)] = token_grad(g)
            return carry

        lax.fori_loop(0, per_part, one_block, 0)
        for slot, row in near:
            near_copy(slot, row, i).start()
        if i > 0:
            pass_half(i - 1)
    pass_half(depth - 1)

    def pass_sum(i):
        at = lanes_of(i)
        near_copy(1, same_chip, i).wait_recv()
        arrived(dx_far.at[:, at], far_send.at[0, i], far_recv.at[0, i], {"rows": across})
        dx_sum[i] = (
            dx[span(r, tokens), at].astype(jnp.float32)
            + dx_near[1, :, at].astype(jnp.float32)
            + dx_far[:, at].astype(jnp.float32)
        ).astype(jnp.bfloat16)
        if i < depth - 1:
            go(
                dx_sum.at[i],
                dx_last.at[i],
                far_send.at[1, i],
                far_recv.at[1, i],
                {"hid": part_of(i)},
            )

    waits = [(a, c) for c in range(1, cols) for a in (1, 0)]
    sums = list(range(depth))
    while len(waits) > 2:
        settle(*waits.pop(0))
        if sums:
            pass_sum(sums.pop(0))
    while sums:
        pass_sum(sums.pop(0))
    arrived(kern_part.at[1, 0], kern_send.at[0], kern_recv.at[1, 0], {"crop": 1 - y})
    kern_part[0, r] = (
        kern_own[...].astype(jnp.float32) + kern_part[1, 0].astype(jnp.float32)
    ).astype(jnp.bfloat16)
    for slot, row in enumerate(group):
        go(
            kern_part.at[0, r],
            kern_part.at[0, r],
            kern_send.at[slot + 1],
            kern_recv.at[0, r],
            {"rows": row},
        )
    settle(*waits.pop(0))
    total = dx_sum[depth - 1].astype(jnp.float32)
    for step in range(depth - 1):
        arrived(dx_last.at[step], far_send.at[1, step], far_recv.at[1, step], {"hid": part_of(step)})
        total += dx_last[step].astype(jnp.float32)
    dx_mine[...] = total.astype(jnp.bfloat16)
    for row in group:
        arrived(kern_part.at[0, row], kern_send.at[0], kern_recv.at[0, row], {"rows": same_chip})
    wide = kern.shape[1]
    for row in range(4):
        kern_all[:, row * wide : (row + 1) * wide] = kern_part[0, row].astype(jnp.float32)
    for a, c in waits:
        settle(a, c)
    for a in (1, 0):
        for c in range(cols):
            for slot, row in enumerate((across, diagonal, same_chip)):
                arrived(
                    mine.at[a, :, span(row * cols + c, lanes)],
                    part_send.at[a, c, slot],
                    part_recv.at[a, c, slot],
                    {"rows": row},
                )
    for i in range(depth):
        for slot, row in near:
            near_copy(slot, row, i).wait_send()
    for copy in started:
        copy.wait_send()
    for a in range(2):
        for c in range(cols):
            give_copy(a, c).wait_send()
    drain()


def finish_kernel(
    all_cols, nnz, mine, dx_mine, kern_all, in_grad, out_grad, dx_grad, kern_grad, stage
):
    block = in_grad.shape[1]
    step = mine.shape[1]
    dx_grad[...] = dx_mine[...]
    kern_grad[...] = kern_all[: kern_grad.shape[0]]
    for src, dst in ((mine.at[0], in_grad), (mine.at[1], out_grad)):
        for h in range(block // 128):
            for c in range(all_cols):
                for k in range(nnz):
                    at = (c * nnz + k) * block + h * 128
                    stage[h, pl.ds(k * all_cols + c, step, stride=nnz * all_cols), :] = src[
                        :, at : at + 128
                    ].astype(jnp.float32)
            dst[:, h * 128 : (h + 1) * 128] = stage[h]


def split_hidden(tokens, cotangent, weight_in, weight_out, mix_kernel, block_rows):
    n_rows, depth = lax.axis_size("rows"), lax.axis_size("hid")
    _, height, width, features = tokens.shape
    rows, all_cols, nnz, block = weight_in.shape
    count = height * width
    whole = count * n_rows
    model = features * depth
    cols = all_cols // n_rows
    lanes = cols * nnz * block
    hidden = cols * block
    bf16, f32 = jnp.bfloat16, jnp.float32
    dma, sds = pltpu.SemaphoreType.DMA, jax.ShapeDtypeStruct
    params = functools.partial(pltpu.CompilerParams, vmem_limit_bytes=60 * 1024 * 1024)
    out_rows = block // (n_rows * lax.axis_size("crop"))
    panel = nnz * block
    dx_mine, mine, kern_all = pl.pallas_call(
        functools.partial(grads_kernel, depth, width, block, cols, nnz),
        name="grads_and_sums",
        out_shape=[
            sds((count, features), bf16),
            sds((2, out_rows, all_cols * panel), bf16),
            sds((16, hidden * n_rows), f32),
        ],
        in_specs=[SMEM] + [ANY] * 4 + [VMEM],
        out_specs=[VMEM] * 3,
        scratch_shapes=[
            pltpu.VMEM((model // block, whole, block), bf16),
            pltpu.VMEM((model // block, whole, block), bf16),
            pltpu.VMEM((cols * nnz + 1, block, block), bf16),
            pltpu.VMEM((cols * nnz, block, block), bf16),
            pltpu.VMEM((2, rows, nnz * all_cols, block), bf16),
            pltpu.VMEM((2, all_cols * nnz, rows, block), bf16),
            pltpu.VMEM((block // 128, rows * all_cols, 128), f32),
            dma((2, 2, depth, 4)),
            dma((2, n_rows, depth)),
            dma((2, 5)),
            dma((2, n_rows, 2)),
            dma((2, features // block + 1)),
            dma((2,)),
            pltpu.VMEM((16, hidden), f32),
            pltpu.VMEM((whole, hidden), bf16),
            pltpu.VMEM((whole, hidden), bf16),
        ]
        + [pltpu.VMEM((whole, block), f32)] * 4
        + [
            pltpu.VMEM((2, block, lanes), bf16),
            pltpu.VMEM((2, cols, block // 2, panel), bf16),
            pltpu.VMEM((whole, model), bf16),
            pltpu.VMEM((2, count, model), bf16),
            pltpu.VMEM((count, model), bf16),
            pltpu.VMEM((count, model), bf16),
            pltpu.VMEM((depth, count, features), bf16),
            pltpu.VMEM((depth - 1, count, features), bf16),
            pltpu.VMEM((16, hidden), bf16),
            pltpu.VMEM((2, n_rows, 16, hidden), bf16),
            dma((2, depth)),
            dma((2, depth)),
            dma((2, depth)),
            dma((2, depth)),
            dma((2, cols)),
            dma((2, cols)),
            dma((2, cols, 3)),
            dma((2, cols, 3)),
            dma((4,)),
            dma((2, n_rows)),
        ],
        compiler_params=params(collective_id=2, has_side_effects=True),
    )(
        block_rows.T,
        tokens.reshape(count, features),
        cotangent.reshape(count, features),
        weight_in.transpose(0, 2, 1, 3).reshape(rows, nnz * all_cols, block),
        weight_out.transpose(0, 2, 1, 3).reshape(rows, nnz * all_cols, block),
        mix_kernel,
    )
    step = 8
    part = pl.BlockSpec((count * step // out_rows, features), lambda i: (i, 0))
    flat_spec = pl.BlockSpec((2, step, all_cols * nnz * block), lambda i: (0, i, 0))
    grad_spec = pl.BlockSpec((step * nnz * all_cols, block), lambda i: (i, 0))
    in_grad, out_grad, dx_grad, kern_grad = pl.pallas_call(
        functools.partial(finish_kernel, all_cols, nnz),
        name="finish_weights",
        grid=(out_rows // step,),
        out_shape=[sds((out_rows * nnz * all_cols, block), f32)] * 2
        + [sds((count, features), bf16), sds(mix_kernel.shape, f32)],
        in_specs=[flat_spec, part, VMEM],
        out_specs=[grad_spec] * 2 + [part, VMEM],
        scratch_shapes=[pltpu.VMEM((block // 128, step * nnz * all_cols, 128), f32)],
        compiler_params=params(),
    )(mine, dx_mine, kern_all)
    in_grad, out_grad = [
        grad.reshape(out_rows, nnz, all_cols, block).transpose(0, 2, 1, 3) for grad in (in_grad, out_grad)
    ]
    return (dx_grad.reshape(tokens.shape), in_grad, out_grad, kern_grad)


def padded(shard, sides, width):
    for axis, dim in sides:
        devices, length = (lax.axis_size(axis), shard.shape[dim])
        up = [(i, (i + 1) % devices) for i in range(devices - 1)]
        down = [(j, i) for i, j in up]
        last = lax.slice_in_dim(shard, length - width, length, axis=dim)
        initial = lax.slice_in_dim(shard, 0, width, axis=dim)
        before = lax.ppermute(last, axis, up)
        after = lax.ppermute(initial, axis, down)
        shard = jnp.concatenate([before, shard, after], axis=dim)
    return shard


def gelu_pair(preact):
    inner = root_two_pi * (preact + cubic_coef * preact * preact * preact)
    tanh_val = jnp.tanh(inner)
    gelu_out = 0.5 * preact * (1.0 + tanh_val)
    slopes = 0.5 * (1.0 + tanh_val) + 0.5 * preact * (1.0 - tanh_val * tanh_val) * root_two_pi * (
        1.0 + 3.0 * cubic_coef * preact * preact
    )
    return (gelu_out, slopes)


def on_device(tokens, cotangent, weight_in, weight_out, mix_kernel, block_rows):
    in_panel, out_panel = (
        lax.all_gather(weight_in, "rows", axis=0, tiled=True),
        lax.all_gather(weight_out, "rows", axis=0, tiled=True),
    )
    tok_full, cot_full = (
        lax.all_gather(tokens, "hid", axis=3, tiled=True),
        lax.all_gather(cotangent, "hid", axis=3, tiled=True),
    )
    crop_count, height, grid_width, depth_all = tok_full.shape
    tok_count = crop_count * height * grid_width
    block_size = in_panel.shape[0]
    col_count = in_panel.shape[1]
    nnz_count = in_panel.shape[2]
    block_count = depth_all // block_size
    hidden_local = col_count * block_size
    flat_rows = block_rows.reshape(-1)
    in_select = jnp.take(
        tok_full.reshape(tok_count, block_count, block_size), flat_rows, axis=1
    ).reshape(tok_count, col_count, nnz_count, block_size)
    grad_select = jnp.take(
        cot_full.reshape(tok_count, block_count, block_size), flat_rows, axis=1
    ).reshape(tok_count, col_count, nnz_count, block_size)
    pre_act = jnp.einsum("tckb,bcke->tce", in_select, in_panel, preferred_element_type=jnp.float32)
    gelu_out, slopes = gelu_pair(pre_act)
    active = gelu_out.astype(jnp.bfloat16).reshape(crop_count, height, grid_width, hidden_local)
    act_rim = padded(active, (("rows", 1),), 1)
    mix_grad = (
        jnp.einsum("tckd,fckd->tcf", grad_select, out_panel, preferred_element_type=jnp.float32)
        .astype(jnp.bfloat16)
        .reshape(crop_count, height, grid_width, hidden_local)
    )
    grad_rim = padded(mix_grad, (("rows", 1),), 1)
    act_pad = jnp.pad(act_rim.astype(jnp.float32), ((0, 0), (0, 0), (1, 1), (0, 0)))
    grad_pad = jnp.pad(grad_rim.astype(jnp.float32), ((0, 0), (0, 0), (1, 1), (0, 0)))
    grad_grid = mix_grad.astype(jnp.float32)
    mix_sum = jnp.zeros((crop_count, height, grid_width, hidden_local), jnp.float32)
    act_grad = jnp.zeros((crop_count, height, grid_width, hidden_local), jnp.float32)
    kern_terms = []
    for row_off in range(3):
        for col_off in range(3):
            tap = mix_kernel[3 * row_off + col_off]
            shifted = act_pad[:, row_off : row_off + height, col_off : col_off + grid_width]
            mix_sum = mix_sum + tap * shifted
            act_grad = (
                act_grad
                + tap
                * grad_pad[
                    :, 2 - row_off : 2 - row_off + height, 2 - col_off : 2 - col_off + grid_width
                ]
            )
            kern_terms.append(jnp.sum(shifted * grad_grid, axis=(0, 1, 2)))
    kern_local = jnp.stack(kern_terms, axis=0) * loss_scale
    mix_out = mix_sum.astype(jnp.bfloat16).reshape(tok_count, col_count, block_size)
    pre_grad = (act_grad.reshape(tok_count, col_count, block_size) * slopes).astype(jnp.bfloat16)
    kern_total = lax.psum(kern_local.astype(jnp.bfloat16), ("crop", "rows")).astype(jnp.float32)
    back_select = jnp.einsum(
        "tce,bcke->tckb", pre_grad, in_panel, preferred_element_type=jnp.float32
    )
    one_hot = (
        block_rows[:, :, None] == jnp.arange(block_count, dtype=jnp.int32)[None, None, :]
    ).astype(jnp.float32)
    token_terms = jnp.einsum(
        "tckb,ckr->trb", back_select, one_hot, precision=lax.Precision.HIGHEST
    ).reshape(crop_count, height, grid_width, depth_all)
    grad_tokens = lax.psum_scatter(
        token_terms.astype(jnp.bfloat16), "hid", scatter_dimension=3, tiled=True
    )
    first_term = jnp.einsum(
        "tckb,tce->bcke", in_select, pre_grad, preferred_element_type=jnp.float32
    )
    second_term = jnp.einsum(
        "tcf,tckd->fckd", mix_out, grad_select, preferred_element_type=jnp.float32
    )
    share_sums = lax.psum_scatter(
        (jnp.stack([first_term, second_term], axis=1) * loss_scale).astype(jnp.bfloat16),
        ("crop", "rows"),
        scatter_dimension=0,
        tiled=True,
    ).astype(jnp.float32)
    return (grad_tokens, share_sums[:, 0], share_sums[:, 1], kern_total)


def solution(mesh):
    placed = (
        P("crop", "rows", None, "hid"),
        P("crop", "rows", None, "hid"),
        P("rows", "hid", None, None),
        P("rows", "hid", None, None),
        P(None, "hid"),
        P("hid", None),
    )
    n_crop, n_rows = mesh.shape["crop"], mesh.shape["rows"]
    n_hid = mesh.shape["hid"]

    def step(tokens, cotangent, weight_in, weight_out, mix_kernel, block_rows):
        fits = (
            n_crop == 2
            and n_rows == 4
            and tokens.shape[0] == 1
            and weight_in.shape[1] % n_rows == 0
            and tokens.shape[1] * tokens.shape[2] * n_rows * tokens.shape[3] * n_hid <= 2**22
        )
        chosen = split_hidden if fits else on_device
        return chosen(tokens, cotangent, weight_in, weight_out, mix_kernel, block_rows)

    return jax.shard_map(
        step,
        mesh=mesh,
        in_specs=placed,
        out_specs=(
            P("crop", "rows", None, "hid"),
            P(("crop", "rows"), "hid", None, None),
            P(("crop", "rows"), "hid", None, None),
            P(None, "hid"),
        ),
        check_vma=False,
    )
```

```python
import functools

import jax
import jax.numpy as jnp
from jax import lax
from jax.experimental import pallas as pl
from jax.experimental.pallas import tpu as pltpu
from jax.sharding import PartitionSpec as P

root_two_pi = 0.7978845608
cubic_coef = 0.044715
loss_scale = 0.03125

MESH_ID = pl.DeviceIdType.MESH
ANY = pl.BlockSpec(memory_space=pl.ANY)
VMEM = pl.BlockSpec(memory_space=pltpu.VMEM)
SMEM = pl.BlockSpec(memory_space=pltpu.SMEM)


def span(start, size):
    return pl.ds(pl.multiple_of(start * size, size), size)


def neighbours():
    y, r, z = lax.axis_index("crop"), lax.axis_index("rows"), lax.axis_index("hid")
    x, core = r // 2, r % 2
    same_chip = x * 2 + (1 - core)
    across = (1 - x) * 2 + core
    diagonal = (1 - x) * 2 + (1 - core)
    return y, r, z, same_chip, across, diagonal


def enter(partners):
    barrier = pltpu.get_barrier_semaphore()
    for partner in partners:
        pl.semaphore_signal(barrier, inc=1, device_id=partner, device_id_type=MESH_ID)
    pl.semaphore_wait(barrier, len(partners))


def remote(src, dst, send_sem, recv_sem, target):
    return pltpu.make_async_remote_copy(
        src_ref=src,
        dst_ref=dst,
        send_sem=send_sem,
        recv_sem=recv_sem,
        device_id=target,
        device_id_type=MESH_ID,
    )


def gather_stage(
    depth, partners, tok_h, cot_h, in_h, out_h, tok, cot, w_in, w_out,
    raw, flat, stage, tok_send, tok_recv, w_send, w_recv, own_sem, raw_sem,
):
    y, r, z, same_chip, across, diagonal = neighbours()
    tokens, features = tok_h.shape
    rows = in_h.shape[0]
    half = rows // 2
    block = tok.shape[2]
    per_part = features // block
    panels_own = w_out.shape[0]
    all_cols = stage.shape[1] // rows
    nnz = in_h.shape[1] // all_cols
    own = [
        pltpu.make_async_copy(
            src.at[:, j * block : (j + 1) * block],
            full.at[z * per_part + j, span(r, tokens), :],
            own_sem.at[a, j],
        )
        for a, (src, full) in enumerate(((cot_h, cot), (tok_h, tok)))
        for j in range(per_part)
    ]
    loads = [
        pltpu.make_async_copy(src, raw.at[a], raw_sem.at[a]) for a, src in enumerate((in_h, out_h))
    ]
    for load in own + loads:
        load.start()
    enter(partners)
    for load in own:
        load.wait()
    streams = (cot, tok)
    panels = ((flat.at[0], w_in), (flat.at[1], w_out))
    targets = ({"hid": z + 1}, {"hid": z - 1}, {"rows": across}, {"rows": same_chip})
    has_up, has_down = z + 1 < depth, z >= 1
    sends, local = [], []

    def launch(make, have=None):
        sends.append((make, have))
        if have is None:
            make().start()
        else:
            pl.when(have)(lambda: make().start())

    def piece(full, row, col):
        return full.at[span(col, per_part), span(row, tokens), :]

    def pass_on(a, which, col, kind, have=None):
        def make():
            row = (r, across)[which]
            part = piece(streams[a], row, col)
            return remote(
                part,
                part,
                tok_send.at[a, which, col, kind],
                tok_recv.at[a, row, col],
                targets[kind],
            )

        launch(make, have)

    def await_piece(a, row, col, have=None):
        def wait():
            part = piece(streams[a], row, col)
            remote(
                part, part, tok_send.at[a, 0, 0, 3], tok_recv.at[a, row, col], {"rows": same_chip}
            ).wait_recv()

        if have is None:
            wait()
        else:
            pl.when(have)(wait)

    def half_rows(full, row, h):
        at = pl.ds(pl.multiple_of(row * rows + h * half, half), half)
        return full.at[pl.ds(0, panels_own), at, :]

    def whole_rows(full, row):
        return full.at[pl.ds(0, panels_own), span(row, rows), :]

    def flatten(a):
        def turn(k, carry):
            for h in range(block // 128):
                part = raw[a, :, span(k, all_cols), h * 128 : (h + 1) * 128]
                stage[h] = part.astype(jnp.float32).reshape(rows * all_cols, 128)
            for c in range(all_cols):
                for h in range(block // 128):
                    flat[a, c * nnz + k, :, h * 128 : (h + 1) * 128] = stage[
                        h, pl.ds(c, rows, stride=all_cols), :
                    ].astype(jnp.bfloat16)
            return carry

        lax.fori_loop(0, nnz, turn, 0)

    def give_weights(a):
        src, full = panels[a]
        loads[a].wait()
        flatten(a)
        for slot, dest in ((1, across), (2, diagonal)):
            launch(
                lambda slot=slot, dest=dest: remote(
                    src.at[span(dest, panels_own), span(y, half), :],
                    half_rows(full, r, y),
                    w_send.at[a, slot],
                    w_recv.at[a, r, y],
                    {"rows": dest},
                )
            )
        launch(
            lambda: remote(
                src.at[span(same_chip, panels_own)],
                whole_rows(full, r),
                w_send.at[a, 0],
                w_recv.at[a, r, 0],
                {"rows": same_chip},
            )
        )
        keep = pltpu.make_async_copy(
            src.at[span(r, panels_own)], whole_rows(full, r), own_sem.at[a, per_part]
        )
        keep.start()
        local.append(keep)

    def mirror_weights(a):
        full = panels[a][1]
        for slot, row in ((3, across), (4, diagonal)):
            part = half_rows(full, row, y)
            remote(part, part, w_send.at[a, slot], w_recv.at[a, row, y], {"rows": row}).wait_recv()
            launch(
                lambda slot=slot, row=row, part=part: remote(
                    part, part, w_send.at[a, slot], w_recv.at[a, row, y], {"crop": 1 - y}
                )
            )

    def line_step(step):
        for below in (True, False):
            col = z - step if below else z + step
            have = col >= 0 if below else col < depth
            onward = jnp.logical_and(have, has_up if below else has_down)
            for a, which in ((0, 0), (1, 0), (1, 1)):
                await_piece(a, (r, across)[which], col, have)
                pass_on(a, which, col, 0 if below else 1, onward)
                if a == 0:
                    pass_on(a, which, col, 2, have)
                pass_on(a, which, col, 3, have)

    for a, kind in ((1, 2), (0, 0), (0, 1), (1, 0), (1, 1), (0, 2), (0, 3), (1, 3)):
        pass_on(a, 0, z, kind, (has_up, has_down, None, None)[kind])
    give_weights(0)
    await_piece(1, across, z)
    for kind in (0, 1, 3):
        pass_on(1, 1, z, kind, (has_up, has_down, None, None)[kind])
    give_weights(1)
    for step in range(1, depth):
        line_step(step)
        if step <= 2:
            mirror_weights(step - 1)
    for a in range(depth - 1, 2):
        mirror_weights(a)
    def await_rows(a):
        for row in (same_chip, diagonal):
            for step in range(depth):
                await_piece(a, row, (z + step) % depth)

    def await_weights(a):
        full = panels[a][1]
        part = whole_rows(full, same_chip)
        remote(
            part, part, w_send.at[a, 0], w_recv.at[a, same_chip, 0], {"rows": same_chip}
        ).wait_recv()
        for row in (across, diagonal):
            part = half_rows(full, row, 1 - y)
            remote(
                part, part, w_send.at[a, 0], w_recv.at[a, row, 1 - y], {"crop": 1 - y}
            ).wait_recv()
        local[a].wait()

    await_rows(1)
    await_weights(0)

    def await_rest():
        for step in range(depth):
            col = (z + step) % depth
            await_piece(0, across, col)
            pass_on(0, 1, col, 3)
        await_weights(1)
        await_rows(0)

    def drain():
        for make, have in sends:
            if have is None:
                make().wait_send()
            else:
                pl.when(have)(lambda make=make: make().wait_send())

    return await_rest, drain


def nt(a, b):
    return lax.dot_general(a, b, (((1,), (1,)), ((), ())), preferred_element_type=jnp.float32)


def tn(a, b):
    return lax.dot_general(a, b, (((0,), (0,)), ((), ())), preferred_element_type=jnp.float32)


def column_math(width, block, cols, nnz, ids, tok, cot, w_in, w_out, taps, kern, mixed, pgrad, pre_s, act_s, slope_s, mg_s, gw):
    count = tok.shape[1]
    me = lax.axis_index("rows")
    place = lax.broadcasted_iota(jnp.int32, (count, block), 0) % width

    def spread(value):
        before = jnp.where(place == 0, 0.0, pltpu.roll(value, 1, 0))
        after = jnp.where(place == width - 1, 0.0, pltpu.roll(value, count - 1, 0))
        return (before, value, after)

    def stack_rows(up, mid, down):
        edge = jnp.zeros((width, block), jnp.float32)
        return (
            mid
            + jnp.concatenate([edge, up[:-width]], axis=0)
            + jnp.concatenate([down[width:], edge], axis=0)
        )

    def feats(c, k):
        return ids[k, me * cols + c]

    def panel(c, k):
        return span(c * nnz + k, block)

    def tap(c, a, b):
        row = 3 * (a + 1) + (b + 1)
        return taps[row : row + 1, span(me * cols + c, block)]

    def forward(c):
        hidden = span(c, block)
        pre = jnp.dot(tok[feats(c, 0)], w_in[c * nnz], preferred_element_type=jnp.float32)
        for k in range(1, nnz):
            pre += jnp.dot(tok[feats(c, k)], w_in[c * nnz + k], preferred_element_type=jnp.float32)
        pre_s[...] = pre
        p = pre_s[...]
        t = jnp.tanh(root_two_pi * (p + cubic_coef * p * p * p))
        act_s[...] = (0.5 * p * (1.0 + t)).astype(jnp.bfloat16).astype(jnp.float32)
        slope_s[...] = 0.5 * (1.0 + t) + 0.5 * p * (1.0 - t * t) * root_two_pi * (
            1.0 + 3.0 * cubic_coef * p * p
        )
        acts = spread(act_s[...])
        mixed[:, hidden] = stack_rows(
            *[sum(tap(c, a, b) * acts[b + 1] for b in (-1, 0, 1)) for a in (-1, 0, 1)]
        ).astype(jnp.bfloat16)

    def backward(c):
        hidden = span(c, block)
        mg = nt(cot[feats(c, 0)], w_out[c * nnz])
        for k in range(1, nnz):
            mg += nt(cot[feats(c, k)], w_out[c * nnz + k])
        mg_s[...] = mg.astype(jnp.bfloat16).astype(jnp.float32)
        acts = spread(act_s[...])
        grads = mg_s[...]
        for b in (-1, 0, 1):
            seen = acts[b + 1]
            sums = (
                jnp.sum(seen[:-width] * grads[width:], axis=0, keepdims=True),
                jnp.sum(seen * grads, axis=0, keepdims=True),
                jnp.sum(seen[width:] * grads[:-width], axis=0, keepdims=True),
            )
            for a in (-1, 0, 1):
                row = 3 * (a + 1) + (b + 1)
                kern[row : row + 1, hidden] = sums[a + 1] * loss_scale
        backs = spread(mg_s[...])
        gathered = stack_rows(
            *[sum(tap(c, a, b) * backs[1 - b] for b in (-1, 0, 1)) for a in (1, 0, -1)]
        )
        pgrad[:, hidden] = (gathered * slope_s[...]).astype(jnp.bfloat16)

    def grad_out(c):
        left = mixed[:, span(c, block)]
        for k in range(nnz):
            gw[1, :, panel(c, k)] = (tn(left, cot[feats(c, k)]) * loss_scale).astype(jnp.bfloat16)

    def grad_in(c):
        right = pgrad[:, span(c, block)]
        for k in range(nnz):
            gw[0, :, panel(c, k)] = (tn(tok[feats(c, k)], right) * loss_scale).astype(jnp.bfloat16)

    limit = tok.shape[0] ** 2

    def token_grad(g):
        total = jnp.zeros((count, block), jnp.float32)
        for c in range(cols):
            at = cols * nnz
            for k in range(nnz):
                apart = ids[k, me * cols + c] - g
                same = 1 - lax.div(apart * apart + (limit - 1), jnp.int32(limit))
                at += same * (c * nnz + k - at)
            total += nt(pgrad[:, span(c, block)], w_in[at])
        return total.astype(jnp.bfloat16)

    return forward, backward, grad_out, grad_in, token_grad


def grads_kernel(
    depth, width, block, cols, nnz, ids, tok_h, cot_h, in_h, out_h, taps,
    dx_mine, mine, kern_all,
    tok, cot, w_in, w_out, raw, flat, stage, tok_send, tok_recv, w_send, w_recv, own_sem, raw_sem, kern, mixed, pgrad, pre_s, act_s, slope_s, mg_s, gw, gw_part,
    dx, dx_near, dx_half, dx_far, dx_sum, dx_last, kern_own, kern_part,
    dx_send, dx_recv, far_send, far_recv, gw_send, gw_recv, part_send, part_recv,
    kern_send, kern_recv,
):
    y, r, z, same_chip, across, diagonal = neighbours()
    group = [same_chip, across, diagonal]
    tokens, features = dx_mine.shape
    rows = mine.shape[1]
    half = block // 2
    lanes = nnz * block
    per_part = features // block
    w_in[cols * nnz] = jnp.zeros((block, block), jnp.bfloat16)
    kern[...] = jnp.zeros_like(kern)
    await_rest, drain = gather_stage(
        depth,
        [{"rows": row} for row in group]
        + [{"crop": 1 - y}]
        + [{"hid": (z + step) % depth} for step in range(1, depth)],
        tok_h, cot_h, in_h, out_h, tok, cot, w_in, w_out,
        raw, flat, stage, tok_send, tok_recv, w_send, w_recv, own_sem, raw_sem,
    )
    started = []

    def go(*args):
        copy = remote(*args)
        copy.start()
        started.append(copy)

    def arrived(ref, send_sem, recv_sem, target):
        remote(ref, ref, send_sem, recv_sem, target).wait_recv()

    forward, backward, grad_out, grad_in, token_grad = column_math(
        width, block, cols, nnz, ids, tok, cot, w_in, w_out, taps, kern, mixed, pgrad,
        pre_s, act_s, slope_s, mg_s, gw,
    )

    def give_copy(a, c, far):
        side = (r // 2, 1 - r // 2)[far]
        return remote(
            gw.at[a, span((1 - y) * 2 + side, half // 2), span(c, lanes)],
            gw_part.at[a, c, span(side, half // 2), :],
            gw_send.at[a, c, far],
            gw_recv.at[a, c, far],
            {"crop": 1 - y},
        )

    def give(a, c):
        for far in (1, 0):
            give_copy(a, c, far).start()

    def settle_side(a, c, far):
        side = (r // 2, 1 - r // 2)[far]
        at = span(side, half // 2)
        give_copy(a, c, far).wait_recv()
        gw_part[a, c, at, :] = (
            gw[a, span(y * 2 + side, half // 2), span(c, lanes)].astype(jnp.float32)
            + gw_part[a, c, at, :].astype(jnp.float32)
        ).astype(jnp.bfloat16)
        at = span(r * cols + c, lanes)
        for slot, row in ((0, across), (1, diagonal)) if far else ((2, same_chip),):
            go(
                gw_part.at[a, c, span(row, rows), :],
                mine.at[a, :, at],
                part_send.at[a, c, slot],
                part_recv.at[a, c, slot],
                {"rows": row},
            )
        if not far:
            mine[a, :, at] = gw_part[a, c, span(r, rows), :]

    def settle(a, c):
        settle_side(a, c, 1)
        settle_side(a, c, 0)

    def part_of(i):
        return (z + 1 + i) % depth

    def lanes_of(i):
        return span(part_of(i), features)

    forward(0)
    await_rest()
    grad_out(0)
    give(1, 0)
    backward(0)
    grad_in(0)
    give(0, 0)

    def one_column(c, carry):
        forward(c)
        grad_out(c)
        backward(c)
        grad_in(c)
        return carry

    near = ((0, diagonal), (1, same_chip))

    def near_copy(slot, row, i):
        at = lanes_of(i)
        return remote(
            dx.at[span(row, tokens), at],
            dx_near.at[slot, :, at],
            dx_send.at[slot, i],
            dx_recv.at[slot, i],
            {"rows": same_chip},
        )

    def pass_half(i):
        near_copy(0, diagonal, i).wait_recv()
        at = lanes_of(i)
        dx_half[:, at] = (
            dx[span(across, tokens), at].astype(jnp.float32) + dx_near[0, :, at].astype(jnp.float32)
        ).astype(jnp.bfloat16)
        go(dx_half.at[:, at], dx_far.at[:, at], far_send.at[0, i], far_recv.at[0, i], {"rows": across})

    def inner_column(c, carry):
        one_column(c, carry)

        @pl.when(c == cols - 1)
        def _():
            kern_own[...] = kern[...].astype(jnp.bfloat16)
            kern_copy.start()

        for a in (1, 0):
            give(a, c)
        return carry

    kern_copy = remote(
        kern_own, kern_part.at[1, 0], kern_send.at[0], kern_recv.at[1, 0], {"crop": 1 - y}
    )
    lax.fori_loop(1, 2, inner_column, 0)
    settle(1, 0)
    lax.fori_loop(2, cols, inner_column, 0)
    settle(0, 0)
    for i in range(depth):

        def one_block(j, carry):
            g = part_of(i) * per_part + j
            dx[:, span(g, block)] = token_grad(g)
            return carry

        lax.fori_loop(0, per_part, one_block, 0)
        for slot, row in near:
            near_copy(slot, row, i).start()
        if i > 0:
            pass_half(i - 1)
    pass_half(depth - 1)

    def pass_sum(i):
        at = lanes_of(i)
        near_copy(1, same_chip, i).wait_recv()
        arrived(dx_far.at[:, at], far_send.at[0, i], far_recv.at[0, i], {"rows": across})
        dx_sum[i] = (
            dx[span(r, tokens), at].astype(jnp.float32)
            + dx_near[1, :, at].astype(jnp.float32)
            + dx_far[:, at].astype(jnp.float32)
        ).astype(jnp.bfloat16)
        if i < depth - 1:
            go(
                dx_sum.at[i],
                dx_last.at[i],
                far_send.at[1, i],
                far_recv.at[1, i],
                {"hid": part_of(i)},
            )

    waits = [(a, c) for c in range(1, cols) for a in (1, 0)]
    sums = list(range(depth))
    while len(waits) > 2:
        settle(*waits.pop(0))
        if sums:
            pass_sum(sums.pop(0))
    while sums:
        pass_sum(sums.pop(0))
    kern_copy.wait_recv()
    kern_part[0, r] = (
        kern_own[...].astype(jnp.float32) + kern_part[1, 0].astype(jnp.float32)
    ).astype(jnp.bfloat16)
    for slot, row in enumerate(group):
        go(
            kern_part.at[0, r],
            kern_part.at[0, r],
            kern_send.at[slot + 1],
            kern_recv.at[0, r],
            {"rows": row},
        )
    settle(*waits.pop(0))
    total = dx_sum[depth - 1].astype(jnp.float32)
    for step in range(depth - 1):
        arrived(dx_last.at[step], far_send.at[1, step], far_recv.at[1, step], {"hid": part_of(step)})
        total += dx_last[step].astype(jnp.float32)
    dx_mine[...] = total.astype(jnp.bfloat16)
    for row in group:
        arrived(kern_part.at[0, row], kern_send.at[0], kern_recv.at[0, row], {"rows": same_chip})
    wide = kern.shape[1]
    for row in range(4):
        kern_all[:, row * wide : (row + 1) * wide] = kern_part[0, row].astype(jnp.float32)
    for a, c in waits:
        settle(a, c)
    for a in (1, 0):
        for c in range(cols):
            for slot, row in enumerate((across, diagonal, same_chip)):
                arrived(
                    mine.at[a, :, span(row * cols + c, lanes)],
                    part_send.at[a, c, slot],
                    part_recv.at[a, c, slot],
                    {"rows": row},
                )
    for i in range(depth):
        for slot, row in near:
            near_copy(slot, row, i).wait_send()
    for copy in started:
        copy.wait_send()
    kern_copy.wait_send()
    for a in range(2):
        for c in range(cols):
            for far in range(2):
                give_copy(a, c, far).wait_send()
    drain()


def finish_kernel(
    all_cols, nnz, mine, dx_mine, kern_all, in_grad, out_grad, dx_grad, kern_grad, stage
):
    block = in_grad.shape[1]
    step = mine.shape[1]
    dx_grad[...] = dx_mine[...]
    kern_grad[...] = kern_all[: kern_grad.shape[0]]
    for src, dst in ((mine.at[0], in_grad), (mine.at[1], out_grad)):
        for h in range(block // 128):
            for c in range(all_cols):
                for k in range(nnz):
                    at = (c * nnz + k) * block + h * 128
                    stage[h, pl.ds(k * all_cols + c, step, stride=nnz * all_cols), :] = src[
                        :, at : at + 128
                    ].astype(jnp.float32)
            dst[:, h * 128 : (h + 1) * 128] = stage[h]


def split_hidden(tokens, cotangent, weight_in, weight_out, mix_kernel, block_rows):
    n_rows, depth = lax.axis_size("rows"), lax.axis_size("hid")
    _, height, width, features = tokens.shape
    rows, all_cols, nnz, block = weight_in.shape
    count = height * width
    whole = count * n_rows
    model = features * depth
    cols = all_cols // n_rows
    lanes = cols * nnz * block
    hidden = cols * block
    bf16, f32 = jnp.bfloat16, jnp.float32
    dma, sds = pltpu.SemaphoreType.DMA, jax.ShapeDtypeStruct
    params = functools.partial(pltpu.CompilerParams, vmem_limit_bytes=60 * 1024 * 1024)
    out_rows = block // (n_rows * lax.axis_size("crop"))
    panel = nnz * block
    dx_mine, mine, kern_all = pl.pallas_call(
        functools.partial(grads_kernel, depth, width, block, cols, nnz),
        name="grads_and_sums",
        out_shape=[
            sds((count, features), bf16),
            sds((2, out_rows, all_cols * panel), bf16),
            sds((16, hidden * n_rows), f32),
        ],
        in_specs=[SMEM] + [ANY] * 4 + [VMEM],
        out_specs=[VMEM] * 3,
        scratch_shapes=[
            pltpu.VMEM((model // block, whole, block), bf16),
            pltpu.VMEM((model // block, whole, block), bf16),
            pltpu.VMEM((cols * nnz + 1, block, block), bf16),
            pltpu.VMEM((cols * nnz, block, block), bf16),
            pltpu.VMEM((2, rows, nnz * all_cols, block), bf16),
            pltpu.VMEM((2, all_cols * nnz, rows, block), bf16),
            pltpu.VMEM((block // 128, rows * all_cols, 128), f32),
            dma((2, 2, depth, 4)),
            dma((2, n_rows, depth)),
            dma((2, 5)),
            dma((2, n_rows, 2)),
            dma((2, features // block + 1)),
            dma((2,)),
            pltpu.VMEM((16, hidden), f32),
            pltpu.VMEM((whole, hidden), bf16),
            pltpu.VMEM((whole, hidden), bf16),
        ]
        + [pltpu.VMEM((whole, block), f32)] * 4
        + [
            pltpu.VMEM((2, block, lanes), bf16),
            pltpu.VMEM((2, cols, block // 2, panel), bf16),
            pltpu.VMEM((whole, model), bf16),
            pltpu.VMEM((2, count, model), bf16),
            pltpu.VMEM((count, model), bf16),
            pltpu.VMEM((count, model), bf16),
            pltpu.VMEM((depth, count, features), bf16),
            pltpu.VMEM((depth - 1, count, features), bf16),
            pltpu.VMEM((16, hidden), bf16),
            pltpu.VMEM((2, n_rows, 16, hidden), bf16),
            dma((2, depth)),
            dma((2, depth)),
            dma((2, depth)),
            dma((2, depth)),
            dma((2, cols, 2)),
            dma((2, cols, 2)),
            dma((2, cols, 3)),
            dma((2, cols, 3)),
            dma((4,)),
            dma((2, n_rows)),
        ],
        compiler_params=params(collective_id=2, has_side_effects=True),
    )(
        block_rows.T,
        tokens.reshape(count, features),
        cotangent.reshape(count, features),
        weight_in.transpose(0, 2, 1, 3).reshape(rows, nnz * all_cols, block),
        weight_out.transpose(0, 2, 1, 3).reshape(rows, nnz * all_cols, block),
        mix_kernel,
    )
    step = 8
    part = pl.BlockSpec((count * step // out_rows, features), lambda i: (i, 0))
    flat_spec = pl.BlockSpec((2, step, all_cols * nnz * block), lambda i: (0, i, 0))
    grad_spec = pl.BlockSpec((step * nnz * all_cols, block), lambda i: (i, 0))
    in_grad, out_grad, dx_grad, kern_grad = pl.pallas_call(
        functools.partial(finish_kernel, all_cols, nnz),
        name="finish_weights",
        grid=(out_rows // step,),
        out_shape=[sds((out_rows * nnz * all_cols, block), f32)] * 2
        + [sds((count, features), bf16), sds(mix_kernel.shape, f32)],
        in_specs=[flat_spec, part, VMEM],
        out_specs=[grad_spec] * 2 + [part, VMEM],
        scratch_shapes=[pltpu.VMEM((block // 128, step * nnz * all_cols, 128), f32)],
        compiler_params=params(),
    )(mine, dx_mine, kern_all)
    in_grad, out_grad = [
        grad.reshape(out_rows, nnz, all_cols, block).transpose(0, 2, 1, 3) for grad in (in_grad, out_grad)
    ]
    return (dx_grad.reshape(tokens.shape), in_grad, out_grad, kern_grad)


def padded(shard, sides, width):
    for axis, dim in sides:
        devices, length = (lax.axis_size(axis), shard.shape[dim])
        up = [(i, (i + 1) % devices) for i in range(devices - 1)]
        down = [(j, i) for i, j in up]
        last = lax.slice_in_dim(shard, length - width, length, axis=dim)
        initial = lax.slice_in_dim(shard, 0, width, axis=dim)
        before = lax.ppermute(last, axis, up)
        after = lax.ppermute(initial, axis, down)
        shard = jnp.concatenate([before, shard, after], axis=dim)
    return shard


def gelu_pair(preact):
    inner = root_two_pi * (preact + cubic_coef * preact * preact * preact)
    tanh_val = jnp.tanh(inner)
    gelu_out = 0.5 * preact * (1.0 + tanh_val)
    slopes = 0.5 * (1.0 + tanh_val) + 0.5 * preact * (1.0 - tanh_val * tanh_val) * root_two_pi * (
        1.0 + 3.0 * cubic_coef * preact * preact
    )
    return (gelu_out, slopes)


def on_device(tokens, cotangent, weight_in, weight_out, mix_kernel, block_rows):
    in_panel, out_panel = (
        lax.all_gather(weight_in, "rows", axis=0, tiled=True),
        lax.all_gather(weight_out, "rows", axis=0, tiled=True),
    )
    tok_full, cot_full = (
        lax.all_gather(tokens, "hid", axis=3, tiled=True),
        lax.all_gather(cotangent, "hid", axis=3, tiled=True),
    )
    crop_count, height, grid_width, depth_all = tok_full.shape
    tok_count = crop_count * height * grid_width
    block_size = in_panel.shape[0]
    col_count = in_panel.shape[1]
    nnz_count = in_panel.shape[2]
    block_count = depth_all // block_size
    hidden_local = col_count * block_size
    flat_rows = block_rows.reshape(-1)
    in_select = jnp.take(
        tok_full.reshape(tok_count, block_count, block_size), flat_rows, axis=1
    ).reshape(tok_count, col_count, nnz_count, block_size)
    grad_select = jnp.take(
        cot_full.reshape(tok_count, block_count, block_size), flat_rows, axis=1
    ).reshape(tok_count, col_count, nnz_count, block_size)
    pre_act = jnp.einsum("tckb,bcke->tce", in_select, in_panel, preferred_element_type=jnp.float32)
    gelu_out, slopes = gelu_pair(pre_act)
    active = gelu_out.astype(jnp.bfloat16).reshape(crop_count, height, grid_width, hidden_local)
    act_rim = padded(active, (("rows", 1),), 1)
    mix_grad = (
        jnp.einsum("tckd,fckd->tcf", grad_select, out_panel, preferred_element_type=jnp.float32)
        .astype(jnp.bfloat16)
        .reshape(crop_count, height, grid_width, hidden_local)
    )
    grad_rim = padded(mix_grad, (("rows", 1),), 1)
    act_pad = jnp.pad(act_rim.astype(jnp.float32), ((0, 0), (0, 0), (1, 1), (0, 0)))
    grad_pad = jnp.pad(grad_rim.astype(jnp.float32), ((0, 0), (0, 0), (1, 1), (0, 0)))
    grad_grid = mix_grad.astype(jnp.float32)
    mix_sum = jnp.zeros((crop_count, height, grid_width, hidden_local), jnp.float32)
    act_grad = jnp.zeros((crop_count, height, grid_width, hidden_local), jnp.float32)
    kern_terms = []
    for row_off in range(3):
        for col_off in range(3):
            tap = mix_kernel[3 * row_off + col_off]
            shifted = act_pad[:, row_off : row_off + height, col_off : col_off + grid_width]
            mix_sum = mix_sum + tap * shifted
            act_grad = (
                act_grad
                + tap
                * grad_pad[
                    :, 2 - row_off : 2 - row_off + height, 2 - col_off : 2 - col_off + grid_width
                ]
            )
            kern_terms.append(jnp.sum(shifted * grad_grid, axis=(0, 1, 2)))
    kern_local = jnp.stack(kern_terms, axis=0) * loss_scale
    mix_out = mix_sum.astype(jnp.bfloat16).reshape(tok_count, col_count, block_size)
    pre_grad = (act_grad.reshape(tok_count, col_count, block_size) * slopes).astype(jnp.bfloat16)
    kern_total = lax.psum(kern_local.astype(jnp.bfloat16), ("crop", "rows")).astype(jnp.float32)
    back_select = jnp.einsum(
        "tce,bcke->tckb", pre_grad, in_panel, preferred_element_type=jnp.float32
    )
    one_hot = (
        block_rows[:, :, None] == jnp.arange(block_count, dtype=jnp.int32)[None, None, :]
    ).astype(jnp.float32)
    token_terms = jnp.einsum(
        "tckb,ckr->trb", back_select, one_hot, precision=lax.Precision.HIGHEST
    ).reshape(crop_count, height, grid_width, depth_all)
    grad_tokens = lax.psum_scatter(
        token_terms.astype(jnp.bfloat16), "hid", scatter_dimension=3, tiled=True
    )
    first_term = jnp.einsum(
        "tckb,tce->bcke", in_select, pre_grad, preferred_element_type=jnp.float32
    )
    second_term = jnp.einsum(
        "tcf,tckd->fckd", mix_out, grad_select, preferred_element_type=jnp.float32
    )
    share_sums = lax.psum_scatter(
        (jnp.stack([first_term, second_term], axis=1) * loss_scale).astype(jnp.bfloat16),
        ("crop", "rows"),
        scatter_dimension=0,
        tiled=True,
    ).astype(jnp.float32)
    return (grad_tokens, share_sums[:, 0], share_sums[:, 1], kern_total)


def solution(mesh):
    placed = (
        P("crop", "rows", None, "hid"),
        P("crop", "rows", None, "hid"),
        P("rows", "hid", None, None),
        P("rows", "hid", None, None),
        P(None, "hid"),
        P("hid", None),
    )
    n_crop, n_rows = mesh.shape["crop"], mesh.shape["rows"]
    n_hid = mesh.shape["hid"]

    def step(tokens, cotangent, weight_in, weight_out, mix_kernel, block_rows):
        fits = (
            n_crop == 2
            and n_rows == 4
            and tokens.shape[0] == 1
            and weight_in.shape[1] % n_rows == 0
            and weight_in.shape[1] >= 2 * n_rows
            and tokens.shape[1] * tokens.shape[2] * n_rows * tokens.shape[3] * n_hid <= 2**22
        )
        chosen = split_hidden if fits else on_device
        return chosen(tokens, cotangent, weight_in, weight_out, mix_kernel, block_rows)

    return jax.shard_map(
        step,
        mesh=mesh,
        in_specs=placed,
        out_specs=(
            P("crop", "rows", None, "hid"),
            P(("crop", "rows"), "hid", None, None),
            P(("crop", "rows"), "hid", None, None),
            P(None, "hid"),
        ),
        check_vma=False,
    )
```

```python
import functools

import jax
import jax.numpy as jnp
from jax import lax
from jax.experimental import pallas as pl
from jax.experimental.pallas import tpu as pltpu
from jax.sharding import PartitionSpec as P

root_two_pi = 0.7978845608
cubic_coef = 0.044715
loss_scale = 0.03125

MESH_ID = pl.DeviceIdType.MESH
ANY = pl.BlockSpec(memory_space=pl.ANY)
VMEM = pl.BlockSpec(memory_space=pltpu.VMEM)
SMEM = pl.BlockSpec(memory_space=pltpu.SMEM)


def span(start, size):
    return pl.ds(pl.multiple_of(start * size, size), size)


def neighbours():
    y, r, z = lax.axis_index("crop"), lax.axis_index("rows"), lax.axis_index("hid")
    x, core = r // 2, r % 2
    same_chip = x * 2 + (1 - core)
    across = (1 - x) * 2 + core
    diagonal = (1 - x) * 2 + (1 - core)
    return y, r, z, same_chip, across, diagonal


def enter(partners):
    barrier = pltpu.get_barrier_semaphore()
    for partner in partners:
        pl.semaphore_signal(barrier, inc=1, device_id=partner, device_id_type=MESH_ID)
    pl.semaphore_wait(barrier, len(partners))


def remote(src, dst, send_sem, recv_sem, target):
    return pltpu.make_async_remote_copy(
        src_ref=src,
        dst_ref=dst,
        send_sem=send_sem,
        recv_sem=recv_sem,
        device_id=target,
        device_id_type=MESH_ID,
    )


def gather_stage(
    depth, partners, tok_h, cot_h, in_h, out_h, tok, cot, w_in, w_out,
    raw, flat, stage, tok_send, tok_recv, w_send, w_recv, own_sem, raw_sem,
):
    y, r, z, same_chip, across, diagonal = neighbours()
    tokens, features = tok_h.shape
    rows = in_h.shape[0]
    half = rows // 2
    block = tok.shape[2]
    per_part = features // block
    panels_own = w_out.shape[0]
    all_cols = stage.shape[1] // rows
    nnz = in_h.shape[1] // all_cols
    own = [
        pltpu.make_async_copy(
            src.at[:, j * block : (j + 1) * block],
            full.at[z * per_part + j, span(r, tokens), :],
            own_sem.at[a, j],
        )
        for a, (src, full) in enumerate(((cot_h, cot), (tok_h, tok)))
        for j in range(per_part)
    ]
    loads = [
        pltpu.make_async_copy(src, raw.at[a], raw_sem.at[a]) for a, src in enumerate((in_h, out_h))
    ]
    for load in own + loads:
        load.start()
    enter(partners)
    for load in own:
        load.wait()
    streams = (cot, tok)
    panels = ((flat.at[0], w_in), (flat.at[1], w_out))
    targets = ({"hid": z + 1}, {"hid": z - 1}, {"rows": across}, {"rows": same_chip})
    has_up, has_down = z + 1 < depth, z >= 1
    sends, local = [], []

    def launch(make, have=None):
        sends.append((make, have))
        if have is None:
            make().start()
        else:
            pl.when(have)(lambda: make().start())

    def piece(full, row, col):
        return full.at[span(col, per_part), span(row, tokens), :]

    def pass_on(a, which, col, kind, have=None):
        def make():
            row = (r, across)[which]
            part = piece(streams[a], row, col)
            return remote(
                part,
                part,
                tok_send.at[a, which, col, kind],
                tok_recv.at[a, row, col],
                targets[kind],
            )

        launch(make, have)

    def await_piece(a, row, col, have=None):
        def wait():
            part = piece(streams[a], row, col)
            remote(
                part, part, tok_send.at[a, 0, 0, 3], tok_recv.at[a, row, col], {"rows": same_chip}
            ).wait_recv()

        if have is None:
            wait()
        else:
            pl.when(have)(wait)

    def half_rows(full, row, h):
        at = pl.ds(pl.multiple_of(row * rows + h * half, half), half)
        return full.at[pl.ds(0, panels_own), at, :]

    def whole_rows(full, row):
        return full.at[pl.ds(0, panels_own), span(row, rows), :]

    def flatten(a):
        def turn(k, carry):
            for h in range(block // 128):
                part = raw[a, :, span(k, all_cols), h * 128 : (h + 1) * 128]
                stage[h] = part.astype(jnp.float32).reshape(rows * all_cols, 128)
            for c in range(all_cols):
                for h in range(block // 128):
                    flat[a, c * nnz + k, :, h * 128 : (h + 1) * 128] = stage[
                        h, pl.ds(c, rows, stride=all_cols), :
                    ].astype(jnp.bfloat16)
            return carry

        lax.fori_loop(0, nnz, turn, 0)

    def give_weights(a):
        src, full = panels[a]
        loads[a].wait()
        flatten(a)
        for slot, dest in ((1, across), (2, diagonal)):
            launch(
                lambda slot=slot, dest=dest: remote(
                    src.at[span(dest, panels_own), span(y, half), :],
                    half_rows(full, r, y),
                    w_send.at[a, slot],
                    w_recv.at[a, r, y],
                    {"rows": dest},
                )
            )
        launch(
            lambda: remote(
                src.at[span(same_chip, panels_own)],
                whole_rows(full, r),
                w_send.at[a, 0],
                w_recv.at[a, r, 0],
                {"rows": same_chip},
            )
        )
        keep = pltpu.make_async_copy(
            src.at[span(r, panels_own)], whole_rows(full, r), own_sem.at[a, per_part]
        )
        keep.start()
        local.append(keep)

    def mirror_weights(a):
        full = panels[a][1]
        for slot, row in ((3, across), (4, diagonal)):
            part = half_rows(full, row, y)
            remote(part, part, w_send.at[a, slot], w_recv.at[a, row, y], {"rows": row}).wait_recv()
            launch(
                lambda slot=slot, row=row, part=part: remote(
                    part, part, w_send.at[a, slot], w_recv.at[a, row, y], {"crop": 1 - y}
                )
            )

    def line_step(step):
        for below in (True, False):
            col = z - step if below else z + step
            have = col >= 0 if below else col < depth
            onward = jnp.logical_and(have, has_up if below else has_down)
            for a, which in ((0, 0), (1, 0), (1, 1)):
                await_piece(a, (r, across)[which], col, have)
                pass_on(a, which, col, 0 if below else 1, onward)
                if a == 0:
                    pass_on(a, which, col, 2, have)
                pass_on(a, which, col, 3, have)

    for a, kind in ((1, 2), (0, 0), (0, 1), (1, 0), (1, 1), (0, 2), (0, 3), (1, 3)):
        pass_on(a, 0, z, kind, (has_up, has_down, None, None)[kind])
    give_weights(0)
    await_piece(1, across, z)
    for kind in (0, 1, 3):
        pass_on(1, 1, z, kind, (has_up, has_down, None, None)[kind])
    give_weights(1)
    for step in range(1, depth):
        line_step(step)
        if step <= 2:
            mirror_weights(step - 1)
    for a in range(depth - 1, 2):
        mirror_weights(a)
    def await_rows(a):
        for row in (same_chip, diagonal):
            for step in range(depth):
                await_piece(a, row, (z + step) % depth)

    def await_weights(a):
        full = panels[a][1]
        part = whole_rows(full, same_chip)
        remote(
            part, part, w_send.at[a, 0], w_recv.at[a, same_chip, 0], {"rows": same_chip}
        ).wait_recv()
        for row in (across, diagonal):
            part = half_rows(full, row, 1 - y)
            remote(
                part, part, w_send.at[a, 0], w_recv.at[a, row, 1 - y], {"crop": 1 - y}
            ).wait_recv()
        local[a].wait()

    await_rows(1)
    await_weights(0)

    def await_rest():
        for step in range(depth):
            col = (z + step) % depth
            await_piece(0, across, col)
            pass_on(0, 1, col, 3)
        await_weights(1)
        await_rows(0)

    def drain():
        for make, have in sends:
            if have is None:
                make().wait_send()
            else:
                pl.when(have)(lambda make=make: make().wait_send())

    return await_rest, drain


def nt(a, b):
    return lax.dot_general(a, b, (((1,), (1,)), ((), ())), preferred_element_type=jnp.float32)


def tn(a, b):
    return lax.dot_general(a, b, (((0,), (0,)), ((), ())), preferred_element_type=jnp.float32)


def column_math(width, block, cols, nnz, ids, tok, cot, w_in, w_out, taps, kern, mixed, pgrad, pre_s, act_s, slope_s, mg_s, gw):
    count = tok.shape[1]
    me = lax.axis_index("rows")
    place = lax.broadcasted_iota(jnp.int32, (count, block), 0) % width

    def spread(value):
        before = jnp.where(place == 0, 0.0, pltpu.roll(value, 1, 0))
        after = jnp.where(place == width - 1, 0.0, pltpu.roll(value, count - 1, 0))
        return (before, value, after)

    def stack_rows(up, mid, down):
        edge = jnp.zeros((width, block), jnp.float32)
        return (
            mid
            + jnp.concatenate([edge, up[:-width]], axis=0)
            + jnp.concatenate([down[width:], edge], axis=0)
        )

    def feats(c, k):
        return ids[k, me * cols + c]

    def panel(c, k):
        return span(c * nnz + k, block)

    def tap(c, a, b):
        row = 3 * (a + 1) + (b + 1)
        return taps[row : row + 1, span(me * cols + c, block)]

    def forward(c):
        hidden = span(c, block)
        pre = jnp.dot(tok[feats(c, 0)], w_in[c * nnz], preferred_element_type=jnp.float32)
        for k in range(1, nnz):
            pre += jnp.dot(tok[feats(c, k)], w_in[c * nnz + k], preferred_element_type=jnp.float32)
        pre_s[...] = pre
        p = pre_s[...]
        t = jnp.tanh(root_two_pi * (p + cubic_coef * p * p * p))
        act_s[...] = (0.5 * p * (1.0 + t)).astype(jnp.bfloat16).astype(jnp.float32)
        slope_s[...] = 0.5 * (1.0 + t) + 0.5 * p * (1.0 - t * t) * root_two_pi * (
            1.0 + 3.0 * cubic_coef * p * p
        )
        acts = spread(act_s[...])
        mixed[:, hidden] = stack_rows(
            *[sum(tap(c, a, b) * acts[b + 1] for b in (-1, 0, 1)) for a in (-1, 0, 1)]
        ).astype(jnp.bfloat16)

    def backward(c):
        hidden = span(c, block)
        mg = nt(cot[feats(c, 0)], w_out[c * nnz])
        for k in range(1, nnz):
            mg += nt(cot[feats(c, k)], w_out[c * nnz + k])
        mg_s[...] = mg.astype(jnp.bfloat16).astype(jnp.float32)
        acts = spread(act_s[...])
        grads = mg_s[...]
        for b in (-1, 0, 1):
            seen = acts[b + 1]
            sums = (
                jnp.sum(seen[:-width] * grads[width:], axis=0, keepdims=True),
                jnp.sum(seen * grads, axis=0, keepdims=True),
                jnp.sum(seen[width:] * grads[:-width], axis=0, keepdims=True),
            )
            for a in (-1, 0, 1):
                row = 3 * (a + 1) + (b + 1)
                kern[row : row + 1, hidden] = sums[a + 1] * loss_scale
        backs = spread(mg_s[...])
        gathered = stack_rows(
            *[sum(tap(c, a, b) * backs[1 - b] for b in (-1, 0, 1)) for a in (1, 0, -1)]
        )
        pgrad[:, hidden] = (gathered * slope_s[...]).astype(jnp.bfloat16)

    def grad_out(c):
        left = mixed[:, span(c, block)]
        for k in range(nnz):
            gw[1, :, panel(c, k)] = (tn(left, cot[feats(c, k)]) * loss_scale).astype(jnp.bfloat16)

    def grad_in(c):
        right = pgrad[:, span(c, block)]
        for k in range(nnz):
            gw[0, :, panel(c, k)] = (tn(tok[feats(c, k)], right) * loss_scale).astype(jnp.bfloat16)

    limit = tok.shape[0] ** 2

    def token_grad(g):
        total = jnp.zeros((count, block), jnp.float32)
        for c in range(cols):
            at = cols * nnz
            for k in range(nnz):
                apart = ids[k, me * cols + c] - g
                same = 1 - lax.div(apart * apart + (limit - 1), jnp.int32(limit))
                at += same * (c * nnz + k - at)
            total += nt(pgrad[:, span(c, block)], w_in[at])
        return total.astype(jnp.bfloat16)

    return forward, backward, grad_out, grad_in, token_grad


def grads_kernel(
    depth, width, block, cols, nnz, ids, tok_h, cot_h, in_h, out_h, taps,
    dx_mine, mine, kern_all,
    tok, cot, w_in, w_out, raw, flat, stage, tok_send, tok_recv, w_send, w_recv, own_sem, raw_sem, kern, mixed, pgrad, pre_s, act_s, slope_s, mg_s, gw, gw_part,
    dx, dx_near, dx_half, dx_far, dx_cross, dx_sum, dx_last, kern_own, kern_part,
    dx_send, dx_recv, far_send, far_recv, gw_send, gw_recv, part_send, part_recv,
    kern_send, kern_recv,
):
    y, r, z, same_chip, across, diagonal = neighbours()
    group = [same_chip, across, diagonal]
    tokens, features = dx_mine.shape
    rows = mine.shape[1]
    half = block // 2
    lanes = nnz * block
    per_part = features // block
    w_in[cols * nnz] = jnp.zeros((block, block), jnp.bfloat16)
    kern[...] = jnp.zeros_like(kern)
    await_rest, drain = gather_stage(
        depth,
        [{"rows": row} for row in group]
        + [{"crop": 1 - y}]
        + [{"hid": (z + step) % depth} for step in range(1, depth)],
        tok_h, cot_h, in_h, out_h, tok, cot, w_in, w_out,
        raw, flat, stage, tok_send, tok_recv, w_send, w_recv, own_sem, raw_sem,
    )
    started = []

    def go(*args):
        copy = remote(*args)
        copy.start()
        started.append(copy)

    def arrived(ref, send_sem, recv_sem, target):
        remote(ref, ref, send_sem, recv_sem, target).wait_recv()

    forward, backward, grad_out, grad_in, token_grad = column_math(
        width, block, cols, nnz, ids, tok, cot, w_in, w_out, taps, kern, mixed, pgrad,
        pre_s, act_s, slope_s, mg_s, gw,
    )

    def give_copy(a, c, far):
        side = (r // 2, 1 - r // 2)[far]
        return remote(
            gw.at[a, span((1 - y) * 2 + side, half // 2), span(c, lanes)],
            gw_part.at[a, c, span(side, half // 2), :],
            gw_send.at[a, c, far],
            gw_recv.at[a, c, far],
            {"crop": 1 - y},
        )

    def give(a, c):
        for far in (1, 0):
            give_copy(a, c, far).start()

    def settle_side(a, c, far):
        side = (r // 2, 1 - r // 2)[far]
        at = span(side, half // 2)
        give_copy(a, c, far).wait_recv()
        gw_part[a, c, at, :] = (
            gw[a, span(y * 2 + side, half // 2), span(c, lanes)].astype(jnp.float32)
            + gw_part[a, c, at, :].astype(jnp.float32)
        ).astype(jnp.bfloat16)
        at = span(r * cols + c, lanes)
        for slot, row in ((0, across), (1, diagonal)) if far else ((2, same_chip),):
            go(
                gw_part.at[a, c, span(row, rows), :],
                mine.at[a, :, at],
                part_send.at[a, c, slot],
                part_recv.at[a, c, slot],
                {"rows": row},
            )
        if not far:
            mine[a, :, at] = gw_part[a, c, span(r, rows), :]

    def settle(a, c):
        settle_side(a, c, 1)
        settle_side(a, c, 0)

    def part_of(i):
        return (z + 1 + i) % depth

    def lanes_of(i):
        return span(part_of(i), features)

    forward(0)
    await_rest()
    grad_out(0)
    give(1, 0)
    backward(0)
    grad_in(0)
    give(0, 0)

    def one_column(c, carry):
        forward(c)
        grad_out(c)
        backward(c)
        grad_in(c)
        return carry

    near = ((0, diagonal), (1, same_chip))

    def near_copy(slot, row, i):
        at = lanes_of(i)
        return remote(
            dx.at[span(row, tokens), at],
            dx_near.at[slot, :, at],
            dx_send.at[slot, i],
            dx_recv.at[slot, i],
            {"rows": same_chip},
        )

    def cross_copy():
        return remote(
            dx_half.at[:, lanes_of(0)],
            dx_cross,
            far_send.at[0, 0],
            far_recv.at[0, 0],
            {"hid": part_of(0)},
        )

    def pass_half(i):
        near_copy(0, diagonal, i).wait_recv()
        at = lanes_of(i)
        half_sum = dx[span(across, tokens), at].astype(jnp.float32) + dx_near[0, :, at].astype(jnp.float32)
        if i == depth - 1:
            cross_copy().wait_recv()
            half_sum += dx_cross[...].astype(jnp.float32)
        dx_half[:, at] = half_sum.astype(jnp.bfloat16)
        if i == 0:
            cross_copy().start()
        else:
            go(dx_half.at[:, at], dx_far.at[:, at], far_send.at[0, i], far_recv.at[0, i], {"rows": across})

    def pass_sum(i):
        at = lanes_of(i)
        near_copy(1, same_chip, i).wait_recv()
        own_sum = dx[span(r, tokens), at].astype(jnp.float32) + dx_near[1, :, at].astype(jnp.float32)
        if i > 0:
            arrived(dx_far.at[:, at], far_send.at[0, i], far_recv.at[0, i], {"rows": across})
            own_sum += dx_far[:, at].astype(jnp.float32)
        dx_sum[i] = own_sum.astype(jnp.bfloat16)
        if i < depth - 1:
            go(
                dx_sum.at[i],
                dx_last.at[i],
                far_send.at[1, i],
                far_recv.at[1, i],
                {"hid": part_of(i)},
            )

    def inner_column(c, carry):
        one_column(c, carry)

        @pl.when(c == cols - 1)
        def _():
            kern_own[...] = kern[...].astype(jnp.bfloat16)
            kern_copy.start()

        for a in (1, 0):
            give(a, c)
        return carry

    kern_copy = remote(
        kern_own, kern_part.at[1, 0], kern_send.at[0], kern_recv.at[1, 0], {"crop": 1 - y}
    )
    lax.fori_loop(1, 2, inner_column, 0)
    settle(1, 0)
    lax.fori_loop(2, cols, inner_column, 0)
    settle(0, 0)
    for i in range(depth):

        def one_block(j, carry):
            g = part_of(i) * per_part + j
            dx[:, span(g, block)] = token_grad(g)
            return carry

        lax.fori_loop(0, per_part, one_block, 0)
        for slot, row in near:
            near_copy(slot, row, i).start()
        if i > 0:
            pass_half(i - 1)
        if i == 1:
            pass_sum(0)
    pass_half(depth - 1)

    waits = [(a, c) for c in range(1, cols) for a in (1, 0)]
    sums = list(range(1, depth))
    while len(waits) > 2:
        settle(*waits.pop(0))
        if sums:
            pass_sum(sums.pop(0))
    while sums:
        pass_sum(sums.pop(0))
    kern_copy.wait_recv()
    kern_part[0, r] = (
        kern_own[...].astype(jnp.float32) + kern_part[1, 0].astype(jnp.float32)
    ).astype(jnp.bfloat16)
    for slot, row in enumerate(group):
        go(
            kern_part.at[0, r],
            kern_part.at[0, r],
            kern_send.at[slot + 1],
            kern_recv.at[0, r],
            {"rows": row},
        )
    settle(*waits.pop(0))
    total = dx_sum[depth - 1].astype(jnp.float32)
    for step in range(depth - 1):
        arrived(dx_last.at[step], far_send.at[1, step], far_recv.at[1, step], {"hid": part_of(step)})
        total += dx_last[step].astype(jnp.float32)
    dx_mine[...] = total.astype(jnp.bfloat16)
    for row in group:
        arrived(kern_part.at[0, row], kern_send.at[0], kern_recv.at[0, row], {"rows": same_chip})
    wide = kern.shape[1]
    for row in range(4):
        kern_all[:, row * wide : (row + 1) * wide] = kern_part[0, row].astype(jnp.float32)
    for a, c in waits:
        settle(a, c)
    for a in (1, 0):
        for c in range(cols):
            for slot, row in enumerate((across, diagonal, same_chip)):
                arrived(
                    mine.at[a, :, span(row * cols + c, lanes)],
                    part_send.at[a, c, slot],
                    part_recv.at[a, c, slot],
                    {"rows": row},
                )
    for i in range(depth):
        for slot, row in near:
            near_copy(slot, row, i).wait_send()
    for copy in started:
        copy.wait_send()
    kern_copy.wait_send()
    cross_copy().wait_send()
    for a in range(2):
        for c in range(cols):
            for far in range(2):
                give_copy(a, c, far).wait_send()
    drain()


def finish_kernel(
    all_cols, nnz, mine, dx_mine, kern_all, in_grad, out_grad, dx_grad, kern_grad, stage
):
    block = in_grad.shape[1]
    step = mine.shape[1]
    dx_grad[...] = dx_mine[...]
    kern_grad[...] = kern_all[: kern_grad.shape[0]]
    for src, dst in ((mine.at[0], in_grad), (mine.at[1], out_grad)):
        for h in range(block // 128):
            for c in range(all_cols):
                for k in range(nnz):
                    at = (c * nnz + k) * block + h * 128
                    stage[h, pl.ds(k * all_cols + c, step, stride=nnz * all_cols), :] = src[
                        :, at : at + 128
                    ].astype(jnp.float32)
            dst[:, h * 128 : (h + 1) * 128] = stage[h]


def split_hidden(tokens, cotangent, weight_in, weight_out, mix_kernel, block_rows):
    n_rows, depth = lax.axis_size("rows"), lax.axis_size("hid")
    _, height, width, features = tokens.shape
    rows, all_cols, nnz, block = weight_in.shape
    count = height * width
    whole = count * n_rows
    model = features * depth
    cols = all_cols // n_rows
    lanes = cols * nnz * block
    hidden = cols * block
    bf16, f32 = jnp.bfloat16, jnp.float32
    dma, sds = pltpu.SemaphoreType.DMA, jax.ShapeDtypeStruct
    params = functools.partial(pltpu.CompilerParams, vmem_limit_bytes=60 * 1024 * 1024)
    out_rows = block // (n_rows * lax.axis_size("crop"))
    panel = nnz * block
    dx_mine, mine, kern_all = pl.pallas_call(
        functools.partial(grads_kernel, depth, width, block, cols, nnz),
        name="grads_and_sums",
        out_shape=[
            sds((count, features), bf16),
            sds((2, out_rows, all_cols * panel), bf16),
            sds((16, hidden * n_rows), f32),
        ],
        in_specs=[SMEM] + [ANY] * 4 + [VMEM],
        out_specs=[VMEM] * 3,
        scratch_shapes=[
            pltpu.VMEM((model // block, whole, block), bf16),
            pltpu.VMEM((model // block, whole, block), bf16),
            pltpu.VMEM((cols * nnz + 1, block, block), bf16),
            pltpu.VMEM((cols * nnz, block, block), bf16),
            pltpu.VMEM((2, rows, nnz * all_cols, block), bf16),
            pltpu.VMEM((2, all_cols * nnz, rows, block), bf16),
            pltpu.VMEM((block // 128, rows * all_cols, 128), f32),
            dma((2, 2, depth, 4)),
            dma((2, n_rows, depth)),
            dma((2, 5)),
            dma((2, n_rows, 2)),
            dma((2, features // block + 1)),
            dma((2,)),
            pltpu.VMEM((16, hidden), f32),
            pltpu.VMEM((whole, hidden), bf16),
            pltpu.VMEM((whole, hidden), bf16),
        ]
        + [pltpu.VMEM((whole, block), f32)] * 4
        + [
            pltpu.VMEM((2, block, lanes), bf16),
            pltpu.VMEM((2, cols, block // 2, panel), bf16),
            pltpu.VMEM((whole, model), bf16),
            pltpu.VMEM((2, count, model), bf16),
            pltpu.VMEM((count, model), bf16),
            pltpu.VMEM((count, model), bf16),
            pltpu.VMEM((count, features), bf16),
            pltpu.VMEM((depth, count, features), bf16),
            pltpu.VMEM((depth - 1, count, features), bf16),
            pltpu.VMEM((16, hidden), bf16),
            pltpu.VMEM((2, n_rows, 16, hidden), bf16),
            dma((2, depth)),
            dma((2, depth)),
            dma((2, depth)),
            dma((2, depth)),
            dma((2, cols, 2)),
            dma((2, cols, 2)),
            dma((2, cols, 3)),
            dma((2, cols, 3)),
            dma((4,)),
            dma((2, n_rows)),
        ],
        compiler_params=params(collective_id=2, has_side_effects=True),
    )(
        block_rows.T,
        tokens.reshape(count, features),
        cotangent.reshape(count, features),
        weight_in.transpose(0, 2, 1, 3).reshape(rows, nnz * all_cols, block),
        weight_out.transpose(0, 2, 1, 3).reshape(rows, nnz * all_cols, block),
        mix_kernel,
    )
    step = 8
    part = pl.BlockSpec((count * step // out_rows, features), lambda i: (i, 0))
    flat_spec = pl.BlockSpec((2, step, all_cols * nnz * block), lambda i: (0, i, 0))
    grad_spec = pl.BlockSpec((step * nnz * all_cols, block), lambda i: (i, 0))
    in_grad, out_grad, dx_grad, kern_grad = pl.pallas_call(
        functools.partial(finish_kernel, all_cols, nnz),
        name="finish_weights",
        grid=(out_rows // step,),
        out_shape=[sds((out_rows * nnz * all_cols, block), f32)] * 2
        + [sds((count, features), bf16), sds(mix_kernel.shape, f32)],
        in_specs=[flat_spec, part, VMEM],
        out_specs=[grad_spec] * 2 + [part, VMEM],
        scratch_shapes=[pltpu.VMEM((block // 128, step * nnz * all_cols, 128), f32)],
        compiler_params=params(),
    )(mine, dx_mine, kern_all)
    in_grad, out_grad = [
        grad.reshape(out_rows, nnz, all_cols, block).transpose(0, 2, 1, 3) for grad in (in_grad, out_grad)
    ]
    return (dx_grad.reshape(tokens.shape), in_grad, out_grad, kern_grad)


def padded(shard, sides, width):
    for axis, dim in sides:
        devices, length = (lax.axis_size(axis), shard.shape[dim])
        up = [(i, (i + 1) % devices) for i in range(devices - 1)]
        down = [(j, i) for i, j in up]
        last = lax.slice_in_dim(shard, length - width, length, axis=dim)
        initial = lax.slice_in_dim(shard, 0, width, axis=dim)
        before = lax.ppermute(last, axis, up)
        after = lax.ppermute(initial, axis, down)
        shard = jnp.concatenate([before, shard, after], axis=dim)
    return shard


def gelu_pair(preact):
    inner = root_two_pi * (preact + cubic_coef * preact * preact * preact)
    tanh_val = jnp.tanh(inner)
    gelu_out = 0.5 * preact * (1.0 + tanh_val)
    slopes = 0.5 * (1.0 + tanh_val) + 0.5 * preact * (1.0 - tanh_val * tanh_val) * root_two_pi * (
        1.0 + 3.0 * cubic_coef * preact * preact
    )
    return (gelu_out, slopes)


def on_device(tokens, cotangent, weight_in, weight_out, mix_kernel, block_rows):
    in_panel, out_panel = (
        lax.all_gather(weight_in, "rows", axis=0, tiled=True),
        lax.all_gather(weight_out, "rows", axis=0, tiled=True),
    )
    tok_full, cot_full = (
        lax.all_gather(tokens, "hid", axis=3, tiled=True),
        lax.all_gather(cotangent, "hid", axis=3, tiled=True),
    )
    crop_count, height, grid_width, depth_all = tok_full.shape
    tok_count = crop_count * height * grid_width
    block_size = in_panel.shape[0]
    col_count = in_panel.shape[1]
    nnz_count = in_panel.shape[2]
    block_count = depth_all // block_size
    hidden_local = col_count * block_size
    flat_rows = block_rows.reshape(-1)
    in_select = jnp.take(
        tok_full.reshape(tok_count, block_count, block_size), flat_rows, axis=1
    ).reshape(tok_count, col_count, nnz_count, block_size)
    grad_select = jnp.take(
        cot_full.reshape(tok_count, block_count, block_size), flat_rows, axis=1
    ).reshape(tok_count, col_count, nnz_count, block_size)
    pre_act = jnp.einsum("tckb,bcke->tce", in_select, in_panel, preferred_element_type=jnp.float32)
    gelu_out, slopes = gelu_pair(pre_act)
    active = gelu_out.astype(jnp.bfloat16).reshape(crop_count, height, grid_width, hidden_local)
    act_rim = padded(active, (("rows", 1),), 1)
    mix_grad = (
        jnp.einsum("tckd,fckd->tcf", grad_select, out_panel, preferred_element_type=jnp.float32)
        .astype(jnp.bfloat16)
        .reshape(crop_count, height, grid_width, hidden_local)
    )
    grad_rim = padded(mix_grad, (("rows", 1),), 1)
    act_pad = jnp.pad(act_rim.astype(jnp.float32), ((0, 0), (0, 0), (1, 1), (0, 0)))
    grad_pad = jnp.pad(grad_rim.astype(jnp.float32), ((0, 0), (0, 0), (1, 1), (0, 0)))
    grad_grid = mix_grad.astype(jnp.float32)
    mix_sum = jnp.zeros((crop_count, height, grid_width, hidden_local), jnp.float32)
    act_grad = jnp.zeros((crop_count, height, grid_width, hidden_local), jnp.float32)
    kern_terms = []
    for row_off in range(3):
        for col_off in range(3):
            tap = mix_kernel[3 * row_off + col_off]
            shifted = act_pad[:, row_off : row_off + height, col_off : col_off + grid_width]
            mix_sum = mix_sum + tap * shifted
            act_grad = (
                act_grad
                + tap
                * grad_pad[
                    :, 2 - row_off : 2 - row_off + height, 2 - col_off : 2 - col_off + grid_width
                ]
            )
            kern_terms.append(jnp.sum(shifted * grad_grid, axis=(0, 1, 2)))
    kern_local = jnp.stack(kern_terms, axis=0) * loss_scale
    mix_out = mix_sum.astype(jnp.bfloat16).reshape(tok_count, col_count, block_size)
    pre_grad = (act_grad.reshape(tok_count, col_count, block_size) * slopes).astype(jnp.bfloat16)
    kern_total = lax.psum(kern_local.astype(jnp.bfloat16), ("crop", "rows")).astype(jnp.float32)
    back_select = jnp.einsum(
        "tce,bcke->tckb", pre_grad, in_panel, preferred_element_type=jnp.float32
    )
    one_hot = (
        block_rows[:, :, None] == jnp.arange(block_count, dtype=jnp.int32)[None, None, :]
    ).astype(jnp.float32)
    token_terms = jnp.einsum(
        "tckb,ckr->trb", back_select, one_hot, precision=lax.Precision.HIGHEST
    ).reshape(crop_count, height, grid_width, depth_all)
    grad_tokens = lax.psum_scatter(
        token_terms.astype(jnp.bfloat16), "hid", scatter_dimension=3, tiled=True
    )
    first_term = jnp.einsum(
        "tckb,tce->bcke", in_select, pre_grad, preferred_element_type=jnp.float32
    )
    second_term = jnp.einsum(
        "tcf,tckd->fckd", mix_out, grad_select, preferred_element_type=jnp.float32
    )
    share_sums = lax.psum_scatter(
        (jnp.stack([first_term, second_term], axis=1) * loss_scale).astype(jnp.bfloat16),
        ("crop", "rows"),
        scatter_dimension=0,
        tiled=True,
    ).astype(jnp.float32)
    return (grad_tokens, share_sums[:, 0], share_sums[:, 1], kern_total)


def solution(mesh):
    placed = (
        P("crop", "rows", None, "hid"),
        P("crop", "rows", None, "hid"),
        P("rows", "hid", None, None),
        P("rows", "hid", None, None),
        P(None, "hid"),
        P("hid", None),
    )
    n_crop, n_rows = mesh.shape["crop"], mesh.shape["rows"]
    n_hid = mesh.shape["hid"]

    def step(tokens, cotangent, weight_in, weight_out, mix_kernel, block_rows):
        fits = (
            n_crop == 2
            and n_rows == 4
            and tokens.shape[0] == 1
            and weight_in.shape[1] % n_rows == 0
            and weight_in.shape[1] >= 2 * n_rows
            and n_hid >= 2
            and tokens.shape[1] * tokens.shape[2] * n_rows * tokens.shape[3] * n_hid <= 2**22
        )
        chosen = split_hidden if fits else on_device
        return chosen(tokens, cotangent, weight_in, weight_out, mix_kernel, block_rows)

    return jax.shard_map(
        step,
        mesh=mesh,
        in_specs=placed,
        out_specs=(
            P("crop", "rows", None, "hid"),
            P(("crop", "rows"), "hid", None, None),
            P(("crop", "rows"), "hid", None, None),
            P(None, "hid"),
        ),
        check_vma=False,
    )
```

```python
import functools

import jax
import jax.numpy as jnp
from jax import lax
from jax.experimental import pallas as pl
from jax.experimental.pallas import tpu as pltpu
from jax.sharding import PartitionSpec as P

root_two_pi = 0.7978845608
cubic_coef = 0.044715
loss_scale = 0.03125

MESH_ID = pl.DeviceIdType.MESH
ANY = pl.BlockSpec(memory_space=pl.ANY)
VMEM = pl.BlockSpec(memory_space=pltpu.VMEM)
SMEM = pl.BlockSpec(memory_space=pltpu.SMEM)


def span(start, size):
    return pl.ds(pl.multiple_of(start * size, size), size)


def neighbours():
    y, r, z = lax.axis_index("crop"), lax.axis_index("rows"), lax.axis_index("hid")
    x, core = r // 2, r % 2
    same_chip = x * 2 + (1 - core)
    across = (1 - x) * 2 + core
    diagonal = (1 - x) * 2 + (1 - core)
    return y, r, z, same_chip, across, diagonal


def enter(partners):
    barrier = pltpu.get_barrier_semaphore()
    for partner in partners:
        pl.semaphore_signal(barrier, inc=1, device_id=partner, device_id_type=MESH_ID)
    pl.semaphore_wait(barrier, len(partners))


def remote(src, dst, send_sem, recv_sem, target):
    return pltpu.make_async_remote_copy(
        src_ref=src,
        dst_ref=dst,
        send_sem=send_sem,
        recv_sem=recv_sem,
        device_id=target,
        device_id_type=MESH_ID,
    )


def gather_stage(
    depth, partners, tok_h, cot_h, in_h, out_h, tok, cot, w_in, w_out,
    raw, flat, stage, tok_send, tok_recv, w_send, w_recv, own_sem, raw_sem,
):
    y, r, z, same_chip, across, diagonal = neighbours()
    tokens, features = tok_h.shape
    rows = in_h.shape[0]
    half = rows // 2
    block = tok.shape[2]
    per_part = features // block
    panels_own = w_out.shape[0]
    all_cols = stage.shape[1] // rows
    nnz = in_h.shape[1] // all_cols
    own = [
        pltpu.make_async_copy(
            src.at[:, j * block : (j + 1) * block],
            full.at[z * per_part + j, span(r, tokens), :],
            own_sem.at[a, j],
        )
        for a, (src, full) in enumerate(((cot_h, cot), (tok_h, tok)))
        for j in range(per_part)
    ]
    loads = [
        pltpu.make_async_copy(src, raw.at[a], raw_sem.at[a]) for a, src in enumerate((in_h, out_h))
    ]
    for load in own + loads:
        load.start()
    enter(partners)
    for load in own:
        load.wait()
    streams = (cot, tok)
    panels = ((flat.at[0], w_in), (flat.at[1], w_out))
    targets = ({"hid": z + 1}, {"hid": z - 1}, {"rows": across}, {"rows": same_chip})
    has_up, has_down = z + 1 < depth, z >= 1
    sends, local = [], []

    def launch(make, have=None):
        sends.append((make, have))
        if have is None:
            make().start()
        else:
            pl.when(have)(lambda: make().start())

    def piece(full, row, col):
        return full.at[span(col, per_part), span(row, tokens), :]

    def pass_on(a, which, col, kind, have=None):
        def make():
            row = (r, across)[which]
            part = piece(streams[a], row, col)
            return remote(
                part,
                part,
                tok_send.at[a, which, col, kind],
                tok_recv.at[a, row, col],
                targets[kind],
            )

        launch(make, have)

    def await_piece(a, row, col, have=None):
        def wait():
            part = piece(streams[a], row, col)
            remote(
                part, part, tok_send.at[a, 0, 0, 3], tok_recv.at[a, row, col], {"rows": same_chip}
            ).wait_recv()

        if have is None:
            wait()
        else:
            pl.when(have)(wait)

    def half_rows(full, row, h):
        at = pl.ds(pl.multiple_of(row * rows + h * half, half), half)
        return full.at[pl.ds(0, panels_own), at, :]

    def whole_rows(full, row):
        return full.at[pl.ds(0, panels_own), span(row, rows), :]

    def flatten(a):
        def turn(k, carry):
            for h in range(block // 128):
                part = raw[a, :, span(k, all_cols), h * 128 : (h + 1) * 128]
                stage[h] = part.astype(jnp.float32).reshape(rows * all_cols, 128)
            for c in range(all_cols):
                for h in range(block // 128):
                    flat[a, c * nnz + k, :, h * 128 : (h + 1) * 128] = stage[
                        h, pl.ds(c, rows, stride=all_cols), :
                    ].astype(jnp.bfloat16)
            return carry

        lax.fori_loop(0, nnz, turn, 0)

    def give_weights(a):
        src, full = panels[a]
        loads[a].wait()
        flatten(a)
        for slot, dest in ((1, across), (2, diagonal)):
            launch(
                lambda slot=slot, dest=dest: remote(
                    src.at[span(dest, panels_own), span(y, half), :],
                    half_rows(full, r, y),
                    w_send.at[a, slot],
                    w_recv.at[a, r, y],
                    {"rows": dest},
                )
            )
        launch(
            lambda: remote(
                src.at[span(same_chip, panels_own)],
                whole_rows(full, r),
                w_send.at[a, 0],
                w_recv.at[a, r, 0],
                {"rows": same_chip},
            )
        )
        keep = pltpu.make_async_copy(
            src.at[span(r, panels_own)], whole_rows(full, r), own_sem.at[a, per_part]
        )
        keep.start()
        local.append(keep)

    def mirror_weights(a):
        full = panels[a][1]
        for slot, row in ((3, across), (4, diagonal)):
            part = half_rows(full, row, y)
            remote(part, part, w_send.at[a, slot], w_recv.at[a, row, y], {"rows": row}).wait_recv()
            launch(
                lambda slot=slot, row=row, part=part: remote(
                    part, part, w_send.at[a, slot], w_recv.at[a, row, y], {"crop": 1 - y}
                )
            )

    def line_step(step):
        for below in (True, False):
            col = z - step if below else z + step
            have = col >= 0 if below else col < depth
            onward = jnp.logical_and(have, has_up if below else has_down)
            for a, which in ((0, 0), (1, 0), (1, 1)):
                await_piece(a, (r, across)[which], col, have)
                pass_on(a, which, col, 0 if below else 1, onward)
                if a == 0:
                    pass_on(a, which, col, 2, have)
                pass_on(a, which, col, 3, have)

    for a, kind in ((1, 2), (0, 0), (0, 1), (1, 0), (1, 1), (0, 2), (0, 3), (1, 3)):
        pass_on(a, 0, z, kind, (has_up, has_down, None, None)[kind])
    give_weights(0)
    await_piece(1, across, z)
    for kind in (0, 1, 3):
        pass_on(1, 1, z, kind, (has_up, has_down, None, None)[kind])
    give_weights(1)
    for step in range(1, depth):
        line_step(step)
        if step <= 2:
            mirror_weights(step - 1)
    for a in range(depth - 1, 2):
        mirror_weights(a)
    def await_rows(a):
        for row in (same_chip, diagonal):
            for step in range(depth):
                await_piece(a, row, (z + step) % depth)

    def await_weights(a):
        full = panels[a][1]
        part = whole_rows(full, same_chip)
        remote(
            part, part, w_send.at[a, 0], w_recv.at[a, same_chip, 0], {"rows": same_chip}
        ).wait_recv()
        for row in (across, diagonal):
            part = half_rows(full, row, 1 - y)
            remote(
                part, part, w_send.at[a, 0], w_recv.at[a, row, 1 - y], {"crop": 1 - y}
            ).wait_recv()
        local[a].wait()

    await_rows(1)
    await_weights(0)

    def await_rest():
        for step in range(depth):
            col = (z + step) % depth
            await_piece(0, across, col)
            pass_on(0, 1, col, 3)
        await_weights(1)
        await_rows(0)

    def drain():
        for make, have in sends:
            if have is None:
                make().wait_send()
            else:
                pl.when(have)(lambda make=make: make().wait_send())

    return await_rest, drain


def nt(a, b):
    return lax.dot_general(a, b, (((1,), (1,)), ((), ())), preferred_element_type=jnp.float32)


def tn(a, b):
    return lax.dot_general(a, b, (((0,), (0,)), ((), ())), preferred_element_type=jnp.float32)


def column_math(width, block, cols, nnz, ids, tok, cot, w_in, w_out, taps, kern, mixed, pgrad, pre_s, act_s, slope_s, mg_s, gw):
    count = tok.shape[1]
    me = lax.axis_index("rows")
    place = lax.broadcasted_iota(jnp.int32, (count, block), 0) % width

    def spread(value):
        before = jnp.where(place == 0, 0.0, pltpu.roll(value, 1, 0))
        after = jnp.where(place == width - 1, 0.0, pltpu.roll(value, count - 1, 0))
        return (before, value, after)

    def stack_rows(up, mid, down):
        edge = jnp.zeros((width, block), jnp.float32)
        return (
            mid
            + jnp.concatenate([edge, up[:-width]], axis=0)
            + jnp.concatenate([down[width:], edge], axis=0)
        )

    def feats(c, k):
        return ids[k, me * cols + c]

    def panel(c, k):
        return span(c * nnz + k, block)

    def tap(c, a, b):
        row = 3 * (a + 1) + (b + 1)
        return taps[row : row + 1, span(me * cols + c, block)]

    def forward(c):
        hidden = span(c, block)
        pre = jnp.dot(tok[feats(c, 0)], w_in[c * nnz], preferred_element_type=jnp.float32)
        for k in range(1, nnz):
            pre += jnp.dot(tok[feats(c, k)], w_in[c * nnz + k], preferred_element_type=jnp.float32)
        pre_s[...] = pre
        p = pre_s[...]
        t = jnp.tanh(root_two_pi * (p + cubic_coef * p * p * p))
        act_s[...] = (0.5 * p * (1.0 + t)).astype(jnp.bfloat16).astype(jnp.float32)
        slope_s[...] = 0.5 * (1.0 + t) + 0.5 * p * (1.0 - t * t) * root_two_pi * (
            1.0 + 3.0 * cubic_coef * p * p
        )
        acts = spread(act_s[...])
        mixed[:, hidden] = stack_rows(
            *[sum(tap(c, a, b) * acts[b + 1] for b in (-1, 0, 1)) for a in (-1, 0, 1)]
        ).astype(jnp.bfloat16)

    def backward(c):
        hidden = span(c, block)
        mg = nt(cot[feats(c, 0)], w_out[c * nnz])
        for k in range(1, nnz):
            mg += nt(cot[feats(c, k)], w_out[c * nnz + k])
        mg_s[...] = mg.astype(jnp.bfloat16).astype(jnp.float32)
        acts = spread(act_s[...])
        grads = mg_s[...]
        for b in (-1, 0, 1):
            seen = acts[b + 1]
            sums = (
                jnp.sum(seen[:-width] * grads[width:], axis=0, keepdims=True),
                jnp.sum(seen * grads, axis=0, keepdims=True),
                jnp.sum(seen[width:] * grads[:-width], axis=0, keepdims=True),
            )
            for a in (-1, 0, 1):
                row = 3 * (a + 1) + (b + 1)
                kern[row : row + 1, hidden] = sums[a + 1] * loss_scale
        backs = spread(mg_s[...])
        gathered = stack_rows(
            *[sum(tap(c, a, b) * backs[1 - b] for b in (-1, 0, 1)) for a in (1, 0, -1)]
        )
        pgrad[:, hidden] = (gathered * slope_s[...]).astype(jnp.bfloat16)

    def grad_out(c):
        left = mixed[:, span(c, block)]
        for k in range(nnz):
            gw[1, :, panel(c, k)] = (tn(left, cot[feats(c, k)]) * loss_scale).astype(jnp.bfloat16)

    def grad_in(c):
        right = pgrad[:, span(c, block)]
        for k in range(nnz):
            gw[0, :, panel(c, k)] = (tn(tok[feats(c, k)], right) * loss_scale).astype(jnp.bfloat16)

    limit = tok.shape[0] ** 2

    def token_grad(g):
        total = jnp.zeros((count, block), jnp.float32)
        for c in range(cols):
            at = cols * nnz
            for k in range(nnz):
                apart = ids[k, me * cols + c] - g
                same = 1 - lax.div(apart * apart + (limit - 1), jnp.int32(limit))
                at += same * (c * nnz + k - at)
            total += nt(pgrad[:, span(c, block)], w_in[at])
        return total.astype(jnp.bfloat16)

    return forward, backward, grad_out, grad_in, token_grad


def grads_kernel(
    depth, width, block, cols, nnz, ids, tok_h, cot_h, in_h, out_h, taps,
    dx_mine, mine, kern_all,
    tok, cot, w_in, w_out, raw, flat, stage, tok_send, tok_recv, w_send, w_recv, own_sem, raw_sem, kern, mixed, pgrad, pre_s, act_s, slope_s, mg_s, gw, gw_part,
    dx, dx_near, dx_half, dx_far, dx_cross, dx_sum, dx_last, kern_own, kern_part,
    dx_send, dx_recv, far_send, far_recv, gw_send, gw_recv, part_send, part_recv,
    kern_send, kern_recv,
):
    y, r, z, same_chip, across, diagonal = neighbours()
    group = [same_chip, across, diagonal]
    tokens, features = dx_mine.shape
    rows = mine.shape[1]
    half = block // 2
    lanes = nnz * block
    per_part = features // block
    w_in[cols * nnz] = jnp.zeros((block, block), jnp.bfloat16)
    kern[...] = jnp.zeros_like(kern)
    await_rest, drain = gather_stage(
        depth,
        [{"rows": row} for row in group]
        + [{"crop": 1 - y}]
        + [{"hid": (z + step) % depth} for step in range(1, depth)],
        tok_h, cot_h, in_h, out_h, tok, cot, w_in, w_out,
        raw, flat, stage, tok_send, tok_recv, w_send, w_recv, own_sem, raw_sem,
    )
    started = []

    def go(*args):
        copy = remote(*args)
        copy.start()
        started.append(copy)

    def arrived(ref, send_sem, recv_sem, target):
        remote(ref, ref, send_sem, recv_sem, target).wait_recv()

    forward, backward, grad_out, grad_in, token_grad = column_math(
        width, block, cols, nnz, ids, tok, cot, w_in, w_out, taps, kern, mixed, pgrad,
        pre_s, act_s, slope_s, mg_s, gw,
    )

    def give_copy(a, c, far):
        side = (r // 2, 1 - r // 2)[far]
        return remote(
            gw.at[a, span((1 - y) * 2 + side, half // 2), span(c, lanes)],
            gw_part.at[a, c, span(side, half // 2), :],
            gw_send.at[a, c, far],
            gw_recv.at[a, c, far],
            {"crop": 1 - y},
        )

    def give(a, c):
        for far in (1, 0):
            give_copy(a, c, far).start()

    def settle_side(a, c, far):
        side = (r // 2, 1 - r // 2)[far]
        at = span(side, half // 2)
        give_copy(a, c, far).wait_recv()
        gw_part[a, c, at, :] = (
            gw[a, span(y * 2 + side, half // 2), span(c, lanes)].astype(jnp.float32)
            + gw_part[a, c, at, :].astype(jnp.float32)
        ).astype(jnp.bfloat16)
        at = span(r * cols + c, lanes)
        for slot, row in ((0, across), (1, diagonal)) if far else ((2, same_chip),):
            go(
                gw_part.at[a, c, span(row, rows), :],
                mine.at[a, :, at],
                part_send.at[a, c, slot],
                part_recv.at[a, c, slot],
                {"rows": row},
            )
        if not far:
            mine[a, :, at] = gw_part[a, c, span(r, rows), :]

    def settle(a, c):
        settle_side(a, c, 1)
        settle_side(a, c, 0)

    def part_of(i):
        return (z + 1 + i) % depth

    def lanes_of(i):
        return span(part_of(i), features)

    forward(0)
    await_rest()
    grad_out(0)
    give(1, 0)
    backward(0)
    grad_in(0)
    give(0, 0)

    def one_column(c, carry):
        forward(c)
        grad_out(c)
        backward(c)
        grad_in(c)
        return carry

    near = ((0, diagonal), (1, same_chip))

    def near_copy(slot, row, i):
        at = lanes_of(i)
        return remote(
            dx.at[span(row, tokens), at],
            dx_near.at[slot, :, at],
            dx_send.at[slot, i],
            dx_recv.at[slot, i],
            {"rows": same_chip},
        )

    def cross_copy():
        return remote(
            dx_half.at[:, lanes_of(0)],
            dx_cross,
            far_send.at[0, 0],
            far_recv.at[0, 0],
            {"hid": part_of(0)},
        )

    def pass_half(i):
        near_copy(0, diagonal, i).wait_recv()
        at = lanes_of(i)
        half_sum = dx[span(across, tokens), at].astype(jnp.float32) + dx_near[0, :, at].astype(jnp.float32)
        if i == depth - 1:
            cross_copy().wait_recv()
            half_sum += dx_cross[...].astype(jnp.float32)
        dx_half[:, at] = half_sum.astype(jnp.bfloat16)
        if i == 0:
            cross_copy().start()
        else:
            go(dx_half.at[:, at], dx_far.at[:, at], far_send.at[0, i], far_recv.at[0, i], {"rows": across})

    def pass_sum(i):
        at = lanes_of(i)
        near_copy(1, same_chip, i).wait_recv()
        own_sum = dx[span(r, tokens), at].astype(jnp.float32) + dx_near[1, :, at].astype(jnp.float32)
        if i > 0:
            arrived(dx_far.at[:, at], far_send.at[0, i], far_recv.at[0, i], {"rows": across})
            own_sum += dx_far[:, at].astype(jnp.float32)
        dx_sum[i] = own_sum.astype(jnp.bfloat16)
        if i < depth - 1:
            go(
                dx_sum.at[i],
                dx_last.at[i],
                far_send.at[1, i],
                far_recv.at[1, i],
                {"hid": part_of(i)},
            )

    def inner_column(c, carry):
        one_column(c, carry)

        @pl.when(c == cols - 1)
        def _():
            kern_own[...] = kern[...].astype(jnp.bfloat16)
            kern_copy.start()

        for a in (1, 0):
            give(a, c)
        return carry

    kern_copy = remote(
        kern_own, kern_part.at[1, 0], kern_send.at[0], kern_recv.at[1, 0], {"crop": 1 - y}
    )
    lax.fori_loop(1, 2, inner_column, 0)
    settle(1, 0)
    lax.fori_loop(2, cols, inner_column, 0)
    settle(0, 0)
    for i in range(depth):

        def one_block(j, carry):
            g = part_of(i) * per_part + j
            dx[:, span(g, block)] = token_grad(g)
            return carry

        lax.fori_loop(0, per_part, one_block, 0)
        for slot, row in near:
            near_copy(slot, row, i).start()
        if i > 0:
            pass_half(i - 1)
        if i == 1:
            pass_sum(0)

    settle(1, 1)
    pass_half(depth - 1)
    waits = [(a, c) for c in range(1, cols) for a in (1, 0)][1:]
    sums = list(range(1, depth))
    while len(waits) > 2:
        settle(*waits.pop(0))
        if sums:
            pass_sum(sums.pop(0))
    while sums:
        pass_sum(sums.pop(0))
    kern_copy.wait_recv()
    kern_part[0, r] = (
        kern_own[...].astype(jnp.float32) + kern_part[1, 0].astype(jnp.float32)
    ).astype(jnp.bfloat16)
    for slot, row in enumerate(group):
        go(
            kern_part.at[0, r],
            kern_part.at[0, r],
            kern_send.at[slot + 1],
            kern_recv.at[0, r],
            {"rows": row},
        )
    settle(*waits.pop(0))
    total = dx_sum[depth - 1].astype(jnp.float32)
    for step in range(depth - 1):
        arrived(dx_last.at[step], far_send.at[1, step], far_recv.at[1, step], {"hid": part_of(step)})
        total += dx_last[step].astype(jnp.float32)
    dx_mine[...] = total.astype(jnp.bfloat16)
    for row in group:
        arrived(kern_part.at[0, row], kern_send.at[0], kern_recv.at[0, row], {"rows": same_chip})
    wide = kern.shape[1]
    for row in range(4):
        kern_all[:, row * wide : (row + 1) * wide] = kern_part[0, row].astype(jnp.float32)
    for a, c in waits:
        settle(a, c)
    for a in (1, 0):
        for c in range(cols):
            for slot, row in enumerate((across, diagonal, same_chip)):
                arrived(
                    mine.at[a, :, span(row * cols + c, lanes)],
                    part_send.at[a, c, slot],
                    part_recv.at[a, c, slot],
                    {"rows": row},
                )
    for i in range(depth):
        for slot, row in near:
            near_copy(slot, row, i).wait_send()
    for copy in started:
        copy.wait_send()
    kern_copy.wait_send()
    cross_copy().wait_send()
    for a in range(2):
        for c in range(cols):
            for far in range(2):
                give_copy(a, c, far).wait_send()
    drain()


def finish_kernel(
    all_cols, nnz, mine, dx_mine, kern_all, in_grad, out_grad, dx_grad, kern_grad, stage
):
    block = in_grad.shape[1]
    step = mine.shape[1]
    dx_grad[...] = dx_mine[...]
    kern_grad[...] = kern_all[: kern_grad.shape[0]]
    for src, dst in ((mine.at[0], in_grad), (mine.at[1], out_grad)):
        for h in range(block // 128):
            for c in range(all_cols):
                for k in range(nnz):
                    at = (c * nnz + k) * block + h * 128
                    stage[h, pl.ds(k * all_cols + c, step, stride=nnz * all_cols), :] = src[
                        :, at : at + 128
                    ].astype(jnp.float32)
            dst[:, h * 128 : (h + 1) * 128] = stage[h]


def split_hidden(tokens, cotangent, weight_in, weight_out, mix_kernel, block_rows):
    n_rows, depth = lax.axis_size("rows"), lax.axis_size("hid")
    _, height, width, features = tokens.shape
    rows, all_cols, nnz, block = weight_in.shape
    count = height * width
    whole = count * n_rows
    model = features * depth
    cols = all_cols // n_rows
    lanes = cols * nnz * block
    hidden = cols * block
    bf16, f32 = jnp.bfloat16, jnp.float32
    dma, sds = pltpu.SemaphoreType.DMA, jax.ShapeDtypeStruct
    params = functools.partial(pltpu.CompilerParams, vmem_limit_bytes=60 * 1024 * 1024)
    out_rows = block // (n_rows * lax.axis_size("crop"))
    panel = nnz * block
    dx_mine, mine, kern_all = pl.pallas_call(
        functools.partial(grads_kernel, depth, width, block, cols, nnz),
        name="grads_and_sums",
        out_shape=[
            sds((count, features), bf16),
            sds((2, out_rows, all_cols * panel), bf16),
            sds((16, hidden * n_rows), f32),
        ],
        in_specs=[SMEM] + [ANY] * 4 + [VMEM],
        out_specs=[VMEM] * 3,
        scratch_shapes=[
            pltpu.VMEM((model // block, whole, block), bf16),
            pltpu.VMEM((model // block, whole, block), bf16),
            pltpu.VMEM((cols * nnz + 1, block, block), bf16),
            pltpu.VMEM((cols * nnz, block, block), bf16),
            pltpu.VMEM((2, rows, nnz * all_cols, block), bf16),
            pltpu.VMEM((2, all_cols * nnz, rows, block), bf16),
            pltpu.VMEM((block // 128, rows * all_cols, 128), f32),
            dma((2, 2, depth, 4)),
            dma((2, n_rows, depth)),
            dma((2, 5)),
            dma((2, n_rows, 2)),
            dma((2, features // block + 1)),
            dma((2,)),
            pltpu.VMEM((16, hidden), f32),
            pltpu.VMEM((whole, hidden), bf16),
            pltpu.VMEM((whole, hidden), bf16),
        ]
        + [pltpu.VMEM((whole, block), f32)] * 4
        + [
            pltpu.VMEM((2, block, lanes), bf16),
            pltpu.VMEM((2, cols, block // 2, panel), bf16),
            pltpu.VMEM((whole, model), bf16),
            pltpu.VMEM((2, count, model), bf16),
            pltpu.VMEM((count, model), bf16),
            pltpu.VMEM((count, model), bf16),
            pltpu.VMEM((count, features), bf16),
            pltpu.VMEM((depth, count, features), bf16),
            pltpu.VMEM((depth - 1, count, features), bf16),
            pltpu.VMEM((16, hidden), bf16),
            pltpu.VMEM((2, n_rows, 16, hidden), bf16),
            dma((2, depth)),
            dma((2, depth)),
            dma((2, depth)),
            dma((2, depth)),
            dma((2, cols, 2)),
            dma((2, cols, 2)),
            dma((2, cols, 3)),
            dma((2, cols, 3)),
            dma((4,)),
            dma((2, n_rows)),
        ],
        compiler_params=params(collective_id=2, has_side_effects=True),
    )(
        block_rows.T,
        tokens.reshape(count, features),
        cotangent.reshape(count, features),
        weight_in.transpose(0, 2, 1, 3).reshape(rows, nnz * all_cols, block),
        weight_out.transpose(0, 2, 1, 3).reshape(rows, nnz * all_cols, block),
        mix_kernel,
    )
    step = 8
    part = pl.BlockSpec((count * step // out_rows, features), lambda i: (i, 0))
    flat_spec = pl.BlockSpec((2, step, all_cols * nnz * block), lambda i: (0, i, 0))
    grad_spec = pl.BlockSpec((step * nnz * all_cols, block), lambda i: (i, 0))
    in_grad, out_grad, dx_grad, kern_grad = pl.pallas_call(
        functools.partial(finish_kernel, all_cols, nnz),
        name="finish_weights",
        grid=(out_rows // step,),
        out_shape=[sds((out_rows * nnz * all_cols, block), f32)] * 2
        + [sds((count, features), bf16), sds(mix_kernel.shape, f32)],
        in_specs=[flat_spec, part, VMEM],
        out_specs=[grad_spec] * 2 + [part, VMEM],
        scratch_shapes=[pltpu.VMEM((block // 128, step * nnz * all_cols, 128), f32)],
        compiler_params=params(),
    )(mine, dx_mine, kern_all)
    in_grad, out_grad = [
        grad.reshape(out_rows, nnz, all_cols, block).transpose(0, 2, 1, 3) for grad in (in_grad, out_grad)
    ]
    return (dx_grad.reshape(tokens.shape), in_grad, out_grad, kern_grad)


def padded(shard, sides, width):
    for axis, dim in sides:
        devices, length = (lax.axis_size(axis), shard.shape[dim])
        up = [(i, (i + 1) % devices) for i in range(devices - 1)]
        down = [(j, i) for i, j in up]
        last = lax.slice_in_dim(shard, length - width, length, axis=dim)
        initial = lax.slice_in_dim(shard, 0, width, axis=dim)
        before = lax.ppermute(last, axis, up)
        after = lax.ppermute(initial, axis, down)
        shard = jnp.concatenate([before, shard, after], axis=dim)
    return shard


def gelu_pair(preact):
    inner = root_two_pi * (preact + cubic_coef * preact * preact * preact)
    tanh_val = jnp.tanh(inner)
    gelu_out = 0.5 * preact * (1.0 + tanh_val)
    slopes = 0.5 * (1.0 + tanh_val) + 0.5 * preact * (1.0 - tanh_val * tanh_val) * root_two_pi * (
        1.0 + 3.0 * cubic_coef * preact * preact
    )
    return (gelu_out, slopes)


def on_device(tokens, cotangent, weight_in, weight_out, mix_kernel, block_rows):
    in_panel, out_panel = (
        lax.all_gather(weight_in, "rows", axis=0, tiled=True),
        lax.all_gather(weight_out, "rows", axis=0, tiled=True),
    )
    tok_full, cot_full = (
        lax.all_gather(tokens, "hid", axis=3, tiled=True),
        lax.all_gather(cotangent, "hid", axis=3, tiled=True),
    )
    crop_count, height, grid_width, depth_all = tok_full.shape
    tok_count = crop_count * height * grid_width
    block_size = in_panel.shape[0]
    col_count = in_panel.shape[1]
    nnz_count = in_panel.shape[2]
    block_count = depth_all // block_size
    hidden_local = col_count * block_size
    flat_rows = block_rows.reshape(-1)
    in_select = jnp.take(
        tok_full.reshape(tok_count, block_count, block_size), flat_rows, axis=1
    ).reshape(tok_count, col_count, nnz_count, block_size)
    grad_select = jnp.take(
        cot_full.reshape(tok_count, block_count, block_size), flat_rows, axis=1
    ).reshape(tok_count, col_count, nnz_count, block_size)
    pre_act = jnp.einsum("tckb,bcke->tce", in_select, in_panel, preferred_element_type=jnp.float32)
    gelu_out, slopes = gelu_pair(pre_act)
    active = gelu_out.astype(jnp.bfloat16).reshape(crop_count, height, grid_width, hidden_local)
    act_rim = padded(active, (("rows", 1),), 1)
    mix_grad = (
        jnp.einsum("tckd,fckd->tcf", grad_select, out_panel, preferred_element_type=jnp.float32)
        .astype(jnp.bfloat16)
        .reshape(crop_count, height, grid_width, hidden_local)
    )
    grad_rim = padded(mix_grad, (("rows", 1),), 1)
    act_pad = jnp.pad(act_rim.astype(jnp.float32), ((0, 0), (0, 0), (1, 1), (0, 0)))
    grad_pad = jnp.pad(grad_rim.astype(jnp.float32), ((0, 0), (0, 0), (1, 1), (0, 0)))
    grad_grid = mix_grad.astype(jnp.float32)
    mix_sum = jnp.zeros((crop_count, height, grid_width, hidden_local), jnp.float32)
    act_grad = jnp.zeros((crop_count, height, grid_width, hidden_local), jnp.float32)
    kern_terms = []
    for row_off in range(3):
        for col_off in range(3):
            tap = mix_kernel[3 * row_off + col_off]
            shifted = act_pad[:, row_off : row_off + height, col_off : col_off + grid_width]
            mix_sum = mix_sum + tap * shifted
            act_grad = (
                act_grad
                + tap
                * grad_pad[
                    :, 2 - row_off : 2 - row_off + height, 2 - col_off : 2 - col_off + grid_width
                ]
            )
            kern_terms.append(jnp.sum(shifted * grad_grid, axis=(0, 1, 2)))
    kern_local = jnp.stack(kern_terms, axis=0) * loss_scale
    mix_out = mix_sum.astype(jnp.bfloat16).reshape(tok_count, col_count, block_size)
    pre_grad = (act_grad.reshape(tok_count, col_count, block_size) * slopes).astype(jnp.bfloat16)
    kern_total = lax.psum(kern_local.astype(jnp.bfloat16), ("crop", "rows")).astype(jnp.float32)
    back_select = jnp.einsum(
        "tce,bcke->tckb", pre_grad, in_panel, preferred_element_type=jnp.float32
    )
    one_hot = (
        block_rows[:, :, None] == jnp.arange(block_count, dtype=jnp.int32)[None, None, :]
    ).astype(jnp.float32)
    token_terms = jnp.einsum(
        "tckb,ckr->trb", back_select, one_hot, precision=lax.Precision.HIGHEST
    ).reshape(crop_count, height, grid_width, depth_all)
    grad_tokens = lax.psum_scatter(
        token_terms.astype(jnp.bfloat16), "hid", scatter_dimension=3, tiled=True
    )
    first_term = jnp.einsum(
        "tckb,tce->bcke", in_select, pre_grad, preferred_element_type=jnp.float32
    )
    second_term = jnp.einsum(
        "tcf,tckd->fckd", mix_out, grad_select, preferred_element_type=jnp.float32
    )
    share_sums = lax.psum_scatter(
        (jnp.stack([first_term, second_term], axis=1) * loss_scale).astype(jnp.bfloat16),
        ("crop", "rows"),
        scatter_dimension=0,
        tiled=True,
    ).astype(jnp.float32)
    return (grad_tokens, share_sums[:, 0], share_sums[:, 1], kern_total)


def solution(mesh):
    placed = (
        P("crop", "rows", None, "hid"),
        P("crop", "rows", None, "hid"),
        P("rows", "hid", None, None),
        P("rows", "hid", None, None),
        P(None, "hid"),
        P("hid", None),
    )
    n_crop, n_rows = mesh.shape["crop"], mesh.shape["rows"]
    n_hid = mesh.shape["hid"]

    def step(tokens, cotangent, weight_in, weight_out, mix_kernel, block_rows):
        fits = (
            n_crop == 2
            and n_rows == 4
            and tokens.shape[0] == 1
            and weight_in.shape[1] % n_rows == 0
            and weight_in.shape[1] >= 2 * n_rows
            and n_hid >= 2
            and tokens.shape[1] * tokens.shape[2] * n_rows * tokens.shape[3] * n_hid <= 2**22
        )
        chosen = split_hidden if fits else on_device
        return chosen(tokens, cotangent, weight_in, weight_out, mix_kernel, block_rows)

    return jax.shard_map(
        step,
        mesh=mesh,
        in_specs=placed,
        out_specs=(
            P("crop", "rows", None, "hid"),
            P(("crop", "rows"), "hid", None, None),
            P(("crop", "rows"), "hid", None, None),
            P(None, "hid"),
        ),
        check_vma=False,
    )
```
